32 devices in a mesh: head: 4 (over x, core), tok: 8 (over z, y).
Axes of the slice: x: 2, y: 2, z: 4, core: 2. Of those that a mesh axis runs over, the one named last changes fastest.
Arguments:
- tokens: bfloat16 [4096, 1408], P('tok'), may hold values from -8 to 8
- segment_ids: int32 [1024], P('tok'), may hold values from 0 to 7, never falling along the last dimension, each value on 1 to 640 neighbouring positions
- valid: int32 [4096], P('tok'), may hold values 0 or 1
- owners: int32 [1024, 1], P('tok'), may hold values from 0 to 7; in each aligned block of 128 rows (0 to 127, 128 to 255, ...) at most 32 rows name the same one
- ln1_gain: bfloat16 [1408], replicated, may hold values from 0.099609375 to 1.8984375
- w_qkv: bfloat16 [3, 1408, 1408], P(None, None, 'head'), may hold values from -1 to 1
- w_out: bfloat16 [1408, 1408], P('head'), may hold values from -0.15625 to 0.15625
- ln2_gain: bfloat16 [1408], replicated, may hold values from 0.099609375 to 1.8984375
- w_up: bfloat16 [1408, 6144], P(None, 'head'), may hold values from -0.15625 to 0.15625
- w_down: bfloat16 [6144, 1408], P('head'), may hold values from -0.078125 to 0.078125
- ln3_gain: bfloat16 [1408], replicated, may hold values from 0.099609375 to 1.8984375
- w_merge: bfloat16 [5632, 1408], P(None, 'head'), may hold values from -0.078125 to 0.078125
Outputs:
- delivered: bfloat16 [2048, 1408], P('tok', 'head')
The draws below stay inside these ranges and needn't reach their ends.
Inputs may be any that keep to these rules, and one draw needn't show every extreme that they name: `segment_ids`: segment numbers never fall along the groups; each segment covers 1 to 640 groups and one covers exactly 640. `owners`: among the 128 groups of one device at most 32 name the same owner, a bound that some block reaches of them.
All inputs are finite; a program needn't handle non-finite values. No bound on the sum of `valid` on one device may be relied on, other than what follows from the above.
Results may differ from the reference program's by a relative error of at most 0.014.
Values may be sent and summed in bfloat16 or wider, within the bound.
No kernel may reach another device: no remote copies, remote signals or barrier semaphores. Data moves between devices by JAX's collectives and lax.ppermute only.
A program may use at most 128 MiB of HBM per device.

```python
import math
import jax
import jax.numpy as jnp
import numpy as np
from jax import lax

HEADS = 16
HEAD_DIM = 88
D = 1408
FF = 6144
TOKENS = 4096
GROUPS_DEV = 128
GROUPS = 1024
SEGS = 8
MOST_G = 640
CAP = 32
N_TOK = 8


def draw_tokens(key, part):
    first_key = jax.random.fold_in(key, 0)
    base = jax.random.normal(first_key, (TOKENS, D), jnp.float32)
    return jnp.clip(base, -8.0, 8.0).astype(jnp.bfloat16)


def draw_w_qkv(key, part):
    first_key = jax.random.fold_in(key, 0)
    base = jax.random.normal(first_key, (3, D, D), jnp.float32) / math.sqrt(D)
    base = base * jnp.array([2.5, 2.5, 1.0], jnp.float32)[:, None, None]
    return jnp.clip(base, -1.0, 1.0).astype(jnp.bfloat16)


def with_ends(values, key, smallest, high):
    longest = values.shape.index(max(values.shape))
    spots = []
    for shift in (0, 1):
        where = [jax.random.randint(jax.random.fold_in(key, axis), (), 0, length) for axis, length in enumerate(values.shape)]
        where[longest] = (where[longest] + shift) % values.shape[longest]
        spots.append(tuple(where))
    return values.at[spots[0]].set(smallest).at[spots[1]].set(high)


def block_scale(rng, shape, cuts, smallest, top_value):
    def one(dim, shards_of):
        steps = jax.random.uniform(jax.random.fold_in(jax.random.fold_in(rng, 6), dim), (shards_of,), jnp.float32, smallest / len(cuts), top_value / len(cuts))
        return jnp.repeat(jnp.exp(steps), shape[dim] // shards_of).reshape((-1,) + (1,) * (len(shape) - dim - 1))

    level = one(*cuts[0])
    for cut in cuts[1:]:
        level = level * one(*cut)
    return level


def split_up(number_of, total, bound, skew):
    weights = [(1 << 20) // math.isqrt(standing ** skew) + 1 for standing in range(2, number_of + 1)]
    rest, holding = total - bound - (number_of - 1), [1] * (number_of - 1)
    while rest > 0:
        movable = [i for i in range(number_of - 1) if holding[i] < bound]
        mass, budget = sum([weights[i] for i in movable]), rest
        for i in movable:
            extra = min(bound - holding[i], max(1, budget * weights[i] // mass), rest)
            holding[i] = holding[i] + extra
            rest = rest - extra
    return np.array([bound] + holding)


def ragged(stream_key, number_of, total, limit, skew):
    if number_of == 2:
        one = jax.random.randint(stream_key, (), max(1, total - limit), min(limit, total - 1) + 1)
        return jnp.stack([one, total - one])
    tallies = jnp.asarray(split_up(number_of, total, limit, skew), jnp.int32)
    couples = (number_of - 1) // 2
    giver, receiver = tallies[1:1 + 2 * couples:2], tallies[2:2 + 2 * couples:2]
    margin = jnp.minimum(giver - 1, limit - receiver)
    shifted = jax.random.randint(jax.random.fold_in(stream_key, 1), (couples,), 0, 1 << 20) % (margin + 1)
    tallies = tallies.at[1:1 + 2 * couples:2].set(giver - shifted).at[2:2 + 2 * couples:2].set(receiver + shifted)
    return tallies[jax.random.permutation(jax.random.fold_in(stream_key, 2), number_of)]


def routed_block(key, own, number, rows, number_of, top, reach, lean):
    order = jax.random.permutation(key, number_of)
    packed, usual = load_shares(number_of, rows * top, reach, lean, True), load_shares(number_of, rows * top, reach, lean, False)
    places = jnp.arange(number_of)

    def named(lengths, turn):
        used = int((lengths > 0).sum())
        fixed = max(1, used // 4)
        moved = fixed + (places - fixed + turn * (used - fixed)) % max(1, number_of - fixed)
        return jnp.zeros((number_of,), jnp.int32).at[order[jnp.where(places < fixed, places, moved)]].set(jnp.asarray(lengths, jnp.int32))

    lengths = jnp.where(number % 4 == 0, named(packed, number // 4), named(usual, number - number // 4 - 1))
    mixed = jax.random.permutation(jax.random.fold_in(own, 3), number_of)
    donor, sink = mixed[0:number_of // 2 * 2:2], mixed[1:number_of // 2 * 2:2]
    slack = jnp.minimum(lengths[donor] - 1, reach - lengths[sink]) // 2
    slack = jnp.where((donor == order[0]) | (sink == order[0]) | (lengths[sink] == 0), 0, jnp.maximum(slack, 0))
    moved = jax.random.randint(jax.random.fold_in(own, 4), (number_of // 2,), 0, 1 << 20) % (slack + 1)
    lengths = lengths.at[donor].add(-moved).at[sink].add(moved)
    items = jnp.searchsorted(jnp.cumsum(lengths), jnp.arange(rows * top), side="right").astype(jnp.int32)
    grid = items.reshape(top, rows).T
    grid = grid[jax.random.permutation(jax.random.fold_in(own, 1), rows)]
    turn = jax.random.randint(jax.random.fold_in(own, 2), (rows, 1), 0, top)
    return jnp.take_along_axis(grid, (jnp.arange(top)[None, :] + turn) % top, axis=1)


def load_shares(count, total, limit, lean, full):
    weights = [(1 << 20) // math.isqrt(standing ** lean) + 1 for standing in range(1, count + 1)]
    largest = limit if full else min(limit, max(-(-total // count), total * weights[0] // sum(weights)))
    least = 1 if total - largest >= count - 1 else 0
    given, rest = [largest] + [least] * (count - 1), total - largest - least * (count - 1)
    while rest > 0:
        movable = [i for i in range(1, count) if given[i] < largest] or [i for i in range(1, count) if given[i] < limit]
        whole, remaining = sum([weights[i] for i in movable]), rest
        for i in movable:
            more = min(limit - given[i], max(1, remaining * weights[i] // whole), rest)
            given[i] = given[i] + more
            rest = rest - more
    return np.array(given)


def centred(stream_key, dims, width, limit, pieces=(), kind=jnp.bfloat16):
    drawn = width * jax.random.normal(stream_key, dims, jnp.float32)
    if pieces:
        drawn = drawn * block_scale(stream_key, dims, pieces, -0.22, 0.18)
    return jnp.clip(drawn, -limit, limit).astype(kind)


def setup_inputs(seed: int = 0) -> dict:
    keys = jax.random.split(jax.random.key(seed), 13)
    tokens = draw_tokens(jax.random.fold_in(keys[12], 71), 0)
    segment_ids = jnp.searchsorted(jnp.cumsum(ragged(keys[1], SEGS, GROUPS, MOST_G, 2)), jnp.arange(GROUPS), side="right").astype(jnp.int32)
    valid = with_ends((jax.random.randint(keys[2], (TOKENS,), 0, 16) < 15).astype(jnp.int32), jax.random.fold_in(keys[2], 1), 0, 1)
    owners_keys = jax.random.split(jax.random.fold_in(keys[3], 1), GROUPS // GROUPS_DEV)
    owners_turns = jax.random.permutation(jax.random.fold_in(keys[3], 3), GROUPS // GROUPS_DEV)
    owners = jax.vmap(lambda own, number: routed_block(jax.random.fold_in(keys[3], 2), own, number, GROUPS_DEV, N_TOK, 1, CAP, 2))(owners_keys, owners_turns).reshape((GROUPS, 1))
    ln1_gain = jnp.clip(1.0 + 0.18 * jax.random.normal(keys[4], (D,), jnp.float32), 0.099609375, 1.8984375).astype(jnp.bfloat16)
    w_qkv = draw_w_qkv(jax.random.fold_in(keys[12], 71), 0)
    w_out = centred(keys[6], (D, D), D ** -0.5, 0.15625, ((0, 4),))
    ln2_gain = jnp.clip(1.0 + 0.18 * jax.random.normal(keys[7], (D,), jnp.float32), 0.099609375, 1.8984375).astype(jnp.bfloat16)
    w_up = centred(keys[8], (D, FF), D ** -0.5, 0.15625, ((1, 4),))
    w_down = centred(keys[9], (FF, D), FF ** -0.5, 0.078125, ((0, 4),))
    ln3_gain = jnp.clip(1.0 + 0.18 * jax.random.normal(keys[10], (D,), jnp.float32), 0.099609375, 1.8984375).astype(jnp.bfloat16)
    w_merge = centred(keys[11], (4 * D, D), (4 * D) ** -0.5, 0.078125, ((1, 4),))
    return dict(tokens=tokens, segment_ids=segment_ids, valid=valid, owners=owners, ln1_gain=ln1_gain, w_qkv=w_qkv, w_out=w_out, ln2_gain=ln2_gain, w_up=w_up, w_down=w_down, ln3_gain=ln3_gain, w_merge=w_merge)


def layer_norm(values, gain):
    center = values - lax.optimization_barrier(jnp.mean(values, axis=-1, keepdims=True))
    spread = lax.optimization_barrier(jnp.mean(center * center, axis=-1, keepdims=True))
    return center * lax.rsqrt(spread + 1e-06) * gain.astype(jnp.float32)

def reference(tokens, segment_ids, valid, owners, ln1_gain, w_qkv, w_out, ln2_gain, w_up, w_down, ln3_gain, w_merge):
    residual = tokens.astype(jnp.float32)
    normed = layer_norm(residual, ln1_gain).astype(jnp.bfloat16)
    queries = jnp.dot(normed, w_qkv[0], preferred_element_type=jnp.float32).astype(jnp.bfloat16)
    keys_all = jnp.dot(normed, w_qkv[1], preferred_element_type=jnp.float32).astype(jnp.bfloat16)
    values_all = jnp.dot(normed, w_qkv[2], preferred_element_type=jnp.float32).astype(jnp.bfloat16)
    token_segment = jnp.repeat(segment_ids, 4)
    positions = jnp.arange(TOKENS, dtype=jnp.int32)
    key_live = valid == 1
    query_block = math.gcd(TOKENS, 512)
    keys_wide = keys_all.astype(jnp.float32).reshape(TOKENS, HEADS, HEAD_DIM)
    values_wide = values_all.astype(jnp.float32).reshape(TOKENS, HEADS, HEAD_DIM)
    score_scale = 1.0 / math.sqrt(HEAD_DIM)

    def attend(block_index):
        first_row = block_index * query_block
        block_query = lax.dynamic_slice_in_dim(queries, first_row, query_block, 0)
        block_query = block_query.astype(jnp.float32).reshape(query_block, HEADS, HEAD_DIM)
        block_segment = lax.dynamic_slice_in_dim(token_segment, first_row, query_block, 0)
        block_position = first_row + jnp.arange(query_block, dtype=jnp.int32)
        allowed = (block_segment[:, None] == token_segment[None, :]) & (key_live[None, :] | (block_position[:, None] == positions[None, :]))
        scores = jnp.einsum('qhe,khe->hqk', block_query, keys_wide) * score_scale
        scores = jnp.where(allowed[None], scores, -1e+30)
        highest = lax.optimization_barrier(jnp.max(scores, axis=-1, keepdims=True))
        weights = jnp.where(allowed[None], jnp.exp(scores - highest), 0.0)
        weight_total = lax.optimization_barrier(jnp.sum(weights, axis=-1))
        rounded = lax.optimization_barrier(weights.astype(jnp.bfloat16)).astype(jnp.float32)
        mixed = jnp.einsum('hqk,khe->hqe', rounded, values_wide) / weight_total[..., None]
        return jnp.transpose(mixed, (1, 0, 2)).reshape(query_block, D).astype(jnp.bfloat16)
    attended = lax.map(attend, jnp.arange(TOKENS // query_block, dtype=jnp.int32)).reshape(TOKENS, D)
    hidden1 = residual + jnp.dot(attended, w_out, preferred_element_type=jnp.float32)
    second = layer_norm(hidden1, ln2_gain).astype(jnp.bfloat16)
    activated = jax.nn.gelu(jnp.dot(second, w_up, preferred_element_type=jnp.float32), approximate=False).astype(jnp.bfloat16)
    hidden2 = hidden1 + jnp.dot(activated, w_down, preferred_element_type=jnp.float32)
    merged_in = layer_norm(hidden2, ln3_gain).astype(jnp.bfloat16).reshape(GROUPS, 4 * D)
    projected = jnp.dot(merged_in, w_merge, preferred_element_type=jnp.float32).astype(jnp.bfloat16)
    owner_ids = owners[:, 0]
    picks = (owner_ids[:, None] == jnp.arange(N_TOK, dtype=jnp.int32)[None, :]).astype(jnp.int32)
    picks = picks.reshape(N_TOK, GROUPS_DEV, N_TOK)
    earlier = jnp.cumsum(picks, axis=1, dtype=jnp.int32) - picks
    group_rank = lax.optimization_barrier(jnp.sum(earlier * picks, axis=2, dtype=jnp.int32)).reshape(GROUPS)
    source_block = jnp.arange(GROUPS, dtype=jnp.int32) // GROUPS_DEV
    target_row = owner_ids * (N_TOK * CAP) + source_block * CAP + group_rank
    delivered = jnp.zeros((N_TOK * N_TOK * CAP, D), jnp.bfloat16).at[target_row].set(projected)
    return delivered
```

```python
import math

import jax
import jax.numpy as jnp
from jax import lax
from jax.experimental import pallas as pl
from jax.experimental.pallas import tpu as pltpu
from jax.sharding import PartitionSpec as P

HEAD_DIM = 88
EXT = 128
VEXT = 96
GONE = 64.0
FAR = -1e30
BF = jnp.bfloat16
F32 = jnp.float32
VMEM_LIMIT = 56 * 1024 * 1024


def swap_pairs(size, mask):
    return [(i, i ^ mask) for i in range(size)]


def center_scale(values):
    center = values - jnp.mean(values, axis=-1, keepdims=True)
    spread = jnp.mean(center * center, axis=-1, keepdims=True)
    return center * lax.rsqrt(spread + 1e-06)


def call(kernel, outs, args, specs=None, grid=None, out_specs=None, scratch=(), name=None):
    vm = pl.BlockSpec(memory_space=pltpu.VMEM)
    kw = {}
    if grid is not None:
        kw["grid"] = grid
    return pl.pallas_call(
        kernel,
        out_shape=outs,
        in_specs=specs if specs is not None else [vm] * len(args),
        out_specs=out_specs if out_specs is not None else [vm] * len(outs),
        scratch_shapes=scratch,
        compiler_params=pltpu.CompilerParams(vmem_limit_bytes=VMEM_LIMIT),
        name=name,
        **kw,
    )(*args)


SMEM = pl.BlockSpec(memory_space=pltpu.SMEM)
VM = pl.BlockSpec(memory_space=pltpu.VMEM)
HBM = pl.BlockSpec(memory_space=pl.ANY)


def qkv_stage(where, tokens, gain, w_qkv, seg, valid, heads):
    rows, width = tokens.shape
    local = w_qkv.shape[2]
    scale = math.log2(math.e) / math.sqrt(HEAD_DIM)
    far_rows = VEXT + HEAD_DIM
    near_rows = far_rows + HEAD_DIM

    def kernel(where_ref, tok_ref, gain_ref, w_ref, seg_ref, valid_ref, *rest):
        near = rest[:heads]
        far = rest[heads : 2 * heads]
        normed, parts = rest[2 * heads :]
        step = pl.program_id(0)

        @pl.when(step == 0)
        def _():
            unit = center_scale(tok_ref[...].astype(F32))
            normed[...] = (unit * gain_ref[...].astype(F32)).astype(BF)

        flat = jnp.dot(normed[...], w_ref[0], preferred_element_type=F32)
        flat = flat * jnp.where(step == 0, scale, 1.0)
        turned = flat.T
        for h in range(heads):
            parts[step, h] = turned[h * HEAD_DIM : (h + 1) * HEAD_DIM].astype(BF)

        @pl.when(step == 2)
        def _():
            spread_to = lax.broadcasted_iota(jnp.int32, (rows // 4, rows), 1) // 4
            spread_from = lax.broadcasted_iota(jnp.int32, (rows // 4, rows), 0)
            spread = (spread_to == spread_from).astype(BF)
            seg8 = jnp.broadcast_to(seg_ref[...].astype(F32), (8, rows // 4)).astype(BF)
            tags = jnp.dot(seg8, spread, preferred_element_type=F32)
            gone = jnp.where(valid_ref[...] == 1, 0.0, GONE)
            tags = (tags + jnp.broadcast_to(gone, (8, rows))).astype(BF)
            for j in range(heads):
                h = where_ref[0] ^ j
                for ref in (near[j], far[j]):
                    ref[0:HEAD_DIM] = parts[1, h]
                    ref[HEAD_DIM:VEXT] = tags
                    ref[VEXT:far_rows] = parts[2, h]
                near[j][far_rows:near_rows] = parts[0, h]

    outs = [jax.ShapeDtypeStruct((near_rows, rows), BF)] * heads
    outs += [jax.ShapeDtypeStruct((far_rows, rows), BF)] * heads
    whole = lambda shape: pl.BlockSpec(shape, lambda i: (0,) * len(shape))
    result = call(
        kernel,
        outs,
        (where, tokens, gain, w_qkv, seg, valid),
        specs=[
            SMEM,
            whole((rows, width)),
            whole((1, width)),
            pl.BlockSpec((1, width, local), lambda i: (i, 0, 0)),
            whole((1, rows // 4)),
            whole((1, rows)),
        ],
        grid=(3,),
        out_specs=[whole(o.shape) for o in outs],
        scratch=[pltpu.VMEM((rows, width), BF), pltpu.VMEM((3, heads, HEAD_DIM, rows), BF)],
        name="qkv",
    )
    return result[:heads], result[heads:]


def tag_rows(block):
    tags = block[HEAD_DIM:VEXT].astype(F32)[0:1]
    gone = tags >= GONE
    return jnp.where(gone, tags - GONE, tags), gone


def load_keys(block_ref, keys, values, segments):
    rows = block_ref.shape[1]
    top = block_ref[0:VEXT].astype(F32)
    tags = top[HEAD_DIM : HEAD_DIM + 1]
    gone = tags >= GONE
    seg = jnp.where(gone, tags - GONE, tags)
    mark = jnp.where(gone, float(segments), tags)
    line = lax.broadcasted_iota(jnp.int32, (EXT, rows), 0) - HEAD_DIM
    hot = (line.astype(F32) == mark).astype(F32)
    head_part = jnp.where(line[0:VEXT] >= 0, hot[0:VEXT], top)
    keys[:, 0:VEXT] = head_part.T.astype(BF)
    keys[:, VEXT:EXT] = hot[VEXT:EXT].T.astype(BF)
    vals = block_ref[VEXT : VEXT + HEAD_DIM].astype(F32)
    ones = jnp.ones((VEXT - HEAD_DIM, rows), F32)
    values[...] = jnp.concatenate([vals, ones], axis=0).astype(BF)
    return jnp.min(seg), jnp.max(seg)


def absorb(keys, values, query, top, sums):
    scores = jnp.dot(keys[...], query[...], preferred_element_type=F32)
    newest = jnp.maximum(top[...], jnp.max(scores, axis=0, keepdims=True))
    weights = jnp.exp2(scores - newest).astype(BF)
    factor = jnp.exp2(top[...] - newest)
    sums[...] = sums[...] * factor + jnp.dot(values[...], weights, preferred_element_type=F32)
    top[...] = newest


def near_stage(blocks, segments):
    count = len(blocks)
    rows = blocks[0].shape[1]
    query_at = VEXT + HEAD_DIM

    def kernel(*refs):
        blk = refs[:count]
        queries, tops, sums, low_high = refs[count : count + 4]
        keys, values = refs[count + 4 :]
        bounds = []
        for b in range(count):
            bounds.append(load_keys(blk[b], keys.at[b], values.at[b], segments))
            low_high[2 * b] = bounds[b][0]
            low_high[2 * b + 1] = bounds[b][1]
        for j in range(count):
            query = blk[j][query_at : query_at + HEAD_DIM].astype(F32)
            top = blk[j][0:VEXT].astype(F32)
            tags = top[HEAD_DIM : HEAD_DIM + 1]
            gone = tags >= GONE
            seg = jnp.where(gone, tags - GONE, tags)
            line = lax.broadcasted_iota(jnp.int32, (EXT - HEAD_DIM, rows), 0).astype(F32)
            wall = jnp.where(line == seg, 0.0, FAR)
            queries[j] = jnp.concatenate([query, wall], axis=0).astype(BF)
            own = jnp.sum(query * top[0:HEAD_DIM], axis=0, keepdims=True)
            tops[j] = jnp.where(gone, own, FAR)
            sums[j] = jnp.where(gone, values[j].astype(F32), 0.0)
        for j in range(count):
            for b in range(count):
                if b == j:
                    absorb(keys.at[b], values.at[b], queries.at[j], tops.at[j], sums.at[j])
                else:

                    @pl.when((bounds[b][0] <= bounds[j][1]) & (bounds[b][1] >= bounds[j][0]))
                    def _():
                        absorb(keys.at[b], values.at[b], queries.at[j], tops.at[j], sums.at[j])

    outs = [
        jax.ShapeDtypeStruct((count, EXT, rows), BF),
        jax.ShapeDtypeStruct((count, 1, rows), F32),
        jax.ShapeDtypeStruct((count, VEXT, rows), F32),
        jax.ShapeDtypeStruct((2 * count,), F32),
    ]
    return call(
        kernel,
        outs,
        blocks,
        out_specs=[VM, VM, VM, SMEM],
        scratch=[pltpu.VMEM((count, rows, EXT), BF), pltpu.VMEM((count, VEXT, rows), BF)],
        name="near",
    )


def far_stage(blocks, queries, tops, sums, low_high, segments):
    count = len(blocks)
    heads, _, rows = queries.shape

    def kernel(*refs):
        blk = refs[:count]
        query_ref, top_ref, sum_ref, bound_ref = refs[count : count + 4]
        out = refs[count + 4 : count + 4 + heads]
        keys, values, top, total = refs[count + 4 + heads :]
        bounds = [load_keys(blk[b], keys.at[b], values.at[b], segments) for b in range(count)]
        for j in range(heads):
            top[...] = top_ref[j]
            total[...] = sum_ref[j]
            for b in range(count):

                @pl.when((bounds[b][0] <= bound_ref[2 * j + 1]) & (bounds[b][1] >= bound_ref[2 * j]))
                def _():
                    absorb(keys.at[b], values.at[b], query_ref.at[j], top, total)

            whole = total[...]
            out[j][...] = (whole[0:HEAD_DIM] / whole[HEAD_DIM : HEAD_DIM + 1]).astype(BF)

    outs = [jax.ShapeDtypeStruct((HEAD_DIM, rows), BF)] * heads
    return call(
        kernel,
        outs,
        (*blocks, queries, tops, sums, low_high),
        specs=[VM] * (count + 3) + [SMEM],
        scratch=[
            pltpu.VMEM((count, rows, EXT), BF),
            pltpu.VMEM((count, VEXT, rows), BF),
            pltpu.VMEM((1, rows), F32),
            pltpu.VMEM((VEXT, rows), F32),
        ],
        name="far",
    )


def mlp_stage(where, tokens, attended, w_outs, gain, w_up, w_down):
    rows, width = tokens.shape
    part = attended[0].shape[0]
    pieces = len(attended)
    hidden = w_up.shape[1]
    half, quarter = rows // 2, rows // 4

    def kernel(where_ref, tok_ref, *refs):
        att = refs[:pieces]
        wout_hbm = refs[pieces : 2 * pieces]
        gain_ref, up_hbm, down_hbm, keep, send, own = refs[2 * pieces : 2 * pieces + 6]
        wout, up, down, mixed, stream, second, act, sem = refs[2 * pieces + 6 :]
        copies = [
            pltpu.make_async_copy(wout_hbm[e], wout.at[pl.ds(e * part, part)], sem.at[e])
            for e in range(pieces)
        ]
        copies.append(pltpu.make_async_copy(up_hbm, up, sem.at[pieces]))
        copies.append(pltpu.make_async_copy(down_hbm, down, sem.at[pieces + 1]))
        for c in copies:
            c.start()
        for e in range(pieces):
            mixed[:, e * part : (e + 1) * part] = att[e][...].astype(F32).T.astype(BF)
        for c in copies[:pieces]:
            c.wait()
        stream[...] = tok_ref[...].astype(F32) + jnp.dot(
            mixed[...], wout[...], preferred_element_type=F32
        )
        own[...] = stream[pl.ds(pl.multiple_of(where_ref[1] * quarter, quarter), quarter)]
        second[...] = (center_scale(stream[...]) * gain_ref[...].astype(F32)).astype(BF)
        copies[pieces].wait()
        pre = jnp.dot(second[...], up[...], preferred_element_type=F32)
        act[...] = (0.5 * pre * (1.0 + lax.erf(pre * math.sqrt(0.5)))).astype(BF)
        copies[pieces + 1].wait()
        stream[...] = jnp.dot(act[...], down[...], preferred_element_type=F32)
        keep_at = pl.multiple_of(where_ref[2] * half, half)
        send_at = pl.multiple_of((1 - where_ref[2]) * half, half)
        keep[...] = stream[pl.ds(keep_at, half)].astype(BF)
        send[...] = stream[pl.ds(send_at, half)].astype(BF)

    outs = [
        jax.ShapeDtypeStruct((half, width), BF),
        jax.ShapeDtypeStruct((half, width), BF),
        jax.ShapeDtypeStruct((quarter, width), F32),
    ]
    return call(
        kernel,
        outs,
        (where, tokens, *attended, *w_outs, gain, w_up, w_down),
        specs=[SMEM, VM] + [VM] * pieces + [HBM] * pieces + [VM, HBM, HBM],
        scratch=[
            pltpu.VMEM((pieces * part, width), BF),
            pltpu.VMEM((width, hidden), BF),
            pltpu.VMEM((hidden, width), BF),
            pltpu.VMEM((rows, pieces * part), BF),
            pltpu.VMEM((rows, width), F32),
            pltpu.VMEM((rows, width), BF),
            pltpu.VMEM((rows, hidden), BF),
            pltpu.SemaphoreType.DMA((pieces + 2,)),
        ],
        name="mlp",
    )


def fold_stage(where, keep, arrived, own):
    half, width = keep.shape
    quarter = half // 2

    def kernel(where_ref, keep_ref, arrived_ref, own_ref, send, mine):
        mine_at = pl.multiple_of(where_ref[3] * quarter, quarter)
        send_at = pl.multiple_of((1 - where_ref[3]) * quarter, quarter)
        both = lambda at: (
            keep_ref[pl.ds(at, quarter)].astype(F32) + arrived_ref[pl.ds(at, quarter)].astype(F32)
        )
        send[...] = both(send_at).astype(BF)
        mine[...] = own_ref[...] + both(mine_at)

    outs = [
        jax.ShapeDtypeStruct((quarter, width), BF),
        jax.ShapeDtypeStruct((quarter, width), F32),
    ]
    return call(kernel, outs, (where, keep, arrived, own), specs=[SMEM, VM, VM, VM], name="fold")


def norm_stage(mine, arrived, gain):
    quarter, width = mine.shape
    groups = quarter // 4

    def kernel(mine_ref, arrived_ref, gain_ref, out, unit):
        total = mine_ref[...] + arrived_ref[...].astype(F32)
        normed = center_scale(total) * gain_ref[...].astype(F32)
        for c in range(width // 128):
            unit[c] = normed[:, c * 128 : (c + 1) * 128]
        for u in range(4):
            for c in range(width // 128):
                out[u * groups : (u + 1) * groups, c * 128 : (c + 1) * 128] = unit[
                    c, pl.ds(u, groups, stride=4)
                ].astype(BF)

    return call(
        kernel,
        [jax.ShapeDtypeStruct((quarter, width), BF)],
        (mine, arrived, gain),
        scratch=[pltpu.VMEM((width // 128, quarter, 128), F32)],
        name="norm",
    )[0]


def merge_stage(where, pieces, w_merge, owners, owner_total, capacity):
    quarter, width = pieces[0].shape
    count = len(pieces)
    groups = count * quarter // 4
    part = quarter // 4
    local = w_merge.shape[1]
    slots = owner_total * capacity

    def kernel(where_ref, *refs):
        blk = refs[:count]
        merge_hbm, owner_ref, out, weight, rows, sem = refs[count:]
        copies = [
            pltpu.make_async_copy(
                merge_hbm.at[pl.ds(u * width, width)], weight.at[pl.ds(u * width, width)], sem.at[u]
            )
            for u in range(4)
        ]
        for c in copies:
            c.start()
        for e in range(count):
            spot = where_ref[1] ^ ((e & 1) * 2 + (e >> 1))
            at = pl.multiple_of(
                ((spot & 1) * 1 + (spot >> 1) * 2) * part, part
            )
            for u in range(4):
                rows[u, pl.ds(at, part)] = blk[e][u * part : (u + 1) * part]
        owner = owner_ref[...]
        picks = owner == lax.broadcasted_iota(jnp.int32, (groups, 128), 1)
        below = lax.broadcasted_iota(jnp.int32, (groups, groups), 1) < lax.broadcasted_iota(
            jnp.int32, (groups, groups), 0
        )
        earlier = jnp.dot(below.astype(BF), picks.astype(BF), preferred_element_type=F32)
        rank = jnp.sum(jnp.where(picks, earlier, 0.0), axis=1, keepdims=True)
        slot = owner * capacity + rank.astype(jnp.int32)
        chosen = (slot == lax.broadcasted_iota(jnp.int32, (groups, slots), 1)).astype(F32)
        dispatch = chosen.T.astype(BF)
        total = jnp.zeros((groups, local), F32)
        for u in range(4):
            copies[u].wait()
            total += jnp.dot(
                rows[u], weight[u * width : (u + 1) * width], preferred_element_type=F32
            )
        out[...] = jnp.dot(dispatch, total.astype(BF), preferred_element_type=F32).astype(BF)

    return call(
        kernel,
        [jax.ShapeDtypeStruct((slots, local), BF)],
        (where, *pieces, w_merge, owners),
        specs=[SMEM] + [VM] * count + [HBM, VM],
        scratch=[
            pltpu.VMEM((4 * width, local), BF),
            pltpu.VMEM((4, groups, width), BF),
            pltpu.SemaphoreType.DMA((4,)),
        ],
        name="merge",
    )[0]


def per_device(
    tokens,
    segment_ids,
    valid,
    owners,
    ln1_gain,
    w_qkv,
    w_out,
    ln2_gain,
    w_up,
    w_down,
    ln3_gain,
    w_merge,
):
    rows, width = tokens.shape
    heads = w_qkv.shape[2] // HEAD_DIM
    tok_total = lax.axis_size("tok")
    head_total = lax.axis_size("head")
    tok_at = lax.axis_index("tok")
    head_at = lax.axis_index("head")
    turn = tok_at & (heads - 1)
    core = head_at & 1
    side = head_at >> 1
    where = jnp.stack([turn, core * 2 + side, core, side]).astype(jnp.int32)
    over_tok = lambda value, mask: lax.ppermute(value, "tok", swap_pairs(tok_total, mask))
    over_head = lambda value, mask: lax.ppermute(value, "head", swap_pairs(head_total, mask))

    near, far = qkv_stage(
        where,
        tokens,
        ln1_gain.reshape(1, width),
        w_qkv,
        segment_ids.reshape(1, -1),
        valid.reshape(1, -1),
        heads,
    )
    far_in = [over_tok(far[k & (heads - 1)], k) for k in range(heads, tok_total)]
    near_in = [near[0]] + [over_tok(near[k], k) for k in range(1, heads)]

    w_own, _ = lax.optimization_barrier((w_out, near[0]))
    w_own = jnp.concatenate(
        [
            lax.dynamic_slice_in_dim(w_own, (turn ^ k) * HEAD_DIM, HEAD_DIM, 0)
            for k in range(heads)
        ],
        axis=0,
    )
    w_side = over_head(w_own, 2)
    w_outs = [w_own, over_head(w_own, 1), w_side, over_head(w_side, 1)]

    queries, tops, sums, low_high = near_stage(near_in, tok_total)
    mixed = far_stage(far_in, queries, tops, sums, low_high, tok_total)
    back = [mixed[0]] + [over_tok(mixed[k], k) for k in range(1, heads)]
    att_own = jnp.concatenate(back, axis=0)
    att_side = over_head(att_own, 2)
    attended = [att_own, over_head(att_own, 1), att_side, over_head(att_side, 1)]

    keep, send, own = mlp_stage(
        where, tokens, attended, w_outs, ln2_gain.reshape(1, width), w_up, w_down
    )
    send, mine = fold_stage(where, keep, over_head(send, 1), own)
    merged = norm_stage(mine, over_head(send, 2), ln3_gain.reshape(1, width))
    merged_side = over_head(merged, 2)
    pieces = [merged, over_head(merged, 1), merged_side, over_head(merged_side, 1)]

    groups = rows // 4
    capacity = max(2, 2 * groups // tok_total)
    outgoing = merge_stage(where, pieces, w_merge, owners, tok_total, capacity)
    outgoing = outgoing.reshape(tok_total, capacity, outgoing.shape[1])
    received = lax.all_to_all(outgoing, "tok", split_axis=0, concat_axis=0, tiled=True)
    return received.reshape(tok_total * capacity, outgoing.shape[2])


def solution(mesh):
    in_specs = (
        P("tok", None),
        P("tok"),
        P("tok"),
        P("tok", None),
        P(),
        P(None, None, "head"),
        P("head", None),
        P(),
        P(None, "head"),
        P("head", None),
        P(),
        P(None, "head"),
    )
    out_specs = P("tok", "head")
    return jax.shard_map(
        per_device, mesh=mesh, in_specs=in_specs, out_specs=out_specs, check_vma=False
    )
```

```python
import math

import jax
import jax.numpy as jnp
from jax import lax
from jax.experimental import pallas as pl
from jax.experimental.pallas import tpu as pltpu
from jax.sharding import PartitionSpec as P

HEAD_DIM = 88
EXT = 128
VEXT = 96
GONE = 64.0
FAR = -1e30
BF = jnp.bfloat16
F32 = jnp.float32
CHUNKS = 2


def swap_pairs(size, mask):
    return [(i, i ^ mask) for i in range(size)]


def center_scale(values):
    center = values - jnp.mean(values, axis=-1, keepdims=True)
    spread = jnp.mean(center * center, axis=-1, keepdims=True)
    return center * lax.rsqrt(spread + 1e-06)


SMEM = pl.BlockSpec(memory_space=pltpu.SMEM)
VM = pl.BlockSpec(memory_space=pltpu.VMEM)
HBM = pl.BlockSpec(memory_space=pl.ANY)


def call(kernel, outs, args, specs=None, out_specs=None, scratch=(), name=None, room=24, cost=None):
    specs = specs if specs is not None else [VM] * len(args)
    out_specs = out_specs if out_specs is not None else [VM] * len(outs)
    args = [
        pltpu.with_memory_space_constraint(a, pltpu.VMEM) if s is VM else a
        for a, s in zip(args, specs)
    ]
    outs = [
        pltpu.VMEM(o.shape, o.dtype) if s is VM else o for o, s in zip(outs, out_specs)
    ]
    return pl.pallas_call(
        kernel,
        out_shape=outs,
        in_specs=specs,
        out_specs=out_specs,
        scratch_shapes=scratch,
        compiler_params=pltpu.CompilerParams(vmem_limit_bytes=room * 1024 * 1024),
        cost_estimate=cost,
        name=name,
    )(*args)


def qkv_stage(tokens, gain, w_qkv, seg, valid, heads):
    rows, width = tokens.shape
    local = w_qkv.shape[1]
    scale = math.log2(math.e) / math.sqrt(HEAD_DIM)
    far_rows = VEXT + HEAD_DIM
    near_rows = far_rows + HEAD_DIM
    strip = math.gcd(rows, 128)

    def kernel(tok_hbm, gain_ref, w_hbm, seg_ref, valid_ref, *rest):
        near = rest[0]
        far = rest[1 : 1 + heads]
        tok, weight, normed, sem = rest[1 + heads :]
        tok_copy = pltpu.make_async_copy(tok_hbm, tok, sem.at[3])
        tok_copy.start()
        copies = [pltpu.make_async_copy(w_hbm.at[i], weight.at[i], sem.at[i]) for i in range(3)]
        for i in (1, 2, 0):
            copies[i].start()
        spread_to = lax.broadcasted_iota(jnp.int32, (rows // 4, rows), 1) // 4
        spread_from = lax.broadcasted_iota(jnp.int32, (rows // 4, rows), 0)
        spread = (spread_to == spread_from).astype(BF)
        seg8 = jnp.broadcast_to(seg_ref[...].astype(F32), (8, rows // 4)).astype(BF)
        tags = jnp.dot(seg8, spread, preferred_element_type=F32)
        gone = jnp.where(valid_ref[...] == 1, 0.0, GONE)
        tags = (tags + jnp.broadcast_to(gone, (8, rows))).astype(BF)
        gains = gain_ref[...].astype(F32)
        tok_copy.wait()
        for i in range(rows // strip):
            at = slice(i * strip, (i + 1) * strip)
            normed[at] = (center_scale(tok[at].astype(F32)) * gains).astype(BF)

        for i, place in ((1, 0), (2, VEXT), (0, far_rows)):
            copies[i].wait()
            turned = lax.dot_general(
                weight[i], normed[...], (((1,), (1,)), ((), ())), preferred_element_type=F32
            )
            if i == 0:
                turned = turned * scale
            for h in range(heads):
                near[h, place : place + HEAD_DIM] = turned[
                    h * HEAD_DIM : (h + 1) * HEAD_DIM
                ].astype(BF)
        turn = lax.axis_index("tok") & (heads - 1)
        for h in range(heads):
            near[h, HEAD_DIM:VEXT] = tags
        for j in range(heads):
            far[j][...] = near[turn ^ j, 0:far_rows]

    outs = [jax.ShapeDtypeStruct((heads, near_rows, rows), BF)]
    outs += [jax.ShapeDtypeStruct((far_rows, rows), BF)] * heads
    result = call(
        kernel,
        outs,
        (tokens, gain, w_qkv, seg, valid),
        specs=[HBM, VM, HBM, VM, VM],
        scratch=[
            pltpu.VMEM((rows, width), BF),
            pltpu.VMEM((3, local, width), BF),
            pltpu.VMEM((rows, width), BF),
            pltpu.SemaphoreType.DMA((4,)),
        ],
        name="qkv",
        cost=pl.CostEstimate(flops=4 * 10**9, transcendentals=0, bytes_accessed=10**7),
    )
    return result[0], result[1:]


def load_keys(block_ref, keys, values, segments):
    rows = block_ref.shape[1]
    top = block_ref[0:VEXT].astype(F32)
    tags = top[HEAD_DIM : HEAD_DIM + 1]
    gone = tags >= GONE
    seg = jnp.where(gone, tags - GONE, tags)
    mark = jnp.where(gone, float(segments), tags)
    line = lax.broadcasted_iota(jnp.int32, (EXT, rows), 0) - HEAD_DIM
    hot = (line.astype(F32) == mark).astype(F32)
    head_part = jnp.where(line[0:VEXT] >= 0, hot[0:VEXT], top)
    keys[:, 0:VEXT] = head_part.T.astype(BF)
    keys[:, VEXT:EXT] = hot[VEXT:EXT].T.astype(BF)
    vals = block_ref[VEXT : VEXT + HEAD_DIM].astype(F32)
    ones = jnp.ones((VEXT - HEAD_DIM, rows), F32)
    values[...] = jnp.concatenate([vals, ones], axis=0).astype(BF)
    return jnp.min(seg), jnp.max(seg)


def absorb(keys, values, query, top, sums):
    scores = jnp.dot(keys[...], query[...], preferred_element_type=F32)
    newest = jnp.maximum(top[...], jnp.max(scores, axis=0, keepdims=True))
    weights = jnp.exp2(scores - newest).astype(BF)
    factor = jnp.exp2(top[...] - newest)
    sums[...] = sums[...] * factor + jnp.dot(values[...], weights, preferred_element_type=F32)
    top[...] = newest


def near_stage(blocks, segments):
    count, _, rows = blocks.shape
    query_at = VEXT + HEAD_DIM

    def kernel(blk, queries, tops, sums, low_high, keys, values):
        bounds = []
        for b in range(count):
            bounds.append(load_keys(blk.at[b], keys.at[b], values.at[b], segments))
            low_high[2 * b] = bounds[b][0]
            low_high[2 * b + 1] = bounds[b][1]
        for j in range(count):
            query = blk[j, query_at : query_at + HEAD_DIM].astype(F32)
            top = blk[j, 0:VEXT].astype(F32)
            tags = top[HEAD_DIM : HEAD_DIM + 1]
            gone = tags >= GONE
            seg = jnp.where(gone, tags - GONE, tags)
            line = lax.broadcasted_iota(jnp.int32, (EXT - HEAD_DIM, rows), 0).astype(F32)
            wall = jnp.where(line == seg, 0.0, FAR)
            queries[j] = jnp.concatenate([query, wall], axis=0).astype(BF)
            own = jnp.sum(query * top[0:HEAD_DIM], axis=0, keepdims=True)
            tops[j] = jnp.where(gone, own, FAR)
            sums[j] = jnp.where(gone, values[j].astype(F32), 0.0)
        for j in range(count):
            for b in range(count):

                @pl.when((bounds[b][0] <= bounds[j][1]) & (bounds[b][1] >= bounds[j][0]))
                def _():
                    absorb(keys.at[b], values.at[b], queries.at[j], tops.at[j], sums.at[j])

    outs = [
        jax.ShapeDtypeStruct((count, EXT, rows), BF),
        jax.ShapeDtypeStruct((count, 1, rows), F32),
        jax.ShapeDtypeStruct((count, VEXT, rows), F32),
        jax.ShapeDtypeStruct((2 * count,), F32),
    ]
    return call(
        kernel,
        outs,
        (blocks,),
        out_specs=[VM, VM, VM, SMEM],
        scratch=[pltpu.VMEM((count, rows, EXT), BF), pltpu.VMEM((count, VEXT, rows), BF)],
        name="near",
        cost=pl.CostEstimate(flops=8 * 10**9, transcendentals=4 * 10**6, bytes_accessed=10**7),
    )


def far_stage(blocks, queries, tops, sums, low_high, segments):
    count = len(blocks)
    heads, _, rows = queries.shape

    def kernel(*refs):
        blk = refs[:count]
        query_ref, top_ref, sum_ref, bound_ref = refs[count : count + 4]
        out, keys, values, top, total = refs[count + 4 :]
        bounds = [load_keys(blk[b], keys.at[b], values.at[b], segments) for b in range(count)]
        for j in range(heads):
            top[...] = top_ref[j]
            total[...] = sum_ref[j]
            for b in range(count):

                @pl.when((bounds[b][0] <= bound_ref[2 * j + 1]) & (bounds[b][1] >= bound_ref[2 * j]))
                def _():
                    absorb(keys.at[b], values.at[b], query_ref.at[j], top, total)

            whole = total[...]
            out[j] = (whole[0:HEAD_DIM] / whole[HEAD_DIM : HEAD_DIM + 1]).astype(BF)

    return call(
        kernel,
        [jax.ShapeDtypeStruct((heads, HEAD_DIM, rows), BF)],
        (*blocks, queries, tops, sums, low_high),
        specs=[VM] * (count + 3) + [SMEM],
        scratch=[
            pltpu.VMEM((count, rows, EXT), BF),
            pltpu.VMEM((count, VEXT, rows), BF),
            pltpu.VMEM((1, rows), F32),
            pltpu.VMEM((VEXT, rows), F32),
        ],
        name="far",
        cost=pl.CostEstimate(flops=6 * 10**9, transcendentals=4 * 10**6, bytes_accessed=10**7),
    )[0]


def mlp_stage(first, tokens, attended, w_outs, gain, w_up, w_down):
    width = tokens.shape[1]
    part, rows = attended[0].shape
    pieces = len(attended)
    hidden = w_up.shape[1]
    half, quarter = rows // 2, rows // 4

    def kernel(tok_ref, *refs):
        att = refs[:pieces]
        wout = refs[pieces : 2 * pieces]
        gain_ref, up, down, keep, send, own, stream, second, act = refs[2 * pieces :]
        head_at = lax.axis_index("head")
        core, side = head_at & 1, head_at >> 1
        total = tok_ref[first : first + rows].astype(F32)
        for e in range(pieces):
            total += jnp.dot(
                att[e][...].astype(F32).T.astype(BF), wout[e][...], preferred_element_type=F32
            )
        stream[...] = total
        own[...] = stream[pl.ds(pl.multiple_of((core * 2 + side) * quarter, quarter), quarter)]
        second[...] = (center_scale(stream[...]) * gain_ref[...].astype(F32)).astype(BF)
        pre = jnp.dot(second[...], up[...], preferred_element_type=F32)
        act[...] = (0.5 * pre * (1.0 + lax.erf(pre * math.sqrt(0.5)))).astype(BF)
        stream[...] = jnp.dot(act[...], down[...], preferred_element_type=F32)
        keep[...] = stream[pl.ds(pl.multiple_of(core * half, half), half)].astype(BF)
        send[...] = stream[pl.ds(pl.multiple_of((1 - core) * half, half), half)].astype(BF)

    outs = [
        jax.ShapeDtypeStruct((half, width), BF),
        jax.ShapeDtypeStruct((half, width), BF),
        jax.ShapeDtypeStruct((quarter, width), F32),
    ]
    return call(
        kernel,
        outs,
        (tokens, *attended, *w_outs, gain, w_up, w_down),
        scratch=[
            pltpu.VMEM((rows, width), F32),
            pltpu.VMEM((rows, width), BF),
            pltpu.VMEM((rows, hidden), BF),
        ],
        name="mlp",
        cost=pl.CostEstimate(
            flops=2 * rows * (width * width + 2 * width * hidden),
            transcendentals=rows * hidden,
            bytes_accessed=10**7,
        ),
    )


def fold_stage(keep, arrived, own):
    half, width = keep.shape
    quarter = half // 2

    def kernel(keep_ref, arrived_ref, own_ref, send, mine):
        side = lax.axis_index("head") >> 1
        mine_at = pl.multiple_of(side * quarter, quarter)
        send_at = pl.multiple_of((1 - side) * quarter, quarter)
        both = lambda at: (
            keep_ref[pl.ds(at, quarter)].astype(F32) + arrived_ref[pl.ds(at, quarter)].astype(F32)
        )
        send[...] = both(send_at).astype(BF)
        mine[...] = own_ref[...] + both(mine_at)

    outs = [
        jax.ShapeDtypeStruct((quarter, width), BF),
        jax.ShapeDtypeStruct((quarter, width), F32),
    ]
    return call(kernel, outs, (keep, arrived, own), name="fold", room=8)


def norm_stage(mine, arrived, gain):
    quarter, width = mine.shape
    groups = quarter // 4

    def kernel(mine_ref, arrived_ref, gain_ref, out, unit):
        total = mine_ref[...] + arrived_ref[...].astype(F32)
        normed = center_scale(total) * gain_ref[...].astype(F32)
        for c in range(width // 128):
            unit[c] = normed[:, c * 128 : (c + 1) * 128]
        for u in range(4):
            for c in range(width // 128):
                out[u * groups : (u + 1) * groups, c * 128 : (c + 1) * 128] = unit[
                    c, pl.ds(u, groups, stride=4)
                ].astype(BF)

    return call(
        kernel,
        [jax.ShapeDtypeStruct((quarter, width), BF)],
        (mine, arrived, gain),
        scratch=[pltpu.VMEM((width // 128, quarter, 128), F32)],
        name="norm",
        room=8,
    )[0]


def project(blk, weight, rows):
    quarter, width = blk[0].shape
    part = quarter // 4
    head_at = lax.axis_index("head")
    own = (head_at & 1) * 2 + (head_at >> 1)
    for e, piece in enumerate(blk):
        at = pl.multiple_of((own ^ ((e & 1) * 2 + (e >> 1))) * part, part)
        for u in range(4):
            rows[u, pl.ds(at, part)] = piece[u * part : (u + 1) * part]
    total = jnp.zeros((rows.shape[1], weight.shape[0]), F32)
    for u in range(4):
        total += lax.dot_general(
            rows[u],
            weight[:, u * width : (u + 1) * width],
            (((1,), (1,)), ((), ())),
            preferred_element_type=F32,
        )
    return total.astype(BF)


def merge_stage(pieces, w_merge):
    quarter, width = pieces[0].shape
    count = len(pieces)
    groups = count * quarter // 4

    def kernel(*refs):
        weight, out, rows = refs[count:]
        out[...] = project(refs[:count], weight, rows)

    return call(
        kernel,
        [jax.ShapeDtypeStruct((groups, w_merge.shape[0]), BF)],
        (*pieces, w_merge),
        scratch=[pltpu.VMEM((4, groups, width), BF)],
        name="merge",
        room=12,
    )[0]


def deliver_stage(earlier, pieces, w_merge, owners, owner_total, capacity):
    quarter, width = pieces[0].shape
    count = len(pieces)
    ahead = len(earlier)
    groups = count * quarter // 4
    everyone = owners.shape[1]
    local = w_merge.shape[0]
    slots = owner_total * capacity

    def kernel(*refs):
        done = refs[:ahead]
        weight, owner_ref, out, rows = refs[ahead + count :]
        owner = owner_ref[...]
        picks = owner == lax.broadcasted_iota(jnp.int32, (128, everyone), 0)
        above = lax.broadcasted_iota(jnp.int32, (everyone, everyone), 0) < lax.broadcasted_iota(
            jnp.int32, (everyone, everyone), 1
        )
        before = jnp.dot(picks.astype(BF), above.astype(BF), preferred_element_type=F32)
        rank = jnp.sum(jnp.where(picks, before, 0.0), axis=0, keepdims=True)
        slot = owner * capacity + rank.astype(jnp.int32)
        dispatch = (slot == lax.broadcasted_iota(jnp.int32, (slots, everyone), 0)).astype(BF)
        last = project(refs[ahead : ahead + count], weight, rows)
        whole = jnp.concatenate([d[...] for d in done] + [last], axis=0)
        out[...] = jnp.dot(dispatch, whole, preferred_element_type=F32).astype(BF)

    return call(
        kernel,
        [jax.ShapeDtypeStruct((slots, local), BF)],
        (*earlier, *pieces, w_merge, owners),
        scratch=[pltpu.VMEM((4, groups, width), BF)],
        name="deliver",
        room=12,
    )[0]


def per_device(
    tokens,
    segment_ids,
    valid,
    owners,
    ln1_gain,
    w_qkv,
    w_out,
    ln2_gain,
    w_up,
    w_down,
    ln3_gain,
    w_merge,
):
    rows, width = tokens.shape
    heads = w_qkv.shape[2] // HEAD_DIM
    tok_total = lax.axis_size("tok")
    head_total = lax.axis_size("head")
    over_tok = lambda value, mask: lax.ppermute(value, "tok", swap_pairs(tok_total, mask))
    over_head = lambda value, mask: lax.ppermute(value, "head", swap_pairs(head_total, mask))
    teams = [list(range(g, g + heads)) for g in range(0, tok_total, heads)]
    in_team = lambda value: lax.all_to_all(
        value, "tok", 0, 0, tiled=True, axis_index_groups=teams
    )

    def all_heads(value):
        side = over_head(value, 2)
        return [value, over_head(value, 1), side, over_head(side, 1)]

    w_outs = all_heads(w_out)
    near, far = qkv_stage(
        tokens,
        ln1_gain.reshape(1, width),
        jnp.swapaxes(w_qkv, 1, 2),
        segment_ids.reshape(1, -1),
        valid.reshape(1, -1),
        heads,
    )
    far_in = [over_tok(far[k & (heads - 1)], k) for k in range(heads, tok_total)]
    queries, tops, sums, low_high = near_stage(in_team(near), tok_total)
    mixed = far_stage(far_in, queries, tops, sums, low_high, tok_total)
    att = in_team(mixed).reshape(heads * HEAD_DIM, rows)

    chunk = rows // CHUNKS
    merged = []
    for c in range(CHUNKS):
        attended = all_heads(att[:, c * chunk : (c + 1) * chunk])
        keep, send, own = mlp_stage(
            c * chunk, tokens, attended, w_outs, ln2_gain.reshape(1, width), w_up, w_down
        )
        send, mine = fold_stage(keep, over_head(send, 1), own)
        merged.append(
            all_heads(norm_stage(mine, over_head(send, 2), ln3_gain.reshape(1, width)))
        )

    groups = rows // 4
    capacity = max(2, 2 * groups // tok_total)
    turned = w_merge.T
    earlier = [merge_stage(m, turned) for m in merged[:-1]]
    outgoing = deliver_stage(
        earlier, merged[-1], turned, owners.reshape(1, -1), tok_total, capacity
    )
    outgoing = outgoing.reshape(tok_total, capacity, outgoing.shape[1])
    received = lax.all_to_all(outgoing, "tok", split_axis=0, concat_axis=0, tiled=True)
    return received.reshape(tok_total * capacity, outgoing.shape[2])


def solution(mesh):
    in_specs = (
        P("tok", None),
        P("tok"),
        P("tok"),
        P("tok", None),
        P(),
        P(None, None, "head"),
        P("head", None),
        P(),
        P(None, "head"),
        P("head", None),
        P(),
        P(None, "head"),
    )
    out_specs = P("tok", "head")
    return jax.shard_map(
        per_device, mesh=mesh, in_specs=in_specs, out_specs=out_specs, check_vma=False
    )
```

```python
import math

import jax
import jax.numpy as jnp
from jax import lax
from jax.experimental import pallas as pl
from jax.experimental.pallas import tpu as pltpu
from jax.sharding import PartitionSpec as P

HEAD_DIM = 88
EXT = 128
VEXT = 96
GONE = 64.0
FAR = -1e30
BF = jnp.bfloat16
F32 = jnp.float32
CHUNKS = 2
FLYING = 2


def swap_pairs(size, mask):
    return [(i, i ^ mask) for i in range(size)]


def center_scale(values):
    center = values - jnp.mean(values, axis=-1, keepdims=True)
    spread = jnp.mean(center * center, axis=-1, keepdims=True)
    return center * lax.rsqrt(spread + 1e-06)


SMEM = pl.BlockSpec(memory_space=pltpu.SMEM)
VM = pl.BlockSpec(memory_space=pltpu.VMEM)
HBM = pl.BlockSpec(memory_space=pltpu.HBM)


def call(kernel, outs, args, specs=None, out_specs=None, scratch=(), name=None, room=24, cost=None):
    specs = specs if specs is not None else [VM] * len(args)
    out_specs = out_specs if out_specs is not None else [VM] * len(outs)
    spaces = {id(VM): pltpu.VMEM, id(HBM): pltpu.HBM}
    args = [
        pltpu.with_memory_space_constraint(a, spaces[id(s)]) if id(s) in spaces else a
        for a, s in zip(args, specs)
    ]
    outs = [
        spaces[id(s)](o.shape, o.dtype) if id(s) in spaces else o for o, s in zip(outs, out_specs)
    ]
    return pl.pallas_call(
        kernel,
        out_shape=outs,
        in_specs=specs,
        out_specs=out_specs,
        scratch_shapes=scratch,
        compiler_params=pltpu.CompilerParams(vmem_limit_bytes=room * 1024 * 1024),
        cost_estimate=cost,
        name=name,
    )(*args)


def qkv_stage(tokens, gain, w_qkv, seg, valid, heads):
    rows, width = tokens.shape
    local = w_qkv.shape[1]
    scale = math.log2(math.e) / math.sqrt(HEAD_DIM)
    far_rows = VEXT + HEAD_DIM
    near_rows = far_rows + HEAD_DIM
    strip = math.gcd(rows, 128)

    def kernel(tok_hbm, gain_ref, w_hbm, seg_hbm, valid_hbm, *rest):
        near = rest[0]
        far = rest[1 : 1 + heads]
        tok, weight, normed, seg_ref, valid_ref, sem = rest[1 + heads :]
        tok_copy = pltpu.make_async_copy(tok_hbm, tok, sem.at[3])
        tok_copy.start()
        seg_copy = pltpu.make_async_copy(seg_hbm, seg_ref, sem.at[4])
        seg_copy.start()
        valid_copy = pltpu.make_async_copy(valid_hbm, valid_ref, sem.at[5])
        valid_copy.start()
        copies = [pltpu.make_async_copy(w_hbm.at[i], weight.at[i], sem.at[i]) for i in range(3)]
        for i in (1, 2, 0):
            copies[i].start()
        spread_to = lax.broadcasted_iota(jnp.int32, (rows // 4, rows), 1) // 4
        spread_from = lax.broadcasted_iota(jnp.int32, (rows // 4, rows), 0)
        spread = (spread_to == spread_from).astype(BF)
        seg_copy.wait()
        valid_copy.wait()
        seg8 = jnp.broadcast_to(seg_ref[...].astype(F32), (8, rows // 4)).astype(BF)
        tags = jnp.dot(seg8, spread, preferred_element_type=F32)
        gone = jnp.where(valid_ref[...] == 1, 0.0, GONE)
        tags = (tags + jnp.broadcast_to(gone, (8, rows))).astype(BF)
        gains = gain_ref[...].astype(F32)
        tok_copy.wait()
        for i in range(rows // strip):
            at = slice(i * strip, (i + 1) * strip)
            normed[at] = (center_scale(tok[at].astype(F32)) * gains).astype(BF)

        for i, place in ((1, 0), (2, VEXT), (0, far_rows)):
            copies[i].wait()
            turned = lax.dot_general(
                weight[i], normed[...], (((1,), (1,)), ((), ())), preferred_element_type=F32
            )
            if i == 0:
                turned = turned * scale
            for h in range(heads):
                near[h, place : place + HEAD_DIM] = turned[
                    h * HEAD_DIM : (h + 1) * HEAD_DIM
                ].astype(BF)
        turn = lax.axis_index("tok") & (heads - 1)
        for h in range(heads):
            near[h, HEAD_DIM:VEXT] = tags
        for j in range(heads):
            far[j][...] = near[turn ^ j, 0:far_rows]

    outs = [jax.ShapeDtypeStruct((heads, near_rows, rows), BF)]
    outs += [jax.ShapeDtypeStruct((far_rows, rows), BF)] * heads
    result = call(
        kernel,
        outs,
        (tokens, gain, w_qkv, seg, valid),
        specs=[HBM, VM, HBM, HBM, HBM],
        scratch=[
            pltpu.VMEM((rows, width), BF),
            pltpu.VMEM((3, local, width), BF),
            pltpu.VMEM((rows, width), BF),
            pltpu.VMEM((1, rows // 4), jnp.int32),
            pltpu.VMEM((1, rows), jnp.int32),
            pltpu.SemaphoreType.DMA((6,)),
        ],
        name="qkv",
        cost=pl.CostEstimate(flops=4 * 10**9, transcendentals=0, bytes_accessed=10**7),
    )
    return result[0], result[1:]


def load_keys(block_ref, keys, values, segments):
    rows = block_ref.shape[1]
    top = block_ref[0:VEXT].astype(F32)
    tags = top[HEAD_DIM : HEAD_DIM + 1]
    gone = tags >= GONE
    seg = jnp.where(gone, tags - GONE, tags)
    mark = jnp.where(gone, float(segments), tags)
    line = lax.broadcasted_iota(jnp.int32, (EXT, rows), 0) - HEAD_DIM
    hot = (line.astype(F32) == mark).astype(F32)
    head_part = jnp.where(line[0:VEXT] >= 0, hot[0:VEXT], top)
    keys[:, 0:VEXT] = head_part.T.astype(BF)
    keys[:, VEXT:EXT] = hot[VEXT:EXT].T.astype(BF)
    vals = block_ref[VEXT : VEXT + HEAD_DIM].astype(F32)
    ones = jnp.ones((VEXT - HEAD_DIM, rows), F32)
    values[...] = jnp.concatenate([vals, ones], axis=0).astype(BF)
    return jnp.min(seg), jnp.max(seg)


def absorb(keys, values, query, top, sums):
    scores = jnp.dot(keys[...], query[...], preferred_element_type=F32)
    newest = jnp.maximum(top[...], jnp.max(scores, axis=0, keepdims=True))
    weights = jnp.exp2(scores - newest).astype(BF)
    factor = jnp.exp2(top[...] - newest)
    sums[...] = sums[...] * factor + jnp.dot(values[...], weights, preferred_element_type=F32)
    top[...] = newest


def near_stage(blocks, segments):
    count, _, rows = blocks.shape
    query_at = VEXT + HEAD_DIM

    def kernel(blk, queries, tops, sums, low_high, keys, values):
        bounds = []
        for b in range(count):
            bounds.append(load_keys(blk.at[b], keys.at[b], values.at[b], segments))
            low_high[2 * b] = bounds[b][0]
            low_high[2 * b + 1] = bounds[b][1]
        for j in range(count):
            query = blk[j, query_at : query_at + HEAD_DIM].astype(F32)
            top = blk[j, 0:VEXT].astype(F32)
            tags = top[HEAD_DIM : HEAD_DIM + 1]
            gone = tags >= GONE
            seg = jnp.where(gone, tags - GONE, tags)
            line = lax.broadcasted_iota(jnp.int32, (EXT - HEAD_DIM, rows), 0).astype(F32)
            wall = jnp.where(line == seg, 0.0, FAR)
            queries[j] = jnp.concatenate([query, wall], axis=0).astype(BF)
            own = jnp.sum(query * top[0:HEAD_DIM], axis=0, keepdims=True)
            tops[j] = jnp.where(gone, own, FAR)
            sums[j] = jnp.where(gone, values[j].astype(F32), 0.0)
        for j in range(count):
            for b in range(count):

                @pl.when((bounds[b][0] <= bounds[j][1]) & (bounds[b][1] >= bounds[j][0]))
                def _():
                    absorb(keys.at[b], values.at[b], queries.at[j], tops.at[j], sums.at[j])

    outs = [
        jax.ShapeDtypeStruct((count, EXT, rows), BF),
        jax.ShapeDtypeStruct((count, 1, rows), F32),
        jax.ShapeDtypeStruct((count, VEXT, rows), F32),
        jax.ShapeDtypeStruct((2 * count,), F32),
    ]
    return call(
        kernel,
        outs,
        (blocks,),
        out_specs=[VM, VM, VM, SMEM],
        scratch=[pltpu.VMEM((count, rows, EXT), BF), pltpu.VMEM((count, VEXT, rows), BF)],
        name="near",
        cost=pl.CostEstimate(flops=8 * 10**9, transcendentals=4 * 10**6, bytes_accessed=10**7),
    )


def far_stage(blocks, queries, tops, sums, low_high, segments):
    count = len(blocks)
    heads, _, rows = queries.shape

    def kernel(*refs):
        blk = refs[:count]
        query_ref, top_ref, sum_ref, bound_ref = refs[count : count + 4]
        out, keys, values, top, total, ready, sem = refs[count + 4 :]
        leave = [pltpu.make_async_copy(ready.at[j], out.at[j], sem.at[j]) for j in range(heads)]
        bounds = [load_keys(blk[b], keys.at[b], values.at[b], segments) for b in range(count)]
        for j in range(heads):
            top[...] = top_ref[j]
            total[...] = sum_ref[j]
            for b in range(count):

                @pl.when((bounds[b][0] <= bound_ref[2 * j + 1]) & (bounds[b][1] >= bound_ref[2 * j]))
                def _():
                    absorb(keys.at[b], values.at[b], query_ref.at[j], top, total)

            whole = total[...]
            ready[j] = (whole[0:HEAD_DIM] / whole[HEAD_DIM : HEAD_DIM + 1]).astype(BF)
            leave[j].start()
        for j in range(heads):
            leave[j].wait()

    return call(
        kernel,
        [jax.ShapeDtypeStruct((heads, HEAD_DIM, rows), BF)],
        (*blocks, queries, tops, sums, low_high),
        specs=[VM] * (count + 3) + [SMEM],
        out_specs=[HBM],
        scratch=[
            pltpu.VMEM((count, rows, EXT), BF),
            pltpu.VMEM((count, VEXT, rows), BF),
            pltpu.VMEM((1, rows), F32),
            pltpu.VMEM((VEXT, rows), F32),
            pltpu.VMEM((heads, HEAD_DIM, rows), BF),
            pltpu.SemaphoreType.DMA((heads,)),
        ],
        name="far",
        cost=pl.CostEstimate(flops=6 * 10**9, transcendentals=4 * 10**6, bytes_accessed=10**7),
    )[0]


def mlp_stage(first, tokens, attended, w_outs, gain, w_up, w_down):
    width = tokens.shape[1]
    part, rows = attended[0].shape
    pieces = len(attended)
    hidden = w_up.shape[1]
    half, quarter = rows // 2, rows // 4

    def kernel(tok_ref, *refs):
        att = refs[:pieces]
        wout = refs[pieces : 2 * pieces]
        gain_ref, up_hbm, down_hbm, keep, send, own, stream, second, act, up, down, sem = refs[
            2 * pieces :
        ]
        up_copy = pltpu.make_async_copy(up_hbm, up, sem.at[0])
        up_copy.start()
        down_copy = pltpu.make_async_copy(down_hbm, down, sem.at[1])
        down_copy.start()
        head_at = lax.axis_index("head")
        core, side = head_at & 1, head_at >> 1
        total = tok_ref[first : first + rows].astype(F32)
        for e in range(pieces):
            total += jnp.dot(
                att[e][...].astype(F32).T.astype(BF), wout[e][...], preferred_element_type=F32
            )
        stream[...] = total
        own[...] = stream[pl.ds(pl.multiple_of((core * 2 + side) * quarter, quarter), quarter)]
        second[...] = (center_scale(stream[...]) * gain_ref[...].astype(F32)).astype(BF)
        up_copy.wait()
        pre = jnp.dot(second[...], up[...], preferred_element_type=F32)
        act[...] = (0.5 * pre * (1.0 + lax.erf(pre * math.sqrt(0.5)))).astype(BF)
        down_copy.wait()
        stream[...] = jnp.dot(act[...], down[...], preferred_element_type=F32)
        keep[...] = stream[pl.ds(pl.multiple_of(core * half, half), half)].astype(BF)
        send[...] = stream[pl.ds(pl.multiple_of((1 - core) * half, half), half)].astype(BF)

    outs = [
        jax.ShapeDtypeStruct((half, width), BF),
        jax.ShapeDtypeStruct((half, width), BF),
        jax.ShapeDtypeStruct((quarter, width), F32),
    ]
    return call(
        kernel,
        outs,
        (tokens, *attended, *w_outs, gain, w_up, w_down),
        specs=[VM] * (2 + 2 * pieces) + [HBM, HBM],
        scratch=[
            pltpu.VMEM((rows, width), F32),
            pltpu.VMEM((rows, width), BF),
            pltpu.VMEM((rows, hidden), BF),
            pltpu.VMEM((width, hidden), BF),
            pltpu.VMEM((hidden, width), BF),
            pltpu.SemaphoreType.DMA((2,)),
        ],
        name="mlp",
        cost=pl.CostEstimate(
            flops=2 * rows * (width * width + 2 * width * hidden),
            transcendentals=rows * hidden,
            bytes_accessed=10**7,
        ),
    )


def fold_stage(keep, arrived, own):
    half, width = keep.shape
    quarter = half // 2

    def kernel(keep_ref, arrived_ref, own_ref, send, mine):
        side = lax.axis_index("head") >> 1
        mine_at = pl.multiple_of(side * quarter, quarter)
        send_at = pl.multiple_of((1 - side) * quarter, quarter)
        both = lambda at: (
            keep_ref[pl.ds(at, quarter)].astype(F32) + arrived_ref[pl.ds(at, quarter)].astype(F32)
        )
        send[...] = both(send_at).astype(BF)
        mine[...] = own_ref[...] + both(mine_at)

    outs = [
        jax.ShapeDtypeStruct((quarter, width), BF),
        jax.ShapeDtypeStruct((quarter, width), F32),
    ]
    return call(kernel, outs, (keep, arrived, own), name="fold", room=8)


def norm_stage(mine, arrived, gain):
    quarter, width = mine.shape
    groups = quarter // 4

    def kernel(mine_ref, arrived_ref, gain_ref, out, unit):
        total = mine_ref[...] + arrived_ref[...].astype(F32)
        normed = center_scale(total) * gain_ref[...].astype(F32)
        for c in range(width // 128):
            unit[c] = normed[:, c * 128 : (c + 1) * 128]
        for u in range(4):
            for c in range(width // 128):
                out[u * groups : (u + 1) * groups, c * 128 : (c + 1) * 128] = unit[
                    c, pl.ds(u, groups, stride=4)
                ].astype(BF)

    return call(
        kernel,
        [jax.ShapeDtypeStruct((quarter, width), BF)],
        (mine, arrived, gain),
        scratch=[pltpu.VMEM((width // 128, quarter, 128), F32)],
        name="norm",
        room=8,
    )[0]


def project(blk, weight, rows):
    quarter, width = blk[0].shape
    part = quarter // 4
    head_at = lax.axis_index("head")
    own = (head_at & 1) * 2 + (head_at >> 1)
    for e, piece in enumerate(blk):
        at = pl.multiple_of((own ^ ((e & 1) * 2 + (e >> 1))) * part, part)
        for u in range(4):
            rows[u, pl.ds(at, part)] = piece[u * part : (u + 1) * part]
    total = jnp.zeros((rows.shape[1], weight.shape[0]), F32)
    for u in range(4):
        total += lax.dot_general(
            rows[u],
            weight[:, u * width : (u + 1) * width],
            (((1,), (1,)), ((), ())),
            preferred_element_type=F32,
        )
    return total.astype(BF)


def merge_stage(pieces, w_merge):
    quarter, width = pieces[0].shape
    count = len(pieces)
    groups = count * quarter // 4

    def kernel(*refs):
        weight, out, rows = refs[count:]
        out[...] = project(refs[:count], weight, rows)

    return call(
        kernel,
        [jax.ShapeDtypeStruct((groups, w_merge.shape[0]), BF)],
        (*pieces, w_merge),
        scratch=[pltpu.VMEM((4, groups, width), BF)],
        name="merge",
        room=12,
    )[0]


def deliver_stage(earlier, pieces, w_merge, owners, owner_total, capacity):
    quarter, width = pieces[0].shape
    count = len(pieces)
    ahead = len(earlier)
    groups = count * quarter // 4
    everyone = owners.shape[1]
    local = w_merge.shape[0]
    slots = owner_total * capacity

    def kernel(*refs):
        done = refs[:ahead]
        weight, owner_ref, out, rows = refs[ahead + count :]
        owner = owner_ref[...]
        picks = owner == lax.broadcasted_iota(jnp.int32, (128, everyone), 0)
        above = lax.broadcasted_iota(jnp.int32, (everyone, everyone), 0) < lax.broadcasted_iota(
            jnp.int32, (everyone, everyone), 1
        )
        before = jnp.dot(picks.astype(BF), above.astype(BF), preferred_element_type=F32)
        rank = jnp.sum(jnp.where(picks, before, 0.0), axis=0, keepdims=True)
        slot = owner * capacity + rank.astype(jnp.int32)
        dispatch = (slot == lax.broadcasted_iota(jnp.int32, (slots, everyone), 0)).astype(BF)
        last = project(refs[ahead : ahead + count], weight, rows)
        whole = jnp.concatenate([d[...] for d in done] + [last], axis=0)
        out[...] = jnp.dot(dispatch, whole, preferred_element_type=F32).astype(BF)

    return call(
        kernel,
        [jax.ShapeDtypeStruct((slots, local), BF)],
        (*earlier, *pieces, w_merge, owners),
        scratch=[pltpu.VMEM((4, groups, width), BF)],
        name="deliver",
        room=12,
    )[0]


def per_device(
    tokens,
    segment_ids,
    valid,
    owners,
    ln1_gain,
    w_qkv,
    w_out,
    ln2_gain,
    w_up,
    w_down,
    ln3_gain,
    w_merge,
):
    rows, width = tokens.shape
    heads = w_qkv.shape[2] // HEAD_DIM
    tok_total = lax.axis_size("tok")
    head_total = lax.axis_size("head")
    over_tok = lambda value, mask: lax.ppermute(value, "tok", swap_pairs(tok_total, mask))
    over_head = lambda value, mask: lax.ppermute(value, "head", swap_pairs(head_total, mask))
    teams = [list(range(g, g + heads)) for g in range(0, tok_total, heads)]
    in_team = lambda value: lax.all_to_all(
        value, "tok", 0, 0, tiled=True, axis_index_groups=teams
    )

    def all_heads(value):
        side = over_head(value, 2)
        return [value, over_head(value, 1), side, over_head(side, 1)]

    w_outs = all_heads(w_out)
    near, far = qkv_stage(
        tokens,
        ln1_gain.reshape(1, width),
        jnp.swapaxes(w_qkv, 1, 2),
        segment_ids.reshape(1, -1),
        valid.reshape(1, -1),
        heads,
    )
    far_in = []
    for k in range(heads, tok_total):
        leaving = far[k & (heads - 1)]
        if len(far_in) >= FLYING:
            leaving, far_in[-FLYING] = lax.optimization_barrier((leaving, far_in[-FLYING]))
        far_in.append(over_tok(leaving, k))
    queries, tops, sums, low_high = near_stage(in_team(near), tok_total)
    mixed = far_stage(far_in, queries, tops, sums, low_high, tok_total)
    att = in_team(mixed).reshape(heads * HEAD_DIM, rows)

    chunk = rows // CHUNKS
    merged = []
    attends = [all_heads(att[:, c * chunk : (c + 1) * chunk]) for c in range(CHUNKS)]
    for c, attended in enumerate(attends):
        if c:
            attended[0], send = lax.optimization_barrier((attended[0], send))
        keep, send, own = mlp_stage(
            c * chunk, tokens, attended, w_outs, ln2_gain.reshape(1, width), w_up, w_down
        )
        send, mine = fold_stage(keep, over_head(send, 1), own)
        arrived = over_head(send, 2)
        merged.append((mine, arrived))
    merged = [all_heads(norm_stage(*m, ln3_gain.reshape(1, width))) for m in merged]

    groups = rows // 4
    capacity = max(2, 2 * groups // tok_total)
    turned = w_merge.T
    earlier = [merge_stage(m, turned) for m in merged[:-1]]
    outgoing = deliver_stage(
        earlier, merged[-1], turned, owners.reshape(1, -1), tok_total, capacity
    )
    outgoing = outgoing.reshape(tok_total, capacity, outgoing.shape[1])
    received = lax.all_to_all(outgoing, "tok", split_axis=0, concat_axis=0, tiled=True)
    return received.reshape(tok_total * capacity, outgoing.shape[2])


def solution(mesh):
    in_specs = (
        P("tok", None),
        P("tok"),
        P("tok"),
        P("tok", None),
        P(),
        P(None, None, "head"),
        P("head", None),
        P(),
        P(None, "head"),
        P("head", None),
        P(),
        P(None, "head"),
    )
    out_specs = P("tok", "head")
    return jax.shard_map(
        per_device, mesh=mesh, in_specs=in_specs, out_specs=out_specs, check_vma=False
    )
```

```python
import math

import jax
import jax.numpy as jnp
from jax import lax
from jax.experimental import pallas as pl
from jax.experimental.pallas import tpu as pltpu
from jax.sharding import PartitionSpec as P

HEAD_DIM = 88
EXT = 128
VEXT = 96
GONE = 64.0
FAR = -1e30
BF = jnp.bfloat16
F32 = jnp.float32
CHUNKS = 2
FLYING = 2
SPLIT = 2


def swap_pairs(size, mask):
    return [(i, i ^ mask) for i in range(size)]


def center_scale(values):
    center = values - jnp.mean(values, axis=-1, keepdims=True)
    spread = jnp.mean(center * center, axis=-1, keepdims=True)
    return center * lax.rsqrt(spread + 1e-06)


SMEM = pl.BlockSpec(memory_space=pltpu.SMEM)
VM = pl.BlockSpec(memory_space=pltpu.VMEM)
HBM = pl.BlockSpec(memory_space=pltpu.HBM)


def call(kernel, outs, args, specs=None, out_specs=None, scratch=(), name=None, room=24, cost=None):
    specs = specs if specs is not None else [VM] * len(args)
    out_specs = out_specs if out_specs is not None else [VM] * len(outs)
    spaces = {id(VM): pltpu.VMEM, id(HBM): pltpu.HBM}
    args = [
        pltpu.with_memory_space_constraint(a, spaces[id(s)]) if id(s) in spaces else a
        for a, s in zip(args, specs)
    ]
    outs = [
        spaces[id(s)](o.shape, o.dtype) if id(s) in spaces else o for o, s in zip(outs, out_specs)
    ]
    return pl.pallas_call(
        kernel,
        out_shape=outs,
        in_specs=specs,
        out_specs=out_specs,
        scratch_shapes=scratch,
        compiler_params=pltpu.CompilerParams(vmem_limit_bytes=room * 1024 * 1024),
        cost_estimate=cost,
        name=name,
    )(*args)


def qkv_stage(tokens, gain, w_qkv, seg, valid, heads):
    rows, width = tokens.shape
    local = w_qkv.shape[1]
    scale = math.log2(math.e) / math.sqrt(HEAD_DIM)
    far_rows = VEXT + HEAD_DIM
    near_rows = far_rows + HEAD_DIM
    strip = math.gcd(rows, 128)

    def kernel(tok_hbm, gain_ref, w_hbm, seg_hbm, valid_hbm, *rest):
        near = rest[0]
        far = rest[1 : 1 + heads]
        tok, weight, normed, seg_ref, valid_ref, sem = rest[1 + heads :]
        tok_copy = pltpu.make_async_copy(tok_hbm, tok, sem.at[3])
        tok_copy.start()
        seg_copy = pltpu.make_async_copy(seg_hbm, seg_ref, sem.at[4])
        seg_copy.start()
        valid_copy = pltpu.make_async_copy(valid_hbm, valid_ref, sem.at[5])
        valid_copy.start()
        copies = [pltpu.make_async_copy(w_hbm.at[i], weight.at[i], sem.at[i]) for i in range(3)]
        for i in (1, 2, 0):
            copies[i].start()
        spread_to = lax.broadcasted_iota(jnp.int32, (rows // 4, rows), 1) // 4
        spread_from = lax.broadcasted_iota(jnp.int32, (rows // 4, rows), 0)
        spread = (spread_to == spread_from).astype(BF)
        seg_copy.wait()
        valid_copy.wait()
        seg8 = jnp.broadcast_to(seg_ref[...].astype(F32), (8, rows // 4)).astype(BF)
        tags = jnp.dot(seg8, spread, preferred_element_type=F32)
        gone = jnp.where(valid_ref[...] == 1, 0.0, GONE)
        tags = (tags + jnp.broadcast_to(gone, (8, rows))).astype(BF)
        gains = gain_ref[...].astype(F32)
        tok_copy.wait()
        for i in range(rows // strip):
            at = slice(i * strip, (i + 1) * strip)
            normed[at] = (center_scale(tok[at].astype(F32)) * gains).astype(BF)

        for i, place in ((1, 0), (2, VEXT), (0, far_rows)):
            copies[i].wait()
            turned = lax.dot_general(
                weight[i], normed[...], (((1,), (1,)), ((), ())), preferred_element_type=F32
            )
            if i == 0:
                turned = turned * scale
            for h in range(heads):
                near[h, place : place + HEAD_DIM] = turned[
                    h * HEAD_DIM : (h + 1) * HEAD_DIM
                ].astype(BF)
        turn = lax.axis_index("tok") & (heads - 1)
        for h in range(heads):
            near[h, HEAD_DIM:VEXT] = tags
        for j in range(heads):
            far[j][...] = near[turn ^ j, 0:far_rows]

    outs = [jax.ShapeDtypeStruct((heads, near_rows, rows), BF)]
    outs += [jax.ShapeDtypeStruct((far_rows, rows), BF)] * heads
    result = call(
        kernel,
        outs,
        (tokens, gain, w_qkv, seg, valid),
        specs=[HBM, VM, HBM, HBM, HBM],
        scratch=[
            pltpu.VMEM((rows, width), BF),
            pltpu.VMEM((3, local, width), BF),
            pltpu.VMEM((rows, width), BF),
            pltpu.VMEM((1, rows // 4), jnp.int32),
            pltpu.VMEM((1, rows), jnp.int32),
            pltpu.SemaphoreType.DMA((6,)),
        ],
        name="qkv",
        cost=pl.CostEstimate(flops=4 * 10**9, transcendentals=0, bytes_accessed=10**7),
    )
    return result[0], result[1:]


def load_keys(block_ref, keys, values, segments):
    rows = block_ref.shape[1]
    top = block_ref[0:VEXT].astype(F32)
    tags = top[HEAD_DIM : HEAD_DIM + 1]
    gone = tags >= GONE
    seg = jnp.where(gone, tags - GONE, tags)
    mark = jnp.where(gone, float(segments), tags)
    line = lax.broadcasted_iota(jnp.int32, (EXT, rows), 0) - HEAD_DIM
    hot = (line.astype(F32) == mark).astype(F32)
    head_part = jnp.where(line[0:VEXT] >= 0, hot[0:VEXT], top)
    keys[:, 0:VEXT] = head_part.T.astype(BF)
    keys[:, VEXT:EXT] = hot[VEXT:EXT].T.astype(BF)
    vals = block_ref[VEXT : VEXT + HEAD_DIM].astype(F32)
    ones = jnp.ones((VEXT - HEAD_DIM, rows), F32)
    values[...] = jnp.concatenate([vals, ones], axis=0).astype(BF)
    return jnp.min(seg), jnp.max(seg)


def absorb(keys, values, query, top, sums):
    scores = jnp.dot(keys[...], query[...], preferred_element_type=F32)
    newest = jnp.maximum(top[...], jnp.max(scores, axis=0, keepdims=True))
    weights = jnp.exp2(scores - newest).astype(BF)
    factor = jnp.exp2(top[...] - newest)
    sums[...] = sums[...] * factor + jnp.dot(values[...], weights, preferred_element_type=F32)
    top[...] = newest


def near_stage(blocks, segments):
    count, _, rows = blocks.shape
    query_at = VEXT + HEAD_DIM

    def kernel(blk, queries, tops, sums, low_high, keys, values):
        bounds = []
        for b in range(count):
            bounds.append(load_keys(blk.at[b], keys.at[b], values.at[b], segments))
            low_high[2 * b] = bounds[b][0]
            low_high[2 * b + 1] = bounds[b][1]
        for j in range(count):
            query = blk[j, query_at : query_at + HEAD_DIM].astype(F32)
            top = blk[j, 0:VEXT].astype(F32)
            tags = top[HEAD_DIM : HEAD_DIM + 1]
            gone = tags >= GONE
            seg = jnp.where(gone, tags - GONE, tags)
            line = lax.broadcasted_iota(jnp.int32, (EXT - HEAD_DIM, rows), 0).astype(F32)
            wall = jnp.where(line == seg, 0.0, FAR)
            queries[j] = jnp.concatenate([query, wall], axis=0).astype(BF)
            own = jnp.sum(query * top[0:HEAD_DIM], axis=0, keepdims=True)
            tops[j] = jnp.where(gone, own, FAR)
            sums[j] = jnp.where(gone, values[j].astype(F32), 0.0)
        for j in range(count):
            for b in range(count):

                @pl.when((bounds[b][0] <= bounds[j][1]) & (bounds[b][1] >= bounds[j][0]))
                def _():
                    absorb(keys.at[b], values.at[b], queries.at[j], tops.at[j], sums.at[j])

    outs = [
        jax.ShapeDtypeStruct((count, EXT, rows), BF),
        jax.ShapeDtypeStruct((count, 1, rows), F32),
        jax.ShapeDtypeStruct((count, VEXT, rows), F32),
        jax.ShapeDtypeStruct((2 * count,), F32),
    ]
    return call(
        kernel,
        outs,
        (blocks,),
        out_specs=[VM, VM, VM, SMEM],
        scratch=[pltpu.VMEM((count, rows, EXT), BF), pltpu.VMEM((count, VEXT, rows), BF)],
        name="near",
        cost=pl.CostEstimate(flops=8 * 10**9, transcendentals=4 * 10**6, bytes_accessed=10**7),
    )


def far_stage(blocks, queries, tops, sums, low_high, segments):
    count = len(blocks)
    heads, _, rows = queries.shape

    def kernel(*refs):
        blk = refs[:count]
        query_ref, top_ref, sum_ref, bound_ref = refs[count : count + 4]
        out, keys, values, top, total, ready, sem = refs[count + 4 :]
        leave = [pltpu.make_async_copy(ready.at[j], out.at[j], sem.at[j]) for j in range(heads)]
        bounds = [load_keys(blk[b], keys.at[b], values.at[b], segments) for b in range(count)]
        for j in range(heads):
            top[...] = top_ref[j]
            total[...] = sum_ref[j]
            for b in range(count):

                @pl.when((bounds[b][0] <= bound_ref[2 * j + 1]) & (bounds[b][1] >= bound_ref[2 * j]))
                def _():
                    absorb(keys.at[b], values.at[b], query_ref.at[j], top, total)

            whole = total[...]
            ready[j] = (whole[0:HEAD_DIM] / whole[HEAD_DIM : HEAD_DIM + 1]).astype(BF)
            leave[j].start()
        for j in range(heads):
            leave[j].wait()

    return call(
        kernel,
        [jax.ShapeDtypeStruct((heads, HEAD_DIM, rows), BF)],
        (*blocks, queries, tops, sums, low_high),
        specs=[VM] * (count + 3) + [SMEM],
        out_specs=[HBM],
        scratch=[
            pltpu.VMEM((count, rows, EXT), BF),
            pltpu.VMEM((count, VEXT, rows), BF),
            pltpu.VMEM((1, rows), F32),
            pltpu.VMEM((VEXT, rows), F32),
            pltpu.VMEM((heads, HEAD_DIM, rows), BF),
            pltpu.SemaphoreType.DMA((heads,)),
        ],
        name="far",
        cost=pl.CostEstimate(flops=6 * 10**9, transcendentals=4 * 10**6, bytes_accessed=10**7),
    )[0]


def mlp_stage(first, tokens, attended, w_outs, gain, w_up, w_down):
    width = tokens.shape[1]
    part, rows = attended[0].shape
    pieces = len(attended)
    hidden = w_up.shape[1]
    half, quarter = rows // 2, rows // 4

    def kernel(tok_ref, *refs):
        att = refs[:pieces]
        wout = refs[pieces : 2 * pieces]
        gain_ref, up_hbm, down_hbm, keep, own = refs[2 * pieces : 2 * pieces + 5]
        sends = refs[2 * pieces + 5 : 2 * pieces + 5 + SPLIT]
        stream, second, act, up, down, sem = refs[2 * pieces + 5 + SPLIT :]
        up_copy = pltpu.make_async_copy(up_hbm, up, sem.at[0])
        up_copy.start()
        down_copy = pltpu.make_async_copy(down_hbm, down, sem.at[1])
        head_at = lax.axis_index("head")
        core, side = head_at & 1, head_at >> 1
        total = tok_ref[first : first + rows].astype(F32)
        for e in range(pieces):
            total += jnp.dot(
                att[e][...].astype(F32).T.astype(BF), wout[e][...], preferred_element_type=F32
            )
        stream[...] = total
        own[...] = stream[pl.ds(pl.multiple_of((core * 2 + side) * quarter, quarter), quarter)]
        second[...] = (center_scale(stream[...]) * gain_ref[...].astype(F32)).astype(BF)
        up_copy.wait()
        down_copy.start()
        pre = jnp.dot(second[...], up[...], preferred_element_type=F32)
        act[...] = (0.5 * pre * (1.0 + lax.erf(pre * math.sqrt(0.5)))).astype(BF)
        down_copy.wait()
        stream[...] = jnp.dot(act[...], down[...], preferred_element_type=F32)
        keep[...] = stream[pl.ds(pl.multiple_of(core * half, half), half)].astype(BF)
        for i in range(SPLIT):
            at = pl.multiple_of((1 - core) * half + i * (half // SPLIT), half // SPLIT)
            sends[i][...] = stream[pl.ds(at, half // SPLIT)].astype(BF)

    outs = [
        jax.ShapeDtypeStruct((half, width), BF),
        jax.ShapeDtypeStruct((quarter, width), F32),
    ]
    outs += [jax.ShapeDtypeStruct((half // SPLIT, width), BF)] * SPLIT
    return call(
        kernel,
        outs,
        (tokens, *attended, *w_outs, gain, w_up, w_down),
        specs=[VM] * (2 + 2 * pieces) + [HBM, HBM],
        scratch=[
            pltpu.VMEM((rows, width), F32),
            pltpu.VMEM((rows, width), BF),
            pltpu.VMEM((rows, hidden), BF),
            pltpu.VMEM((width, hidden), BF),
            pltpu.VMEM((hidden, width), BF),
            pltpu.SemaphoreType.DMA((2,)),
        ],
        name="mlp",
        cost=pl.CostEstimate(
            flops=2 * rows * (width * width + 2 * width * hidden),
            transcendentals=rows * hidden,
            bytes_accessed=10**7,
        ),
    )


def fold_stage(keep, own, arrived):
    half, width = keep.shape
    quarter = half // 2
    piece = half // SPLIT

    def kernel(keep_ref, own_ref, *refs):
        blk = refs[:SPLIT]
        send, mine, arrived_ref = refs[SPLIT:]
        for i in range(SPLIT):
            arrived_ref[i * piece : (i + 1) * piece] = blk[i][...]
        side = lax.axis_index("head") >> 1
        mine_at = pl.multiple_of(side * quarter, quarter)
        send_at = pl.multiple_of((1 - side) * quarter, quarter)
        both = lambda at: (
            keep_ref[pl.ds(at, quarter)].astype(F32) + arrived_ref[pl.ds(at, quarter)].astype(F32)
        )
        send[...] = both(send_at).astype(BF)
        mine[...] = own_ref[...] + both(mine_at)

    outs = [
        jax.ShapeDtypeStruct((quarter, width), BF),
        jax.ShapeDtypeStruct((quarter, width), F32),
    ]
    return call(
        kernel,
        outs,
        (keep, own, *arrived),
        scratch=[pltpu.VMEM((half, width), BF)],
        name="fold",
        room=8,
    )


def norm_stage(mine, arrived, gain):
    quarter, width = mine.shape
    groups = quarter // 4

    def kernel(mine_ref, arrived_ref, gain_ref, out, unit):
        total = mine_ref[...] + arrived_ref[...].astype(F32)
        normed = center_scale(total) * gain_ref[...].astype(F32)
        for c in range(width // 128):
            unit[c] = normed[:, c * 128 : (c + 1) * 128]
        for u in range(4):
            for c in range(width // 128):
                out[u * groups : (u + 1) * groups, c * 128 : (c + 1) * 128] = unit[
                    c, pl.ds(u, groups, stride=4)
                ].astype(BF)

    return call(
        kernel,
        [jax.ShapeDtypeStruct((quarter, width), BF)],
        (mine, arrived, gain),
        scratch=[pltpu.VMEM((width // 128, quarter, 128), F32)],
        name="norm",
        room=8,
    )[0]


def project(blk, weight, rows):
    quarter, width = blk[0].shape
    part = quarter // 4
    head_at = lax.axis_index("head")
    own = (head_at & 1) * 2 + (head_at >> 1)
    for e, piece in enumerate(blk):
        at = pl.multiple_of((own ^ ((e & 1) * 2 + (e >> 1))) * part, part)
        for u in range(4):
            rows[u, pl.ds(at, part)] = piece[u * part : (u + 1) * part]
    total = jnp.zeros((rows.shape[1], weight.shape[0]), F32)
    for u in range(4):
        total += lax.dot_general(
            rows[u],
            weight[:, u * width : (u + 1) * width],
            (((1,), (1,)), ((), ())),
            preferred_element_type=F32,
        )
    return total.astype(BF)


def merge_stage(pieces, w_merge):
    quarter, width = pieces[0].shape
    count = len(pieces)
    groups = count * quarter // 4

    def kernel(*refs):
        weight, out, rows = refs[count:]
        out[...] = project(refs[:count], weight, rows)

    return call(
        kernel,
        [jax.ShapeDtypeStruct((groups, w_merge.shape[0]), BF)],
        (*pieces, w_merge),
        scratch=[pltpu.VMEM((4, groups, width), BF)],
        name="merge",
        room=12,
    )[0]


def deliver_stage(earlier, pieces, w_merge, owners, owner_total, capacity):
    quarter, width = pieces[0].shape
    count = len(pieces)
    ahead = len(earlier)
    groups = count * quarter // 4
    everyone = owners.shape[1]
    local = w_merge.shape[0]
    slots = owner_total * capacity

    def kernel(*refs):
        done = refs[:ahead]
        weight, owner_ref, out, rows = refs[ahead + count :]
        owner = owner_ref[...]
        picks = owner == lax.broadcasted_iota(jnp.int32, (128, everyone), 0)
        above = lax.broadcasted_iota(jnp.int32, (everyone, everyone), 0) < lax.broadcasted_iota(
            jnp.int32, (everyone, everyone), 1
        )
        before = jnp.dot(picks.astype(BF), above.astype(BF), preferred_element_type=F32)
        rank = jnp.sum(jnp.where(picks, before, 0.0), axis=0, keepdims=True)
        slot = owner * capacity + rank.astype(jnp.int32)
        dispatch = (slot == lax.broadcasted_iota(jnp.int32, (slots, everyone), 0)).astype(BF)
        last = project(refs[ahead : ahead + count], weight, rows)
        whole = jnp.concatenate([d[...] for d in done] + [last], axis=0)
        out[...] = jnp.dot(dispatch, whole, preferred_element_type=F32).astype(BF)

    return call(
        kernel,
        [jax.ShapeDtypeStruct((slots, local), BF)],
        (*earlier, *pieces, w_merge, owners),
        scratch=[pltpu.VMEM((4, groups, width), BF)],
        name="deliver",
        room=12,
    )[0]


def per_device(
    tokens,
    segment_ids,
    valid,
    owners,
    ln1_gain,
    w_qkv,
    w_out,
    ln2_gain,
    w_up,
    w_down,
    ln3_gain,
    w_merge,
):
    rows, width = tokens.shape
    heads = w_qkv.shape[2] // HEAD_DIM
    tok_total = lax.axis_size("tok")
    head_total = lax.axis_size("head")
    over_tok = lambda value, mask: lax.ppermute(value, "tok", swap_pairs(tok_total, mask))
    over_head = lambda value, mask: lax.ppermute(value, "head", swap_pairs(head_total, mask))
    teams = [list(range(g, g + heads)) for g in range(0, tok_total, heads)]
    in_team = lambda value: lax.all_to_all(
        value, "tok", 0, 0, tiled=True, axis_index_groups=teams
    )

    def all_heads(value):
        side = over_head(value, 2)
        return [value, over_head(value, 1), side, over_head(side, 1)]

    w_outs = all_heads(w_out)
    near, far = qkv_stage(
        tokens,
        ln1_gain.reshape(1, width),
        jnp.swapaxes(w_qkv, 1, 2),
        segment_ids.reshape(1, -1),
        valid.reshape(1, -1),
        heads,
    )
    far_in = []
    for k in range(heads, tok_total):
        leaving = far[k & (heads - 1)]
        if len(far_in) >= FLYING:
            leaving, far_in[-FLYING] = lax.optimization_barrier((leaving, far_in[-FLYING]))
        far_in.append(over_tok(leaving, k))
    queries, tops, sums, low_high = near_stage(in_team(near), tok_total)
    mixed = far_stage(far_in, queries, tops, sums, low_high, tok_total)
    att = in_team(mixed).reshape(heads * HEAD_DIM, rows)

    chunk = rows // CHUNKS
    gain2, gain3 = ln2_gain.reshape(1, width), ln3_gain.reshape(1, width)
    weights = (w_outs, gain2, w_up, w_down)
    first, later = att[:, :chunk], att[:, chunk:]
    attended = all_heads(first)
    side = over_head(later, 2)
    keep, own, *sends = mlp_stage(0, tokens, attended, *weights)
    send, mine0 = fold_stage(keep, own, [over_head(p, 1) for p in sends])
    later, send = lax.optimization_barrier((later, send))
    attended = [later, over_head(later, 1), side, over_head(side, 1)]
    arrived0 = over_head(send, 2)
    keep, own, *sends = mlp_stage(chunk, tokens, attended, *weights)
    keep, arrived0 = lax.optimization_barrier((keep, arrived0))
    send, mine1 = fold_stage(keep, own, [over_head(p, 1) for p in sends])
    arrived1 = over_head(send, 2)
    merged = [
        all_heads(norm_stage(mine0, arrived0, gain3)),
        all_heads(norm_stage(mine1, arrived1, gain3)),
    ]

    groups = rows // 4
    capacity = max(2, 2 * groups // tok_total)
    turned = w_merge.T
    earlier = [merge_stage(m, turned) for m in merged[:-1]]
    outgoing = deliver_stage(
        earlier, merged[-1], turned, owners.reshape(1, -1), tok_total, capacity
    )
    outgoing = outgoing.reshape(tok_total, capacity, outgoing.shape[1])
    received = lax.all_to_all(outgoing, "tok", split_axis=0, concat_axis=0, tiled=True)
    return received.reshape(tok_total * capacity, outgoing.shape[2])


def solution(mesh):
    in_specs = (
        P("tok", None),
        P("tok"),
        P("tok"),
        P("tok", None),
        P(),
        P(None, None, "head"),
        P("head", None),
        P(),
        P(None, "head"),
        P("head", None),
        P(),
        P(None, "head"),
    )
    out_specs = P("tok", "head")
    return jax.shard_map(
        per_device, mesh=mesh, in_specs=in_specs, out_specs=out_specs, check_vma=False
    )
```

```python
import math

import jax
import jax.numpy as jnp
from jax import lax
from jax.experimental import pallas as pl
from jax.experimental.pallas import tpu as pltpu
from jax.sharding import PartitionSpec as P

HEAD_DIM = 88
EXT = 128
VEXT = 96
GONE = 64.0
FAR = -1e30
BF = jnp.bfloat16
F32 = jnp.float32
CHUNKS = 2
FLYING = 4
SPLIT = 2


def swap_pairs(size, mask):
    return [(i, i ^ mask) for i in range(size)]


def center_scale(values):
    center = values - jnp.mean(values, axis=-1, keepdims=True)
    spread = jnp.mean(center * center, axis=-1, keepdims=True)
    return center * lax.rsqrt(spread + 1e-06)


SMEM = pl.BlockSpec(memory_space=pltpu.SMEM)
VM = pl.BlockSpec(memory_space=pltpu.VMEM)
HBM = pl.BlockSpec(memory_space=pltpu.HBM)


def wide(gain_ref):
    return gain_ref[...].astype(F32).reshape(1, gain_ref.shape[0])


def call(kernel, outs, args, specs=None, out_specs=None, scratch=(), name=None, room=24, cost=None):
    specs = specs if specs is not None else [VM] * len(args)
    out_specs = out_specs if out_specs is not None else [VM] * len(outs)
    spaces = {id(VM): pltpu.VMEM, id(HBM): pltpu.HBM}
    args = [
        pltpu.with_memory_space_constraint(a, spaces[id(s)]) if id(s) in spaces else a
        for a, s in zip(args, specs)
    ]
    outs = [
        spaces[id(s)](o.shape, o.dtype) if id(s) in spaces else o for o, s in zip(outs, out_specs)
    ]
    return pl.pallas_call(
        kernel,
        out_shape=outs,
        in_specs=specs,
        out_specs=out_specs,
        scratch_shapes=scratch,
        compiler_params=pltpu.CompilerParams(vmem_limit_bytes=room * 1024 * 1024),
        cost_estimate=cost,
        name=name,
    )(*args)


def qkv_stage(tokens, gain, w_qkv, seg, valid, heads):
    rows, width = tokens.shape
    local = w_qkv.shape[1]
    scale = math.log2(math.e) / math.sqrt(HEAD_DIM)
    far_rows = VEXT + HEAD_DIM
    near_rows = far_rows + HEAD_DIM
    strip = math.gcd(rows, 128)

    def kernel(tok_hbm, gain_ref, w_hbm, seg_hbm, valid_hbm, *rest):
        near_hbm = rest[0]
        far_hbm = rest[1 : 1 + heads]
        near, tok, weight, normed, seg_ref, valid_ref, sem, leave = rest[1 + heads :]
        turn = lax.axis_index("tok") & (heads - 1)
        sends = [
            pltpu.make_async_copy(near.at[turn ^ j, pl.ds(0, far_rows)], far_hbm[j], leave.at[j])
            for j in range(heads)
        ]
        sends += [
            pltpu.make_async_copy(near.at[h], near_hbm.at[h], leave.at[heads + h])
            for h in range(heads)
        ]
        tok_copy = pltpu.make_async_copy(tok_hbm, tok, sem.at[3])
        tok_copy.start()
        seg_copy = pltpu.make_async_copy(seg_hbm, seg_ref, sem.at[4])
        seg_copy.start()
        valid_copy = pltpu.make_async_copy(valid_hbm, valid_ref, sem.at[5])
        valid_copy.start()
        copies = [pltpu.make_async_copy(w_hbm.at[i], weight.at[i], sem.at[i]) for i in range(3)]
        for i in (1, 2, 0):
            copies[i].start()
        spread_to = lax.broadcasted_iota(jnp.int32, (rows // 4, rows), 1) // 4
        spread_from = lax.broadcasted_iota(jnp.int32, (rows // 4, rows), 0)
        spread = (spread_to == spread_from).astype(BF)
        seg_copy.wait()
        valid_copy.wait()
        seg8 = jnp.broadcast_to(seg_ref[...].astype(F32), (8, rows // 4)).astype(BF)
        tags = jnp.dot(seg8, spread, preferred_element_type=F32)
        gone = jnp.where(valid_ref[...] == 1, 0.0, GONE)
        tags = (tags + jnp.broadcast_to(gone, (8, rows))).astype(BF)
        for h in range(heads):
            near[h, HEAD_DIM:VEXT] = tags
        gains = wide(gain_ref)
        tok_copy.wait()
        for i in range(rows // strip):
            at = slice(i * strip, (i + 1) * strip)
            normed[at] = (center_scale(tok[at].astype(F32)) * gains).astype(BF)

        for i, place in ((1, 0), (2, VEXT), (0, far_rows)):
            copies[i].wait()
            turned = lax.dot_general(
                weight[i], normed[...], (((1,), (1,)), ((), ())), preferred_element_type=F32
            )
            if i == 0:
                turned = turned * scale
            for h in range(heads):
                near[h, place : place + HEAD_DIM] = turned[
                    h * HEAD_DIM : (h + 1) * HEAD_DIM
                ].astype(BF)
            if i == 2:
                for j in range(heads):
                    sends[j].start()
            if i == 0:
                for h in range(heads):
                    sends[heads + h].start()
        for c in sends:
            c.wait()

    outs = [jax.ShapeDtypeStruct((heads, near_rows, rows), BF)]
    outs += [jax.ShapeDtypeStruct((far_rows, rows), BF)] * heads
    result = call(
        kernel,
        outs,
        (tokens, gain, w_qkv, seg, valid),
        specs=[HBM, VM, HBM, HBM, HBM],
        out_specs=[HBM] * (1 + heads),
        scratch=[
            pltpu.VMEM((heads, near_rows, rows), BF),
            pltpu.VMEM((rows, width), BF),
            pltpu.VMEM((3, local, width), BF),
            pltpu.VMEM((rows, width), BF),
            pltpu.VMEM((1, rows // 4), jnp.int32),
            pltpu.VMEM((1, rows), jnp.int32),
            pltpu.SemaphoreType.DMA((6,)),
            pltpu.SemaphoreType.DMA((2 * heads,)),
        ],
        name="qkv",
        room=16,
        cost=pl.CostEstimate(flops=4 * 10**9, transcendentals=0, bytes_accessed=10**7),
    )
    return result[0], result[1:]


def load_keys(block_ref, keys, values, segments):
    rows = block_ref.shape[1]
    top = block_ref[0:VEXT].astype(F32)
    tags = top[HEAD_DIM : HEAD_DIM + 1]
    gone = tags >= GONE
    seg = jnp.where(gone, tags - GONE, tags)
    mark = jnp.where(gone, float(segments), tags)
    line = lax.broadcasted_iota(jnp.int32, (EXT, rows), 0) - HEAD_DIM
    hot = (line.astype(F32) == mark).astype(F32)
    head_part = jnp.where(line[0:VEXT] >= 0, hot[0:VEXT], top)
    keys[:, 0:VEXT] = head_part.T.astype(BF)
    keys[:, VEXT:EXT] = hot[VEXT:EXT].T.astype(BF)
    vals = block_ref[VEXT : VEXT + HEAD_DIM].astype(F32)
    ones = jnp.ones((VEXT - HEAD_DIM, rows), F32)
    values[...] = jnp.concatenate([vals, ones], axis=0).astype(BF)
    return jnp.min(seg), jnp.max(seg)


def absorb(keys, values, query, top, sums):
    scores = jnp.dot(keys[...], query[...], preferred_element_type=F32)
    newest = jnp.maximum(top[...], jnp.max(scores, axis=0, keepdims=True))
    weights = jnp.exp2(scores - newest).astype(BF)
    factor = jnp.exp2(top[...] - newest)
    sums[...] = sums[...] * factor + jnp.dot(values[...], weights, preferred_element_type=F32)
    top[...] = newest


def near_stage(blocks, segments, w_up, w_down):
    count, _, rows = blocks.shape
    query_at = VEXT + HEAD_DIM

    def kernel(
        blk, up_hbm, down_hbm, queries, tops, sums, low_high, up, down, keys, values, sem
    ):
        up_copy = pltpu.make_async_copy(up_hbm, up, sem.at[0])
        down_copy = pltpu.make_async_copy(down_hbm, down, sem.at[1])
        up_copy.start()
        down_copy.start()
        bounds = []
        for b in range(count):
            bounds.append(load_keys(blk.at[b], keys.at[b], values.at[b], segments))
            low_high[2 * b] = bounds[b][0]
            low_high[2 * b + 1] = bounds[b][1]
        for j in range(count):
            query = blk[j, query_at : query_at + HEAD_DIM].astype(F32)
            top = blk[j, 0:VEXT].astype(F32)
            tags = top[HEAD_DIM : HEAD_DIM + 1]
            gone = tags >= GONE
            seg = jnp.where(gone, tags - GONE, tags)
            line = lax.broadcasted_iota(jnp.int32, (EXT - HEAD_DIM, rows), 0).astype(F32)
            wall = jnp.where(line == seg, 0.0, FAR)
            queries[j] = jnp.concatenate([query, wall], axis=0).astype(BF)
            own = jnp.sum(query * top[0:HEAD_DIM], axis=0, keepdims=True)
            tops[j] = jnp.where(gone, own, FAR)
            sums[j] = jnp.where(gone, values[j].astype(F32), 0.0)
        for j in range(count):
            for b in range(count):

                @pl.when((bounds[b][0] <= bounds[j][1]) & (bounds[b][1] >= bounds[j][0]))
                def _():
                    absorb(keys.at[b], values.at[b], queries.at[j], tops.at[j], sums.at[j])

        up_copy.wait()
        down_copy.wait()

    outs = [
        jax.ShapeDtypeStruct((count, EXT, rows), BF),
        jax.ShapeDtypeStruct((count, 1, rows), F32),
        jax.ShapeDtypeStruct((count, VEXT, rows), F32),
        jax.ShapeDtypeStruct((2 * count,), F32),
        jax.ShapeDtypeStruct(w_up.shape, BF),
        jax.ShapeDtypeStruct(w_down.shape, BF),
    ]
    return call(
        kernel,
        outs,
        (blocks, w_up, w_down),
        specs=[VM, HBM, HBM],
        out_specs=[VM, VM, VM, SMEM, VM, VM],
        scratch=[
            pltpu.VMEM((count, rows, EXT), BF),
            pltpu.VMEM((count, VEXT, rows), BF),
            pltpu.SemaphoreType.DMA((2,)),
        ],
        name="near",
        room=8,
        cost=pl.CostEstimate(flops=8 * 10**9, transcendentals=4 * 10**6, bytes_accessed=10**7),
    )


def far_stage(blocks, queries, tops, sums, low_high, segments):
    count = len(blocks)
    heads, _, rows = queries.shape

    def kernel(*refs):
        blk = refs[:count]
        query_ref, top_ref, sum_ref, bound_ref = refs[count : count + 4]
        out, keys, values, top, total, ready, sem = refs[count + 4 :]
        leave = [pltpu.make_async_copy(ready.at[j], out.at[j], sem.at[j]) for j in range(heads)]
        bounds = [load_keys(blk[b], keys.at[b], values.at[b], segments) for b in range(count)]
        for j in range(heads):
            top[...] = top_ref[j]
            total[...] = sum_ref[j]
            for b in range(count):

                @pl.when((bounds[b][0] <= bound_ref[2 * j + 1]) & (bounds[b][1] >= bound_ref[2 * j]))
                def _():
                    absorb(keys.at[b], values.at[b], query_ref.at[j], top, total)

            whole = total[...]
            ready[j] = (whole[0:HEAD_DIM] / whole[HEAD_DIM : HEAD_DIM + 1]).astype(BF)
            leave[j].start()
        for j in range(heads):
            leave[j].wait()

    return call(
        kernel,
        [jax.ShapeDtypeStruct((heads, HEAD_DIM, rows), BF)],
        (*blocks, queries, tops, sums, low_high),
        specs=[VM] * (count + 3) + [SMEM],
        out_specs=[HBM],
        scratch=[
            pltpu.VMEM((count, rows, EXT), BF),
            pltpu.VMEM((count, VEXT, rows), BF),
            pltpu.VMEM((1, rows), F32),
            pltpu.VMEM((VEXT, rows), F32),
            pltpu.VMEM((heads, HEAD_DIM, rows), BF),
            pltpu.SemaphoreType.DMA((heads,)),
        ],
        name="far",
        room=6 + count // 2 + count // 4,
        cost=pl.CostEstimate(flops=6 * 10**9, transcendentals=4 * 10**6, bytes_accessed=10**7),
    )[0]


def cut_stage(whole, pieces):
    rows, width = whole.shape
    part = width // pieces

    def kernel(whole_ref, *out):
        for i in range(pieces):
            out[i][...] = whole_ref[:, i * part : (i + 1) * part]

    outs = [jax.ShapeDtypeStruct((rows, part), BF)] * pieces
    return call(kernel, outs, (whole,), name="cut", room=4)


def mlp_stage(first, tokens, attended, w_outs, gain, w_up, w_down):
    width = tokens.shape[1]
    part, rows = attended[0].shape
    pieces = len(attended)
    hidden = w_up.shape[1]
    half = rows // 2

    def kernel(tok_ref, *refs):
        att = refs[:pieces]
        wout = refs[pieces : 2 * pieces]
        gain_ref, up, down, keep, own = refs[2 * pieces : 2 * pieces + 5]
        sends = refs[2 * pieces + 5 : 2 * pieces + 5 + SPLIT]
        stream, second, act = refs[2 * pieces + 5 + SPLIT :]
        core = lax.axis_index("head") & 1
        keep_at = pl.multiple_of(core * half, half)
        total = tok_ref[first : first + rows].astype(F32)
        for e in range(pieces):
            total += jnp.dot(
                att[e][...].astype(F32).T.astype(BF), wout[e][...], preferred_element_type=F32
            )
        stream[...] = total
        own[...] = stream[pl.ds(keep_at, half)]
        second[...] = (center_scale(stream[...]) * wide(gain_ref)).astype(BF)
        pre = jnp.dot(second[...], up[...], preferred_element_type=F32)
        act[...] = (0.5 * pre * (1.0 + lax.erf(pre * math.sqrt(0.5)))).astype(BF)
        stream[...] = jnp.dot(act[...], down[...], preferred_element_type=F32)
        keep[...] = stream[pl.ds(keep_at, half)].astype(BF)
        for i in range(SPLIT):
            at = pl.multiple_of((1 - core) * half + i * (half // SPLIT), half // SPLIT)
            sends[i][...] = stream[pl.ds(at, half // SPLIT)].astype(BF)

    outs = [
        jax.ShapeDtypeStruct((half, width), BF),
        jax.ShapeDtypeStruct((half, width), F32),
    ]
    outs += [jax.ShapeDtypeStruct((half // SPLIT, width), BF)] * SPLIT
    return call(
        kernel,
        outs,
        (tokens, *attended, *w_outs, gain, w_up, w_down),
        scratch=[
            pltpu.VMEM((rows, width), F32),
            pltpu.VMEM((rows, width), BF),
            pltpu.VMEM((rows, hidden), BF),
        ],
        name="mlp",
        room=14,
        cost=pl.CostEstimate(
            flops=2 * rows * (width * width + 2 * width * hidden),
            transcendentals=rows * hidden,
            bytes_accessed=10**7,
        ),
    )


def fold_stage(keep, own, arrived):
    half, width = keep.shape
    piece = half // SPLIT

    def kernel(keep_ref, own_ref, *refs):
        send, mine = refs[SPLIT:]
        for i in range(SPLIT):
            at = slice(i * piece, (i + 1) * piece)
            both = keep_ref[at].astype(F32) + refs[i][...].astype(F32)
            send[at] = both.astype(BF)
            mine[at] = own_ref[at] + both

    outs = [
        jax.ShapeDtypeStruct((half, width), BF),
        jax.ShapeDtypeStruct((half, width), F32),
    ]
    return call(kernel, outs, (keep, own, *arrived), name="fold", room=8)


def norm_stage(mine, arrived, gain):
    half, width = mine.shape
    groups = half // 4

    def kernel(mine_ref, arrived_ref, gain_ref, out, unit):
        total = mine_ref[...] + arrived_ref[...].astype(F32)
        normed = center_scale(total) * wide(gain_ref)
        for c in range(width // 128):
            unit[c] = normed[:, c * 128 : (c + 1) * 128]
        for u in range(4):
            for c in range(width // 128):
                out[u * groups : (u + 1) * groups, c * 128 : (c + 1) * 128] = unit[
                    c, pl.ds(u, groups, stride=4)
                ].astype(BF)

    return call(
        kernel,
        [jax.ShapeDtypeStruct((half, width), BF)],
        (mine, arrived, gain),
        scratch=[pltpu.VMEM((width // 128, half, 128), F32)],
        name="norm",
        room=8,
    )[0]


def project(blk, weight, rows):
    half, width = blk[0].shape
    part = half // 4
    core = lax.axis_index("head") & 1
    for e, piece in enumerate(blk):
        at = pl.multiple_of((core ^ e) * part, part)
        for u in range(4):
            rows[u, pl.ds(at, part)] = piece[u * part : (u + 1) * part]
    total = jnp.zeros((rows.shape[1], weight.shape[0]), F32)
    for u in range(4):
        total += lax.dot_general(
            rows[u],
            weight[:, u * width : (u + 1) * width],
            (((1,), (1,)), ((), ())),
            preferred_element_type=F32,
        )
    return total.astype(BF)


def merge_stage(pieces, w_merge):
    quarter, width = pieces[0].shape
    count = len(pieces)
    groups = count * quarter // 4

    def kernel(*refs):
        weight, out, rows = refs[count:]
        out[...] = project(refs[:count], weight, rows)

    return call(
        kernel,
        [jax.ShapeDtypeStruct((groups, w_merge.shape[0]), BF)],
        (*pieces, w_merge),
        scratch=[pltpu.VMEM((4, groups, width), BF)],
        name="merge",
        room=6,
    )[0]


def deliver_stage(earlier, pieces, w_merge, owners, owner_total, capacity):
    quarter, width = pieces[0].shape
    count = len(pieces)
    ahead = len(earlier)
    groups = count * quarter // 4
    everyone = owners.shape[1]
    local = w_merge.shape[0]
    slots = owner_total * capacity

    def kernel(*refs):
        done = refs[:ahead]
        weight, owner_ref, out, rows = refs[ahead + count :]
        owner = owner_ref[...]
        picks = owner == lax.broadcasted_iota(jnp.int32, (128, everyone), 0)
        above = lax.broadcasted_iota(jnp.int32, (everyone, everyone), 0) < lax.broadcasted_iota(
            jnp.int32, (everyone, everyone), 1
        )
        before = jnp.dot(picks.astype(BF), above.astype(BF), preferred_element_type=F32)
        rank = jnp.sum(jnp.where(picks, before, 0.0), axis=0, keepdims=True)
        slot = owner * capacity + rank.astype(jnp.int32)
        dispatch = (slot == lax.broadcasted_iota(jnp.int32, (slots, everyone), 0)).astype(BF)
        last = project(refs[ahead : ahead + count], weight, rows)
        whole = jnp.concatenate([d[...] for d in done] + [last], axis=0)
        out[...] = jnp.dot(dispatch, whole, preferred_element_type=F32).astype(BF)

    return call(
        kernel,
        [jax.ShapeDtypeStruct((slots, local), BF)],
        (*earlier, *pieces, w_merge, owners),
        scratch=[pltpu.VMEM((4, groups, width), BF)],
        name="deliver",
        room=6,
    )[0]


def per_device(
    tokens,
    segment_ids,
    valid,
    owners,
    ln1_gain,
    w_qkv,
    w_out,
    ln2_gain,
    w_up,
    w_down,
    ln3_gain,
    w_merge,
):
    rows, width = tokens.shape
    heads = w_qkv.shape[2] // HEAD_DIM
    tok_total = lax.axis_size("tok")
    head_total = lax.axis_size("head")
    over_tok = lambda value, mask: lax.ppermute(value, "tok", swap_pairs(tok_total, mask))
    over_head = lambda value, mask: lax.ppermute(value, "head", swap_pairs(head_total, mask))
    teams = [list(range(g, g + heads)) for g in range(0, tok_total, heads)]
    in_team = lambda value: lax.all_to_all(
        value, "tok", 0, 0, tiled=True, axis_index_groups=teams
    )

    def all_heads(value):
        side = over_head(value, 2)
        return [value, over_head(value, 1), side, over_head(side, 1)]

    w_outs = all_heads(w_out)
    near, far = qkv_stage(
        tokens,
        ln1_gain,
        jnp.swapaxes(w_qkv, 1, 2),
        segment_ids.reshape(1, -1),
        valid.reshape(1, -1),
        heads,
    )
    far_in = []
    for k in range(heads, tok_total):
        leaving = far[k & (heads - 1)]
        if len(far_in) >= FLYING:
            leaving, far_in[-FLYING] = lax.optimization_barrier((leaving, far_in[-FLYING]))
        far_in.append(over_tok(leaving, k))
    queries, tops, sums, low_high, up, down = near_stage(
        in_team(near), tok_total, w_up, w_down
    )
    mixed = far_stage(far_in, queries, tops, sums, low_high, tok_total)
    att = in_team(mixed).reshape(heads * HEAD_DIM, rows)

    chunk = rows // CHUNKS
    gain2, gain3 = ln2_gain, ln3_gain
    weights = (w_outs, gain2, up, down)
    first, later = cut_stage(att, CHUNKS)
    attended = all_heads(first)
    side = over_head(later, 2)
    keep, own, *sends = mlp_stage(0, tokens, attended, *weights)
    send, mine0 = fold_stage(keep, own, [over_head(p, 1) for p in sends])
    later, send = lax.optimization_barrier((later, send))
    attended = [later, over_head(later, 1), side, over_head(side, 1)]
    arrived0 = over_head(send, 2)
    keep, own, *sends = mlp_stage(chunk, tokens, attended, *weights)
    keep, arrived0 = lax.optimization_barrier((keep, arrived0))
    send, mine1 = fold_stage(keep, own, [over_head(p, 1) for p in sends])
    arrived1 = over_head(send, 2)
    merged = [norm_stage(mine0, arrived0, gain3), norm_stage(mine1, arrived1, gain3)]
    merged = [[m, over_head(m, 1)] for m in merged]

    groups = rows // 4
    capacity = max(2, 2 * groups // tok_total)
    turned = w_merge.T
    earlier = [merge_stage(m, turned) for m in merged[:-1]]
    outgoing = deliver_stage(
        earlier, merged[-1], turned, owners.reshape(1, -1), tok_total, capacity
    )
    outgoing = outgoing.reshape(tok_total, capacity, outgoing.shape[1])
    received = lax.all_to_all(outgoing, "tok", split_axis=0, concat_axis=0, tiled=True)
    return received.reshape(tok_total * capacity, outgoing.shape[2])


def solution(mesh):
    in_specs = (
        P("tok", None),
        P("tok"),
        P("tok"),
        P("tok", None),
        P(),
        P(None, None, "head"),
        P("head", None),
        P(),
        P(None, "head"),
        P("head", None),
        P(),
        P(None, "head"),
    )
    out_specs = P("tok", "head")
    return jax.shard_map(
        per_device, mesh=mesh, in_specs=in_specs, out_specs=out_specs, check_vma=False
    )
```

```python
import math

import jax
import jax.numpy as jnp
from jax import lax
from jax.experimental import pallas as pl
from jax.experimental.pallas import tpu as pltpu
from jax.sharding import PartitionSpec as P

HEAD_DIM = 88
EXT = 128
VEXT = 96
GONE = 64.0
FAR = -1e30
BF = jnp.bfloat16
F32 = jnp.float32
CHUNKS = 2
FLYING = 4
SPLIT = 2


def swap_pairs(size, mask):
    return [(i, i ^ mask) for i in range(size)]


def center_scale(values):
    center = values - jnp.mean(values, axis=-1, keepdims=True)
    spread = jnp.mean(center * center, axis=-1, keepdims=True)
    return center * lax.rsqrt(spread + 1e-06)


SMEM = pl.BlockSpec(memory_space=pltpu.SMEM)
VM = pl.BlockSpec(memory_space=pltpu.VMEM)
HBM = pl.BlockSpec(memory_space=pltpu.HBM)


def wide(gain_ref):
    return gain_ref[...].astype(F32).reshape(1, gain_ref.shape[0])


def call(kernel, outs, args, specs=None, out_specs=None, scratch=(), name=None, room=24, cost=None):
    specs = specs if specs is not None else [VM] * len(args)
    out_specs = out_specs if out_specs is not None else [VM] * len(outs)
    spaces = {id(VM): pltpu.VMEM, id(HBM): pltpu.HBM}
    args = [
        pltpu.with_memory_space_constraint(a, spaces[id(s)]) if id(s) in spaces else a
        for a, s in zip(args, specs)
    ]
    outs = [
        spaces[id(s)](o.shape, o.dtype) if id(s) in spaces else o for o, s in zip(outs, out_specs)
    ]
    return pl.pallas_call(
        kernel,
        out_shape=outs,
        in_specs=specs,
        out_specs=out_specs,
        scratch_shapes=scratch,
        compiler_params=pltpu.CompilerParams(vmem_limit_bytes=room * 1024 * 1024),
        cost_estimate=cost,
        name=name,
    )(*args)


def qkv_stage(tokens, gain, w_qkv, seg, valid, heads):
    rows, width = tokens.shape
    local = w_qkv.shape[1]
    scale = math.log2(math.e) / math.sqrt(HEAD_DIM)
    far_rows = VEXT + HEAD_DIM
    near_rows = far_rows + HEAD_DIM
    strip = math.gcd(rows, 128)

    def kernel(tok_hbm, gain_hbm, w_hbm, seg_hbm, valid_hbm, *rest):
        near_hbm = rest[0]
        far_hbm = rest[1 : 1 + heads]
        near, tok, weight, normed, seg_ref, valid_ref, gain_ref, sem, leave = rest[1 + heads :]
        turn = lax.axis_index("tok") & (heads - 1)
        sends = [
            pltpu.make_async_copy(near.at[turn ^ j, pl.ds(0, far_rows)], far_hbm[j], leave.at[j])
            for j in range(heads)
        ]
        sends += [
            pltpu.make_async_copy(near.at[h], near_hbm.at[h], leave.at[heads + h])
            for h in range(heads)
        ]
        strips = [slice(i * strip, (i + 1) * strip) for i in range(rows // strip)]
        tok_copies = [
            pltpu.make_async_copy(tok_hbm.at[at], tok.at[at], sem.at[7 + i])
            for i, at in enumerate(strips)
        ]
        for c in tok_copies:
            c.start()
        seg_copy = pltpu.make_async_copy(seg_hbm, seg_ref, sem.at[4])
        seg_copy.start()
        valid_copy = pltpu.make_async_copy(valid_hbm, valid_ref, sem.at[5])
        valid_copy.start()
        gain_copy = pltpu.make_async_copy(gain_hbm, gain_ref, sem.at[6])
        gain_copy.start()
        copies = [pltpu.make_async_copy(w_hbm.at[i], weight.at[i], sem.at[i]) for i in range(3)]
        for i in (1, 2, 0):
            copies[i].start()
        spread_to = lax.broadcasted_iota(jnp.int32, (rows // 4, rows), 1) // 4
        spread_from = lax.broadcasted_iota(jnp.int32, (rows // 4, rows), 0)
        spread = (spread_to == spread_from).astype(BF)
        seg_copy.wait()
        valid_copy.wait()
        seg8 = jnp.broadcast_to(seg_ref[...].astype(F32), (8, rows // 4)).astype(BF)
        tags = jnp.dot(seg8, spread, preferred_element_type=F32)
        gone = jnp.where(valid_ref[...] == 1, 0.0, GONE)
        tags = (tags + jnp.broadcast_to(gone, (8, rows))).astype(BF)
        for h in range(heads):
            near[h, HEAD_DIM:VEXT] = tags
        gain_copy.wait()
        gains = wide(gain_ref)
        for c, at in zip(tok_copies, strips):
            c.wait()
            normed[at] = (center_scale(tok[at].astype(F32)) * gains).astype(BF)

        for i, place in ((1, 0), (2, VEXT), (0, far_rows)):
            copies[i].wait()
            turned = lax.dot_general(
                weight[i], normed[...], (((1,), (1,)), ((), ())), preferred_element_type=F32
            )
            if i == 0:
                turned = turned * scale
            for h in range(heads):
                near[h, place : place + HEAD_DIM] = turned[
                    h * HEAD_DIM : (h + 1) * HEAD_DIM
                ].astype(BF)
            if i == 2:
                for j in range(heads):
                    sends[j].start()
            if i == 0:
                for h in range(heads):
                    sends[heads + h].start()
        for c in sends:
            c.wait()

    outs = [jax.ShapeDtypeStruct((heads, near_rows, rows), BF)]
    outs += [jax.ShapeDtypeStruct((far_rows, rows), BF)] * heads
    result = call(
        kernel,
        outs,
        (tokens, gain, w_qkv, seg, valid),
        specs=[HBM] * 5,
        out_specs=[HBM] * (1 + heads),
        scratch=[
            pltpu.VMEM((heads, near_rows, rows), BF),
            pltpu.VMEM((rows, width), BF),
            pltpu.VMEM((3, local, width), BF),
            pltpu.VMEM((rows, width), BF),
            pltpu.VMEM((1, rows // 4), jnp.int32),
            pltpu.VMEM((1, rows), jnp.int32),
            pltpu.VMEM((width,), BF),
            pltpu.SemaphoreType.DMA((7 + rows // strip,)),
            pltpu.SemaphoreType.DMA((2 * heads,)),
        ],
        name="qkv",
        room=16,
        cost=pl.CostEstimate(flops=4 * 10**9, transcendentals=0, bytes_accessed=10**7),
    )
    return result[0], result[1:]


def load_keys(block_ref, keys, values, segments):
    rows = block_ref.shape[1]
    top = block_ref[0:VEXT].astype(F32)
    tags = top[HEAD_DIM : HEAD_DIM + 1]
    gone = tags >= GONE
    seg = jnp.where(gone, tags - GONE, tags)
    mark = jnp.where(gone, float(segments), tags)
    line = lax.broadcasted_iota(jnp.int32, (EXT, rows), 0) - HEAD_DIM
    hot = (line.astype(F32) == mark).astype(F32)
    head_part = jnp.where(line[0:VEXT] >= 0, hot[0:VEXT], top)
    keys[:, 0:VEXT] = head_part.T.astype(BF)
    keys[:, VEXT:EXT] = hot[VEXT:EXT].T.astype(BF)
    vals = block_ref[VEXT : VEXT + HEAD_DIM].astype(F32)
    ones = jnp.ones((VEXT - HEAD_DIM, rows), F32)
    values[...] = jnp.concatenate([vals, ones], axis=0).astype(BF)
    return jnp.min(seg), jnp.max(seg)


def absorb(keys, values, query, top, sums):
    scores = jnp.dot(keys[...], query[...], preferred_element_type=F32)
    newest = jnp.maximum(top[...], jnp.max(scores, axis=0, keepdims=True))
    weights = jnp.exp2(scores - newest).astype(BF)
    factor = jnp.exp2(top[...] - newest)
    sums[...] = sums[...] * factor + jnp.dot(values[...], weights, preferred_element_type=F32)
    top[...] = newest


def near_stage(blocks, segments, w_up, w_down):
    count, _, rows = blocks.shape
    query_at = VEXT + HEAD_DIM

    def kernel(
        blk, up_hbm, down_hbm, queries, tops, sums, low_high, up, down, keys, values, sem
    ):
        up_copy = pltpu.make_async_copy(up_hbm, up, sem.at[0])
        down_copy = pltpu.make_async_copy(down_hbm, down, sem.at[1])
        up_copy.start()
        down_copy.start()
        bounds = []
        for b in range(count):
            bounds.append(load_keys(blk.at[b], keys.at[b], values.at[b], segments))
            low_high[2 * b] = bounds[b][0]
            low_high[2 * b + 1] = bounds[b][1]
        for j in range(count):
            query = blk[j, query_at : query_at + HEAD_DIM].astype(F32)
            top = blk[j, 0:VEXT].astype(F32)
            tags = top[HEAD_DIM : HEAD_DIM + 1]
            gone = tags >= GONE
            seg = jnp.where(gone, tags - GONE, tags)
            line = lax.broadcasted_iota(jnp.int32, (EXT - HEAD_DIM, rows), 0).astype(F32)
            wall = jnp.where(line == seg, 0.0, FAR)
            queries[j] = jnp.concatenate([query, wall], axis=0).astype(BF)
            own = jnp.sum(query * top[0:HEAD_DIM], axis=0, keepdims=True)
            tops[j] = jnp.where(gone, own, FAR)
            sums[j] = jnp.where(gone, values[j].astype(F32), 0.0)
        for j in range(count):
            for b in range(count):

                @pl.when((bounds[b][0] <= bounds[j][1]) & (bounds[b][1] >= bounds[j][0]))
                def _():
                    absorb(keys.at[b], values.at[b], queries.at[j], tops.at[j], sums.at[j])

        up_copy.wait()
        down_copy.wait()

    outs = [
        jax.ShapeDtypeStruct((count, EXT, rows), BF),
        jax.ShapeDtypeStruct((count, 1, rows), F32),
        jax.ShapeDtypeStruct((count, VEXT, rows), F32),
        jax.ShapeDtypeStruct((2 * count,), F32),
        jax.ShapeDtypeStruct(w_up.shape, BF),
        jax.ShapeDtypeStruct(w_down.shape, BF),
    ]
    return call(
        kernel,
        outs,
        (blocks, w_up, w_down),
        specs=[VM, HBM, HBM],
        out_specs=[VM, VM, VM, SMEM, VM, VM],
        scratch=[
            pltpu.VMEM((count, rows, EXT), BF),
            pltpu.VMEM((count, VEXT, rows), BF),
            pltpu.SemaphoreType.DMA((2,)),
        ],
        name="near",
        room=8,
        cost=pl.CostEstimate(flops=8 * 10**9, transcendentals=4 * 10**6, bytes_accessed=10**7),
    )


def far_stage(blocks, queries, tops, sums, low_high, segments):
    count = len(blocks)
    heads, _, rows = queries.shape

    def kernel(*refs):
        blk = refs[:count]
        query_ref, top_ref, sum_ref, bound_ref = refs[count : count + 4]
        out, keys, values, top, total, ready, sem = refs[count + 4 :]
        leave = [pltpu.make_async_copy(ready.at[j], out.at[j], sem.at[j]) for j in range(heads)]
        bounds = [load_keys(blk[b], keys.at[b], values.at[b], segments) for b in range(count)]
        for j in range(heads):
            top[...] = top_ref[j]
            total[...] = sum_ref[j]
            for b in range(count):

                @pl.when((bounds[b][0] <= bound_ref[2 * j + 1]) & (bounds[b][1] >= bound_ref[2 * j]))
                def _():
                    absorb(keys.at[b], values.at[b], query_ref.at[j], top, total)

            whole = total[...]
            ready[j] = (whole[0:HEAD_DIM] / whole[HEAD_DIM : HEAD_DIM + 1]).astype(BF)
            leave[j].start()
        for j in range(heads):
            leave[j].wait()

    return call(
        kernel,
        [jax.ShapeDtypeStruct((heads, HEAD_DIM, rows), BF)],
        (*blocks, queries, tops, sums, low_high),
        specs=[VM] * (count + 3) + [SMEM],
        out_specs=[HBM],
        scratch=[
            pltpu.VMEM((count, rows, EXT), BF),
            pltpu.VMEM((count, VEXT, rows), BF),
            pltpu.VMEM((1, rows), F32),
            pltpu.VMEM((VEXT, rows), F32),
            pltpu.VMEM((heads, HEAD_DIM, rows), BF),
            pltpu.SemaphoreType.DMA((heads,)),
        ],
        name="far",
        room=6 + count // 2 + count // 4,
        cost=pl.CostEstimate(flops=6 * 10**9, transcendentals=4 * 10**6, bytes_accessed=10**7),
    )[0]


def cut_stage(whole, pieces):
    rows, width = whole.shape
    part = width // pieces

    def kernel(whole_ref, *out):
        for i in range(pieces):
            out[i][...] = whole_ref[:, i * part : (i + 1) * part]

    outs = [jax.ShapeDtypeStruct((rows, part), BF)] * pieces
    return call(kernel, outs, (whole,), name="cut", room=4)


def mlp_stage(first, tokens, attended, w_outs, gain, w_up, w_down):
    width = tokens.shape[1]
    part, rows = attended[0].shape
    pieces = len(attended)
    hidden = w_up.shape[1]
    half = rows // 2

    def kernel(tok_ref, *refs):
        att = refs[:pieces]
        wout = refs[pieces : 2 * pieces]
        gain_ref, up, down, keep, own = refs[2 * pieces : 2 * pieces + 5]
        sends = refs[2 * pieces + 5 : 2 * pieces + 5 + SPLIT]
        stream, second, act = refs[2 * pieces + 5 + SPLIT :]
        core = lax.axis_index("head") & 1
        keep_at = pl.multiple_of(core * half, half)
        total = tok_ref[first : first + rows].astype(F32)
        for e in range(pieces):
            total += jnp.dot(
                att[e][...].astype(F32).T.astype(BF), wout[e][...], preferred_element_type=F32
            )
        stream[...] = total
        own[...] = stream[pl.ds(keep_at, half)]
        second[...] = (center_scale(stream[...]) * wide(gain_ref)).astype(BF)
        pre = jnp.dot(second[...], up[...], preferred_element_type=F32)
        act[...] = (0.5 * pre * (1.0 + lax.erf(pre * math.sqrt(0.5)))).astype(BF)
        stream[...] = jnp.dot(act[...], down[...], preferred_element_type=F32)
        keep[...] = stream[pl.ds(keep_at, half)].astype(BF)
        for i in range(SPLIT):
            at = pl.multiple_of((1 - core) * half + i * (half // SPLIT), half // SPLIT)
            sends[i][...] = stream[pl.ds(at, half // SPLIT)].astype(BF)

    outs = [
        jax.ShapeDtypeStruct((half, width), BF),
        jax.ShapeDtypeStruct((half, width), F32),
    ]
    outs += [jax.ShapeDtypeStruct((half // SPLIT, width), BF)] * SPLIT
    return call(
        kernel,
        outs,
        (tokens, *attended, *w_outs, gain, w_up, w_down),
        scratch=[
            pltpu.VMEM((rows, width), F32),
            pltpu.VMEM((rows, width), BF),
            pltpu.VMEM((rows, hidden), BF),
        ],
        name="mlp",
        room=14,
        cost=pl.CostEstimate(
            flops=2 * rows * (width * width + 2 * width * hidden),
            transcendentals=rows * hidden,
            bytes_accessed=10**7,
        ),
    )


def fold_stage(keep, own, arrived):
    half, width = keep.shape
    piece = half // SPLIT

    def kernel(keep_ref, own_ref, *refs):
        send, mine = refs[SPLIT:]
        for i in range(SPLIT):
            at = slice(i * piece, (i + 1) * piece)
            both = keep_ref[at].astype(F32) + refs[i][...].astype(F32)
            send[at] = both.astype(BF)
            mine[at] = own_ref[at] + both

    outs = [
        jax.ShapeDtypeStruct((half, width), BF),
        jax.ShapeDtypeStruct((half, width), F32),
    ]
    return call(kernel, outs, (keep, own, *arrived), name="fold", room=8)


def norm_stage(mine, arrived, gain, parts):
    half, width = mine.shape
    groups = half // 4
    each = 4 // parts

    def kernel(mine_ref, arrived_ref, gain_ref, *refs):
        out, unit = refs[:parts], refs[parts]
        total = mine_ref[...] + arrived_ref[...].astype(F32)
        normed = center_scale(total) * wide(gain_ref)
        for c in range(width // 128):
            unit[c] = normed[:, c * 128 : (c + 1) * 128]
        for u in range(4):
            for c in range(width // 128):
                at = u % each * groups
                out[u // each][at : at + groups, c * 128 : (c + 1) * 128] = unit[
                    c, pl.ds(u, groups, stride=4)
                ].astype(BF)

    return call(
        kernel,
        [jax.ShapeDtypeStruct((half // parts, width), BF)] * parts,
        (mine, arrived, gain),
        scratch=[pltpu.VMEM((width // 128, half, 128), F32)],
        name="norm",
        room=8,
    )


def project(blk, weight, rows):
    width = blk[0].shape[1]
    part = rows.shape[1] // 2
    each = blk[0].shape[0] // part
    core = lax.axis_index("head") & 1
    for i, piece in enumerate(blk):
        e, first = divmod(i * each, 4)
        at = pl.multiple_of((core ^ e) * part, part)
        for u in range(each):
            rows[first + u, pl.ds(at, part)] = piece[u * part : (u + 1) * part]
    total = jnp.zeros((rows.shape[1], weight.shape[0]), F32)
    for u in range(4):
        total += lax.dot_general(
            rows[u],
            weight[:, u * width : (u + 1) * width],
            (((1,), (1,)), ((), ())),
            preferred_element_type=F32,
        )
    return total.astype(BF)


def merge_stage(pieces, w_merge):
    part, width = pieces[0].shape
    count = len(pieces)
    groups = count * part // 4

    def kernel(*refs):
        weight, out, rows = refs[count:]
        out[...] = project(refs[:count], weight, rows)

    return call(
        kernel,
        [jax.ShapeDtypeStruct((groups, w_merge.shape[0]), BF)],
        (*pieces, w_merge),
        scratch=[pltpu.VMEM((4, groups, width), BF)],
        name="merge",
        room=6,
    )[0]


def deliver_stage(earlier, pieces, w_merge, owners, owner_total, capacity):
    quarter, width = pieces[0].shape
    count = len(pieces)
    ahead = len(earlier)
    groups = count * quarter // 4
    everyone = owners.shape[1]
    local = w_merge.shape[0]
    slots = owner_total * capacity

    def kernel(*refs):
        done = refs[:ahead]
        weight, owner_ref, out, rows = refs[ahead + count :]
        owner = owner_ref[...]
        picks = owner == lax.broadcasted_iota(jnp.int32, (128, everyone), 0)
        above = lax.broadcasted_iota(jnp.int32, (everyone, everyone), 0) < lax.broadcasted_iota(
            jnp.int32, (everyone, everyone), 1
        )
        before = jnp.dot(picks.astype(BF), above.astype(BF), preferred_element_type=F32)
        rank = jnp.sum(jnp.where(picks, before, 0.0), axis=0, keepdims=True)
        slot = owner * capacity + rank.astype(jnp.int32)
        dispatch = (slot == lax.broadcasted_iota(jnp.int32, (slots, everyone), 0)).astype(BF)
        last = project(refs[ahead : ahead + count], weight, rows)
        whole = jnp.concatenate([d[...] for d in done] + [last], axis=0)
        out[...] = jnp.dot(dispatch, whole, preferred_element_type=F32).astype(BF)

    return call(
        kernel,
        [jax.ShapeDtypeStruct((slots, local), BF)],
        (*earlier, *pieces, w_merge, owners),
        scratch=[pltpu.VMEM((4, groups, width), BF)],
        name="deliver",
        room=6,
    )[0]


def per_device(
    tokens,
    segment_ids,
    valid,
    owners,
    ln1_gain,
    w_qkv,
    w_out,
    ln2_gain,
    w_up,
    w_down,
    ln3_gain,
    w_merge,
):
    rows, width = tokens.shape
    heads = w_qkv.shape[2] // HEAD_DIM
    tok_total = lax.axis_size("tok")
    head_total = lax.axis_size("head")
    over_tok = lambda value, mask: lax.ppermute(value, "tok", swap_pairs(tok_total, mask))
    over_head = lambda value, mask: lax.ppermute(value, "head", swap_pairs(head_total, mask))
    teams = [list(range(g, g + heads)) for g in range(0, tok_total, heads)]
    in_team = lambda value: lax.all_to_all(
        value, "tok", 0, 0, tiled=True, axis_index_groups=teams
    )

    def all_heads(value):
        side = over_head(value, 2)
        return [value, over_head(value, 1), side, over_head(side, 1)]

    near, far = qkv_stage(
        tokens,
        ln1_gain,
        jnp.swapaxes(w_qkv, 1, 2),
        segment_ids.reshape(1, -1),
        valid.reshape(1, -1),
        heads,
    )
    far_in = []
    for k in range(heads, tok_total):
        leaving = far[k & (heads - 1)]
        if len(far_in) >= FLYING:
            leaving, far_in[-FLYING] = lax.optimization_barrier((leaving, far_in[-FLYING]))
        far_in.append(over_tok(leaving, k))
    w_outs = all_heads(w_out)
    queries, tops, sums, low_high, up, down = near_stage(
        in_team(near), tok_total, w_up, w_down
    )
    mixed = far_stage(far_in, queries, tops, sums, low_high, tok_total)
    att = in_team(mixed).reshape(heads * HEAD_DIM, rows)

    chunk = rows // CHUNKS
    gain2, gain3 = ln2_gain, ln3_gain
    weights = (w_outs, gain2, up, down)
    first, later = cut_stage(att, CHUNKS)
    attended = all_heads(first)
    side = over_head(later, 2)
    keep, own, *sends = mlp_stage(0, tokens, attended, *weights)
    send, mine0 = fold_stage(keep, own, [over_head(p, 1) for p in sends])
    later, send = lax.optimization_barrier((later, send))
    attended = [later, over_head(later, 1), side, over_head(side, 1)]
    arrived0 = over_head(send, 2)
    keep, own, *sends = mlp_stage(chunk, tokens, attended, *weights)
    send, mine1 = fold_stage(keep, own, [over_head(p, 1) for p in sends])
    mine0, _ = lax.optimization_barrier((mine0, send))
    arrived1 = over_head(send, 2)
    turned = w_merge.T
    both_cores = lambda values: values + [over_head(v, 1) for v in values]
    earlier = merge_stage(both_cores(list(norm_stage(mine0, arrived0, gain3, 2))), turned)
    arrived1, earlier = lax.optimization_barrier((arrived1, earlier))
    last = both_cores(list(norm_stage(mine1, arrived1, gain3, 1)))

    groups = rows // 4
    capacity = max(2, 2 * groups // tok_total)
    outgoing = deliver_stage([earlier], last, turned, owners.reshape(1, -1), tok_total, capacity)
    outgoing = outgoing.reshape(tok_total, capacity, outgoing.shape[1])
    received = lax.all_to_all(outgoing, "tok", split_axis=0, concat_axis=0, tiled=True)
    return received.reshape(tok_total * capacity, outgoing.shape[2])


def solution(mesh):
    in_specs = (
        P("tok", None),
        P("tok"),
        P("tok"),
        P("tok", None),
        P(),
        P(None, None, "head"),
        P("head", None),
        P(),
        P(None, "head"),
        P("head", None),
        P(),
        P(None, "head"),
    )
    out_specs = P("tok", "head")
    return jax.shard_map(
        per_device, mesh=mesh, in_specs=in_specs, out_specs=out_specs, check_vma=False
    )
```

```python
import math

import jax
import jax.numpy as jnp
from jax import lax
from jax.experimental import pallas as pl
from jax.experimental.pallas import tpu as pltpu
from jax.sharding import PartitionSpec as P

HEAD_DIM = 88
EXT = 128
VEXT = 96
GONE = 64.0
FAR = -1e30
BF = jnp.bfloat16
F32 = jnp.float32
CHUNKS = 2
FLYING = 4
SPLIT = 2


def swap_pairs(size, mask):
    return [(i, i ^ mask) for i in range(size)]


def center_scale(values):
    center = values - jnp.mean(values, axis=-1, keepdims=True)
    spread = jnp.mean(center * center, axis=-1, keepdims=True)
    return center * lax.rsqrt(spread + 1e-06)


SMEM = pl.BlockSpec(memory_space=pltpu.SMEM)
VM = pl.BlockSpec(memory_space=pltpu.VMEM)
HBM = pl.BlockSpec(memory_space=pltpu.HBM)


def wide(gain_ref):
    return gain_ref[...].astype(F32).reshape(1, gain_ref.shape[0])


def call(kernel, outs, args, specs=None, out_specs=None, scratch=(), name=None, room=24, cost=None):
    specs = specs if specs is not None else [VM] * len(args)
    out_specs = out_specs if out_specs is not None else [VM] * len(outs)
    spaces = {id(VM): pltpu.VMEM, id(HBM): pltpu.HBM}
    args = [
        pltpu.with_memory_space_constraint(a, spaces[id(s)]) if id(s) in spaces else a
        for a, s in zip(args, specs)
    ]
    outs = [
        spaces[id(s)](o.shape, o.dtype) if id(s) in spaces else o for o, s in zip(outs, out_specs)
    ]
    return pl.pallas_call(
        kernel,
        out_shape=outs,
        in_specs=specs,
        out_specs=out_specs,
        scratch_shapes=scratch,
        compiler_params=pltpu.CompilerParams(vmem_limit_bytes=room * 1024 * 1024),
        cost_estimate=cost,
        name=name,
    )(*args)


def qkv_stage(tokens, gain, w_qkv, seg, valid, heads):
    rows, width = tokens.shape
    local = w_qkv.shape[1]
    scale = math.log2(math.e) / math.sqrt(HEAD_DIM)
    far_rows = VEXT + HEAD_DIM
    near_rows = far_rows + HEAD_DIM
    strip = math.gcd(rows, 128)

    def kernel(tok_hbm, gain_hbm, w_hbm, seg_hbm, valid_hbm, *rest):
        near_hbm = rest[0]
        far_hbm = rest[1 : 1 + heads]
        near, tok, weight, normed, seg_ref, valid_ref, gain_ref, sem, leave = rest[1 + heads :]
        turn = lax.axis_index("tok") & (heads - 1)
        sends = [
            pltpu.make_async_copy(near.at[turn ^ j, pl.ds(0, far_rows)], far_hbm[j], leave.at[j])
            for j in range(heads)
        ]
        sends += [
            pltpu.make_async_copy(
                near.at[h, pl.ds(at, size)], near_hbm.at[h, pl.ds(at, size)], leave.at[to + h]
            )
            for to, at, size in ((heads, 0, far_rows), (2 * heads, far_rows, HEAD_DIM))
            for h in range(heads)
        ]
        strips = [slice(i * strip, (i + 1) * strip) for i in range(rows // strip)]
        tok_copies = [
            pltpu.make_async_copy(tok_hbm.at[at], tok.at[at], sem.at[7 + i])
            for i, at in enumerate(strips)
        ]
        for c in tok_copies:
            c.start()
        seg_copy = pltpu.make_async_copy(seg_hbm, seg_ref, sem.at[4])
        seg_copy.start()
        valid_copy = pltpu.make_async_copy(valid_hbm, valid_ref, sem.at[5])
        valid_copy.start()
        gain_copy = pltpu.make_async_copy(gain_hbm, gain_ref, sem.at[6])
        gain_copy.start()
        copies = [pltpu.make_async_copy(w_hbm.at[i], weight.at[i], sem.at[i]) for i in range(3)]
        for i in (1, 2, 0):
            copies[i].start()
        spread_to = lax.broadcasted_iota(jnp.int32, (rows // 4, rows), 1) // 4
        spread_from = lax.broadcasted_iota(jnp.int32, (rows // 4, rows), 0)
        spread = (spread_to == spread_from).astype(BF)
        seg_copy.wait()
        valid_copy.wait()
        seg8 = jnp.broadcast_to(seg_ref[...].astype(F32), (8, rows // 4)).astype(BF)
        tags = jnp.dot(seg8, spread, preferred_element_type=F32)
        gone = jnp.where(valid_ref[...] == 1, 0.0, GONE)
        tags = (tags + jnp.broadcast_to(gone, (8, rows))).astype(BF)
        for h in range(heads):
            near[h, HEAD_DIM:VEXT] = tags
        gain_copy.wait()
        gains = wide(gain_ref)
        for c, at in zip(tok_copies, strips):
            c.wait()
            normed[at] = (center_scale(tok[at].astype(F32)) * gains).astype(BF)

        for i, place in ((1, 0), (2, VEXT), (0, far_rows)):
            copies[i].wait()
            turned = lax.dot_general(
                weight[i], normed[...], (((1,), (1,)), ((), ())), preferred_element_type=F32
            )
            if i == 0:
                turned = turned * scale
            for h in range(heads):
                near[h, place : place + HEAD_DIM] = turned[
                    h * HEAD_DIM : (h + 1) * HEAD_DIM
                ].astype(BF)
            if i == 2:
                for c in sends[: 2 * heads]:
                    c.start()
            if i == 0:
                for c in sends[2 * heads :]:
                    c.start()
        for c in sends:
            c.wait()

    outs = [jax.ShapeDtypeStruct((heads, near_rows, rows), BF)]
    outs += [jax.ShapeDtypeStruct((far_rows, rows), BF)] * heads
    result = call(
        kernel,
        outs,
        (tokens, gain, w_qkv, seg, valid),
        specs=[HBM] * 5,
        out_specs=[HBM] * (1 + heads),
        scratch=[
            pltpu.VMEM((heads, near_rows, rows), BF),
            pltpu.VMEM((rows, width), BF),
            pltpu.VMEM((3, local, width), BF),
            pltpu.VMEM((rows, width), BF),
            pltpu.VMEM((1, rows // 4), jnp.int32),
            pltpu.VMEM((1, rows), jnp.int32),
            pltpu.VMEM((width,), BF),
            pltpu.SemaphoreType.DMA((7 + rows // strip,)),
            pltpu.SemaphoreType.DMA((3 * heads,)),
        ],
        name="qkv",
        room=16,
        cost=pl.CostEstimate(flops=4 * 10**9, transcendentals=0, bytes_accessed=10**7),
    )
    return result[0], result[1:]


def load_keys(block_ref, keys, values, segments):
    rows = block_ref.shape[1]
    tags = block_ref[0:VEXT].astype(F32)[HEAD_DIM : HEAD_DIM + 1]
    seg = jnp.where(tags >= GONE, tags - GONE, tags)
    turned = block_ref[0:EXT].astype(F32).T
    mark = turned[:, HEAD_DIM : HEAD_DIM + 1]
    mark = jnp.where(mark >= GONE, float(segments), mark)
    line = lax.broadcasted_iota(jnp.int32, (rows, EXT), 1) - HEAD_DIM
    hot = jnp.where(line.astype(F32) == mark, 1.0, 0.0)
    keys[...] = jnp.where(line >= 0, hot, turned).astype(BF)
    vals = block_ref[VEXT : VEXT + HEAD_DIM].astype(F32)
    ones = jnp.ones((VEXT - HEAD_DIM, rows), F32)
    values[...] = jnp.concatenate([vals, ones], axis=0).astype(BF)
    return jnp.min(seg), jnp.max(seg)


def absorb(keys, values, query, top, sums):
    scores = jnp.dot(keys[...], query[...], preferred_element_type=F32)
    newest = jnp.maximum(top[...], jnp.max(scores, axis=0, keepdims=True))
    weights = jnp.exp2(scores - newest).astype(BF)
    factor = jnp.exp2(top[...] - newest)
    sums[...] = sums[...] * factor + jnp.dot(values[...], weights, preferred_element_type=F32)
    top[...] = newest


def near_stage(blocks, segments, w_up, w_down):
    count, _, rows = blocks.shape
    query_at = VEXT + HEAD_DIM

    def kernel(
        blk, up_hbm, down_hbm, queries, tops, sums, low_high, up, down, keys, values, sem
    ):
        up_copy = pltpu.make_async_copy(up_hbm, up, sem.at[0])
        down_copy = pltpu.make_async_copy(down_hbm, down, sem.at[1])
        up_copy.start()
        down_copy.start()
        bounds = []
        for b in range(count):
            bounds.append(load_keys(blk.at[b], keys.at[b], values.at[b], segments))
            low_high[2 * b] = bounds[b][0]
            low_high[2 * b + 1] = bounds[b][1]
        for j in range(count):
            query = blk[j, query_at : query_at + HEAD_DIM].astype(F32)
            top = blk[j, 0:VEXT].astype(F32)
            tags = top[HEAD_DIM : HEAD_DIM + 1]
            gone = tags >= GONE
            seg = jnp.where(gone, tags - GONE, tags)
            line = lax.broadcasted_iota(jnp.int32, (EXT - HEAD_DIM, rows), 0).astype(F32)
            wall = jnp.where(line == seg, 0.0, FAR)
            queries[j] = jnp.concatenate([query, wall], axis=0).astype(BF)
            own = jnp.sum(query * top[0:HEAD_DIM], axis=0, keepdims=True)
            tops[j] = jnp.where(gone, own, FAR)
            sums[j] = jnp.where(gone, values[j].astype(F32), 0.0)
        for j in range(count):
            for b in range(count):

                @pl.when((bounds[b][0] <= bounds[j][1]) & (bounds[b][1] >= bounds[j][0]))
                def _():
                    absorb(keys.at[b], values.at[b], queries.at[j], tops.at[j], sums.at[j])

        up_copy.wait()
        down_copy.wait()

    outs = [
        jax.ShapeDtypeStruct((count, EXT, rows), BF),
        jax.ShapeDtypeStruct((count, 1, rows), F32),
        jax.ShapeDtypeStruct((count, VEXT, rows), F32),
        jax.ShapeDtypeStruct((2 * count,), F32),
        jax.ShapeDtypeStruct(w_up.shape, BF),
        jax.ShapeDtypeStruct(w_down.shape, BF),
    ]
    return call(
        kernel,
        outs,
        (blocks, w_up, w_down),
        specs=[VM, HBM, HBM],
        out_specs=[VM, VM, VM, SMEM, VM, VM],
        scratch=[
            pltpu.VMEM((count, rows, EXT), BF),
            pltpu.VMEM((count, VEXT, rows), BF),
            pltpu.SemaphoreType.DMA((2,)),
        ],
        name="near",
        room=8,
        cost=pl.CostEstimate(flops=8 * 10**9, transcendentals=4 * 10**6, bytes_accessed=10**7),
    )


def far_stage(blocks, queries, tops, sums, low_high, segments):
    count = len(blocks)
    heads, _, rows = queries.shape

    def kernel(*refs):
        blk = refs[:count]
        query_ref, top_ref, sum_ref, bound_ref = refs[count : count + 4]
        out, keys, values, top, total, ready, sem = refs[count + 4 :]
        leave = [pltpu.make_async_copy(ready.at[j], out.at[j], sem.at[j]) for j in range(heads)]
        bounds = [load_keys(blk[b], keys.at[b], values.at[b], segments) for b in range(count)]
        for j in range(heads):
            top[...] = top_ref[j]
            total[...] = sum_ref[j]
            for b in range(count):

                @pl.when((bounds[b][0] <= bound_ref[2 * j + 1]) & (bounds[b][1] >= bound_ref[2 * j]))
                def _():
                    absorb(keys.at[b], values.at[b], query_ref.at[j], top, total)

            whole = total[...]
            ready[j] = (whole[0:HEAD_DIM] / whole[HEAD_DIM : HEAD_DIM + 1]).astype(BF)
            leave[j].start()
        for j in range(heads):
            leave[j].wait()

    return call(
        kernel,
        [jax.ShapeDtypeStruct((heads, HEAD_DIM, rows), BF)],
        (*blocks, queries, tops, sums, low_high),
        specs=[VM] * (count + 3) + [SMEM],
        out_specs=[HBM],
        scratch=[
            pltpu.VMEM((count, rows, EXT), BF),
            pltpu.VMEM((count, VEXT, rows), BF),
            pltpu.VMEM((1, rows), F32),
            pltpu.VMEM((VEXT, rows), F32),
            pltpu.VMEM((heads, HEAD_DIM, rows), BF),
            pltpu.SemaphoreType.DMA((heads,)),
        ],
        name="far",
        room=6 + count // 2 + count // 4,
        cost=pl.CostEstimate(flops=6 * 10**9, transcendentals=4 * 10**6, bytes_accessed=10**7),
    )[0]


def cut_stage(whole, pieces):
    rows, width = whole.shape
    part = width // pieces

    def kernel(whole_ref, *out):
        for i in range(pieces):
            out[i][...] = whole_ref[:, i * part : (i + 1) * part]

    outs = [jax.ShapeDtypeStruct((rows, part), BF)] * pieces
    return call(kernel, outs, (whole,), name="cut", room=4)


def mlp_stage(first, tokens, attended, w_outs, gain, w_up, w_down):
    width = tokens.shape[1]
    part, rows = attended[0].shape
    pieces = len(attended)
    hidden = w_up.shape[1]
    half = rows // 2

    def kernel(tok_ref, *refs):
        att = refs[:pieces]
        wout = refs[pieces : 2 * pieces]
        gain_ref, up, down, keep, own = refs[2 * pieces : 2 * pieces + 5]
        sends = refs[2 * pieces + 5 : 2 * pieces + 5 + SPLIT]
        stream, second, act = refs[2 * pieces + 5 + SPLIT :]
        core = lax.axis_index("head") & 1
        keep_at = pl.multiple_of(core * half, half)
        total = tok_ref[first : first + rows].astype(F32)
        for e in range(pieces):
            total += jnp.dot(
                att[e][...].astype(F32).T.astype(BF), wout[e][...], preferred_element_type=F32
            )
        stream[...] = total
        own[...] = stream[pl.ds(keep_at, half)]
        second[...] = (center_scale(stream[...]) * wide(gain_ref)).astype(BF)
        pre = jnp.dot(second[...], up[...], preferred_element_type=F32)
        act[...] = (0.5 * pre * (1.0 + lax.erf(pre * math.sqrt(0.5)))).astype(BF)
        stream[...] = jnp.dot(act[...], down[...], preferred_element_type=F32)
        keep[...] = stream[pl.ds(keep_at, half)].astype(BF)
        for i in range(SPLIT):
            at = pl.multiple_of((1 - core) * half + i * (half // SPLIT), half // SPLIT)
            sends[i][...] = stream[pl.ds(at, half // SPLIT)].astype(BF)

    outs = [
        jax.ShapeDtypeStruct((half, width), BF),
        jax.ShapeDtypeStruct((half, width), F32),
    ]
    outs += [jax.ShapeDtypeStruct((half // SPLIT, width), BF)] * SPLIT
    return call(
        kernel,
        outs,
        (tokens, *attended, *w_outs, gain, w_up, w_down),
        scratch=[
            pltpu.VMEM((rows, width), F32),
            pltpu.VMEM((rows, width), BF),
            pltpu.VMEM((rows, hidden), BF),
        ],
        name="mlp",
        room=14,
        cost=pl.CostEstimate(
            flops=2 * rows * (width * width + 2 * width * hidden),
            transcendentals=rows * hidden,
            bytes_accessed=10**7,
        ),
    )


def fold_stage(keep, own, arrived):
    half, width = keep.shape
    piece = half // SPLIT

    def kernel(keep_ref, own_ref, *refs):
        send, mine = refs[SPLIT:]
        for i in range(SPLIT):
            at = slice(i * piece, (i + 1) * piece)
            both = keep_ref[at].astype(F32) + refs[i][...].astype(F32)
            send[at] = both.astype(BF)
            mine[at] = own_ref[at] + both

    outs = [
        jax.ShapeDtypeStruct((half, width), BF),
        jax.ShapeDtypeStruct((half, width), F32),
    ]
    return call(kernel, outs, (keep, own, *arrived), name="fold", room=8)


def norm_stage(mine, arrived, gain, parts):
    half, width = mine.shape
    groups = half // 4
    each = 4 // parts

    def kernel(mine_ref, arrived_ref, gain_ref, *refs):
        out, unit = refs[:parts], refs[parts]
        total = mine_ref[...] + arrived_ref[...].astype(F32)
        normed = center_scale(total) * wide(gain_ref)
        for c in range(width // 128):
            unit[c] = normed[:, c * 128 : (c + 1) * 128]
        for u in range(4):
            for c in range(width // 128):
                at = u % each * groups
                out[u // each][at : at + groups, c * 128 : (c + 1) * 128] = unit[
                    c, pl.ds(u, groups, stride=4)
                ].astype(BF)

    return call(
        kernel,
        [jax.ShapeDtypeStruct((half // parts, width), BF)] * parts,
        (mine, arrived, gain),
        scratch=[pltpu.VMEM((width // 128, half, 128), F32)],
        name="norm",
        room=8,
    )


def project(blk, weight, rows):
    width = blk[0].shape[1]
    part = rows.shape[1] // 2
    each = blk[0].shape[0] // part
    core = lax.axis_index("head") & 1
    for i, piece in enumerate(blk):
        e, first = divmod(i * each, 4)
        at = pl.multiple_of((core ^ e) * part, part)
        for u in range(each):
            rows[first + u, pl.ds(at, part)] = piece[u * part : (u + 1) * part]
    total = jnp.zeros((rows.shape[1], weight.shape[0]), F32)
    for u in range(4):
        total += lax.dot_general(
            rows[u],
            weight[:, u * width : (u + 1) * width],
            (((1,), (1,)), ((), ())),
            preferred_element_type=F32,
        )
    return total.astype(BF)


def merge_stage(pieces, w_merge):
    part, width = pieces[0].shape
    count = len(pieces)
    groups = count * part // 4

    def kernel(*refs):
        weight, out, rows = refs[count:]
        out[...] = project(refs[:count], weight, rows)

    return call(
        kernel,
        [jax.ShapeDtypeStruct((groups, w_merge.shape[0]), BF)],
        (*pieces, w_merge),
        scratch=[pltpu.VMEM((4, groups, width), BF)],
        name="merge",
        room=6,
    )[0]


def deliver_stage(earlier, pieces, w_merge, owners, owner_total, capacity):
    quarter, width = pieces[0].shape
    count = len(pieces)
    ahead = len(earlier)
    groups = count * quarter // 4
    everyone = owners.shape[1]
    local = w_merge.shape[0]
    slots = owner_total * capacity

    def kernel(*refs):
        done = refs[:ahead]
        weight, owner_ref, out, rows = refs[ahead + count :]
        owner = owner_ref[...]
        picks = owner == lax.broadcasted_iota(jnp.int32, (128, everyone), 0)
        above = lax.broadcasted_iota(jnp.int32, (everyone, everyone), 0) < lax.broadcasted_iota(
            jnp.int32, (everyone, everyone), 1
        )
        before = jnp.dot(picks.astype(BF), above.astype(BF), preferred_element_type=F32)
        rank = jnp.sum(jnp.where(picks, before, 0.0), axis=0, keepdims=True)
        slot = owner * capacity + rank.astype(jnp.int32)
        dispatch = (slot == lax.broadcasted_iota(jnp.int32, (slots, everyone), 0)).astype(BF)
        last = project(refs[ahead : ahead + count], weight, rows)
        whole = jnp.concatenate([d[...] for d in done] + [last], axis=0)
        out[...] = jnp.dot(dispatch, whole, preferred_element_type=F32).astype(BF)

    return call(
        kernel,
        [jax.ShapeDtypeStruct((slots, local), BF)],
        (*earlier, *pieces, w_merge, owners),
        scratch=[pltpu.VMEM((4, groups, width), BF)],
        name="deliver",
        room=6,
    )[0]


def per_device(
    tokens,
    segment_ids,
    valid,
    owners,
    ln1_gain,
    w_qkv,
    w_out,
    ln2_gain,
    w_up,
    w_down,
    ln3_gain,
    w_merge,
):
    rows, width = tokens.shape
    heads = w_qkv.shape[2] // HEAD_DIM
    tok_total = lax.axis_size("tok")
    head_total = lax.axis_size("head")
    over_tok = lambda value, mask: lax.ppermute(value, "tok", swap_pairs(tok_total, mask))
    over_head = lambda value, mask: lax.ppermute(value, "head", swap_pairs(head_total, mask))
    teams = [list(range(g, g + heads)) for g in range(0, tok_total, heads)]
    in_team = lambda value: lax.all_to_all(
        value, "tok", 0, 0, tiled=True, axis_index_groups=teams
    )

    def all_heads(value):
        side = over_head(value, 2)
        return [value, over_head(value, 1), side, over_head(side, 1)]

    near, far = qkv_stage(
        tokens,
        ln1_gain,
        jnp.swapaxes(w_qkv, 1, 2),
        segment_ids.reshape(1, -1),
        valid.reshape(1, -1),
        heads,
    )
    far_in = []
    for k in range(heads, tok_total):
        leaving = far[k & (heads - 1)]
        if len(far_in) >= FLYING:
            leaving, far_in[-FLYING] = lax.optimization_barrier((leaving, far_in[-FLYING]))
        far_in.append(over_tok(leaving, k))
    w_outs = all_heads(w_out)
    queries, tops, sums, low_high, up, down = near_stage(
        in_team(near), tok_total, w_up, w_down
    )
    mixed = far_stage(far_in, queries, tops, sums, low_high, tok_total)
    att = in_team(mixed).reshape(heads * HEAD_DIM, rows)

    chunk = rows // CHUNKS
    gain2, gain3 = ln2_gain, ln3_gain
    weights = (w_outs, gain2, up, down)
    first, later = cut_stage(att, CHUNKS)
    attended = all_heads(first)
    side = over_head(later, 2)
    keep, own, *sends = mlp_stage(0, tokens, attended, *weights)
    send, mine0 = fold_stage(keep, own, [over_head(p, 1) for p in sends])
    later, send = lax.optimization_barrier((later, send))
    attended = [later, over_head(later, 1), side, over_head(side, 1)]
    arrived0 = over_head(send, 2)
    keep, own, *sends = mlp_stage(chunk, tokens, attended, *weights)
    send, mine1 = fold_stage(keep, own, [over_head(p, 1) for p in sends])
    mine0, _ = lax.optimization_barrier((mine0, send))
    arrived1 = over_head(send, 2)
    turned = w_merge.T
    both_cores = lambda values: values + [over_head(v, 1) for v in values]
    earlier = merge_stage(both_cores(list(norm_stage(mine0, arrived0, gain3, 2))), turned)
    arrived1, earlier = lax.optimization_barrier((arrived1, earlier))
    last = both_cores(list(norm_stage(mine1, arrived1, gain3, 1)))

    groups = rows // 4
    capacity = max(2, 2 * groups // tok_total)
    outgoing = deliver_stage([earlier], last, turned, owners.reshape(1, -1), tok_total, capacity)
    outgoing = outgoing.reshape(tok_total, capacity, outgoing.shape[1])
    received = lax.all_to_all(outgoing, "tok", split_axis=0, concat_axis=0, tiled=True)
    return received.reshape(tok_total * capacity, outgoing.shape[2])


def solution(mesh):
    in_specs = (
        P("tok", None),
        P("tok"),
        P("tok"),
        P("tok", None),
        P(),
        P(None, None, "head"),
        P("head", None),
        P(),
        P(None, "head"),
        P("head", None),
        P(),
        P(None, "head"),
    )
    out_specs = P("tok", "head")
    return jax.shard_map(
        per_device, mesh=mesh, in_specs=in_specs, out_specs=out_specs, check_vma=False
    )
```

```python
import math

import jax
import jax.numpy as jnp
from jax import lax
from jax.experimental import pallas as pl
from jax.experimental.pallas import tpu as pltpu
from jax.sharding import PartitionSpec as P

HEAD_DIM = 88
EXT = 128
VEXT = 96
GONE = 64.0
FAR = -1e30
BF = jnp.bfloat16
F32 = jnp.float32
CHUNKS = 2
FLYING = 4
SPLIT = 2


def swap_pairs(size, mask):
    return [(i, i ^ mask) for i in range(size)]


def center_scale(values):
    center = values - jnp.mean(values, axis=-1, keepdims=True)
    spread = jnp.mean(center * center, axis=-1, keepdims=True)
    return center * lax.rsqrt(spread + 1e-06)


SMEM = pl.BlockSpec(memory_space=pltpu.SMEM)
VM = pl.BlockSpec(memory_space=pltpu.VMEM)
HBM = pl.BlockSpec(memory_space=pltpu.HBM)


def wide(gain_ref):
    return gain_ref[...].astype(F32).reshape(1, gain_ref.shape[0])


def call(kernel, outs, args, specs=None, out_specs=None, scratch=(), name=None, room=24, cost=None):
    specs = specs if specs is not None else [VM] * len(args)
    out_specs = out_specs if out_specs is not None else [VM] * len(outs)
    spaces = {id(VM): pltpu.VMEM, id(HBM): pltpu.HBM}
    args = [
        pltpu.with_memory_space_constraint(a, spaces[id(s)]) if id(s) in spaces else a
        for a, s in zip(args, specs)
    ]
    outs = [
        spaces[id(s)](o.shape, o.dtype) if id(s) in spaces else o for o, s in zip(outs, out_specs)
    ]
    return pl.pallas_call(
        kernel,
        out_shape=outs,
        in_specs=specs,
        out_specs=out_specs,
        scratch_shapes=scratch,
        compiler_params=pltpu.CompilerParams(vmem_limit_bytes=room * 1024 * 1024),
        cost_estimate=cost,
        name=name,
    )(*args)


def qkv_stage(tokens, gain, w_qkv, seg, valid, heads):
    rows, width = tokens.shape
    local = w_qkv.shape[1]
    scale = math.log2(math.e) / math.sqrt(HEAD_DIM)
    far_rows = VEXT + HEAD_DIM
    near_rows = far_rows + HEAD_DIM
    strip = math.gcd(rows, 128)

    def kernel(tok_hbm, gain_hbm, w_hbm, seg_hbm, valid_hbm, *rest):
        near_hbm = rest[0]
        far_hbm = rest[1 : 1 + heads]
        near, tok, weight, normed, seg_ref, valid_ref, gain_ref, sem, leave = rest[1 + heads :]
        turn = lax.axis_index("tok") & (heads - 1)
        sends = [
            pltpu.make_async_copy(near.at[turn ^ j, pl.ds(0, far_rows)], far_hbm[j], leave.at[j])
            for j in range(heads)
        ]
        sends += [
            pltpu.make_async_copy(
                near.at[h, pl.ds(at, size)], near_hbm.at[h, pl.ds(at, size)], leave.at[to + h]
            )
            for to, at, size in ((heads, 0, far_rows), (2 * heads, far_rows, HEAD_DIM))
            for h in range(heads)
        ]
        strips = [slice(i * strip, (i + 1) * strip) for i in range(rows // strip)]
        tok_copies = [
            pltpu.make_async_copy(tok_hbm.at[at], tok.at[at], sem.at[7 + i])
            for i, at in enumerate(strips)
        ]
        for c in tok_copies:
            c.start()
        seg_copy = pltpu.make_async_copy(seg_hbm, seg_ref, sem.at[4])
        seg_copy.start()
        valid_copy = pltpu.make_async_copy(valid_hbm, valid_ref, sem.at[5])
        valid_copy.start()
        gain_copy = pltpu.make_async_copy(gain_hbm, gain_ref, sem.at[6])
        gain_copy.start()
        copies = [pltpu.make_async_copy(w_hbm.at[i], weight.at[i], sem.at[i]) for i in range(3)]
        for i in (1, 2, 0):
            copies[i].start()
        spread_to = lax.broadcasted_iota(jnp.int32, (rows // 4, rows), 1) // 4
        spread_from = lax.broadcasted_iota(jnp.int32, (rows // 4, rows), 0)
        spread = (spread_to == spread_from).astype(BF)
        seg_copy.wait()
        valid_copy.wait()
        seg8 = jnp.broadcast_to(seg_ref[...].astype(F32), (8, rows // 4)).astype(BF)
        tags = jnp.dot(seg8, spread, preferred_element_type=F32)
        gone = jnp.where(valid_ref[...] == 1, 0.0, GONE)
        tags = (tags + jnp.broadcast_to(gone, (8, rows))).astype(BF)
        for h in range(heads):
            near[h, HEAD_DIM:VEXT] = tags
        gain_copy.wait()
        gains = wide(gain_ref)
        for c, at in zip(tok_copies, strips):
            c.wait()
            normed[at] = (center_scale(tok[at].astype(F32)) * gains).astype(BF)

        for i, place in ((1, 0), (2, VEXT), (0, far_rows)):
            copies[i].wait()
            turned = lax.dot_general(
                weight[i], normed[...], (((1,), (1,)), ((), ())), preferred_element_type=F32
            )
            if i == 0:
                turned = turned * scale
            for h in range(heads):
                near[h, place : place + HEAD_DIM] = turned[
                    h * HEAD_DIM : (h + 1) * HEAD_DIM
                ].astype(BF)
            if i == 2:
                for c in sends[: 2 * heads]:
                    c.start()
            if i == 0:
                for c in sends[2 * heads :]:
                    c.start()
        for c in sends:
            c.wait()

    outs = [jax.ShapeDtypeStruct((heads, near_rows, rows), BF)]
    outs += [jax.ShapeDtypeStruct((far_rows, rows), BF)] * heads
    result = call(
        kernel,
        outs,
        (tokens, gain, w_qkv, seg, valid),
        specs=[HBM] * 5,
        out_specs=[HBM] * (1 + heads),
        scratch=[
            pltpu.VMEM((heads, near_rows, rows), BF),
            pltpu.VMEM((rows, width), BF),
            pltpu.VMEM((3, local, width), BF),
            pltpu.VMEM((rows, width), BF),
            pltpu.VMEM((1, rows // 4), jnp.int32),
            pltpu.VMEM((1, rows), jnp.int32),
            pltpu.VMEM((width,), BF),
            pltpu.SemaphoreType.DMA((7 + rows // strip,)),
            pltpu.SemaphoreType.DMA((3 * heads,)),
        ],
        name="qkv",
        room=16,
        cost=pl.CostEstimate(flops=4 * 10**9, transcendentals=0, bytes_accessed=10**7),
    )
    return result[0], result[1:]


def load_keys(block_ref, keys, values, segments):
    rows = block_ref.shape[1]
    tags = block_ref[0:VEXT].astype(F32)[HEAD_DIM : HEAD_DIM + 1]
    seg = jnp.where(tags >= GONE, tags - GONE, tags)
    turned = block_ref[0:EXT].astype(F32).T
    mark = turned[:, HEAD_DIM : HEAD_DIM + 1]
    mark = jnp.where(mark >= GONE, float(segments), mark)
    line = lax.broadcasted_iota(jnp.int32, (rows, EXT), 1) - HEAD_DIM
    hot = jnp.where(line.astype(F32) == mark, 1.0, 0.0)
    keys[...] = jnp.where(line >= 0, hot, turned).astype(BF)
    vals = block_ref[VEXT : VEXT + HEAD_DIM].astype(F32)
    ones = jnp.ones((VEXT - HEAD_DIM, rows), F32)
    values[...] = jnp.concatenate([vals, ones], axis=0).astype(BF)
    return jnp.min(seg), jnp.max(seg)


def absorb(keys, values, query, top, sums):
    scores = jnp.dot(keys[...], query[...], preferred_element_type=F32)
    newest = jnp.maximum(top[...], jnp.max(scores, axis=0, keepdims=True))
    weights = jnp.exp2(scores - newest).astype(BF)
    factor = jnp.exp2(top[...] - newest)
    sums[...] = sums[...] * factor + jnp.dot(values[...], weights, preferred_element_type=F32)
    top[...] = newest


def near_stage(blocks, segments, w_up, w_down):
    count, _, rows = blocks.shape
    query_at = VEXT + HEAD_DIM

    def kernel(
        blk, up_hbm, down_hbm, queries, tops, sums, low_high, up, down, keys, values, sem
    ):
        up_copy = pltpu.make_async_copy(up_hbm, up, sem.at[0])
        down_copy = pltpu.make_async_copy(down_hbm, down, sem.at[1])
        up_copy.start()
        down_copy.start()
        bounds = []
        for b in range(count):
            bounds.append(load_keys(blk.at[b], keys.at[b], values.at[b], segments))
            low_high[2 * b] = bounds[b][0]
            low_high[2 * b + 1] = bounds[b][1]
        for j in range(count):
            query = blk[j, query_at : query_at + HEAD_DIM].astype(F32)
            top = blk[j, 0:VEXT].astype(F32)
            tags = top[HEAD_DIM : HEAD_DIM + 1]
            gone = tags >= GONE
            seg = jnp.where(gone, tags - GONE, tags)
            line = lax.broadcasted_iota(jnp.int32, (EXT - HEAD_DIM, rows), 0).astype(F32)
            wall = jnp.where(line == seg, 0.0, FAR)
            queries[j] = jnp.concatenate([query, wall], axis=0).astype(BF)
            own = jnp.sum(query * top[0:HEAD_DIM], axis=0, keepdims=True)
            tops[j] = jnp.where(gone, own, FAR)
            sums[j] = jnp.where(gone, values[j].astype(F32), 0.0)
        for j in range(count):
            for b in range(count):

                @pl.when((bounds[b][0] <= bounds[j][1]) & (bounds[b][1] >= bounds[j][0]))
                def _():
                    absorb(keys.at[b], values.at[b], queries.at[j], tops.at[j], sums.at[j])

        up_copy.wait()
        down_copy.wait()

    outs = [
        jax.ShapeDtypeStruct((count, EXT, rows), BF),
        jax.ShapeDtypeStruct((count, 1, rows), F32),
        jax.ShapeDtypeStruct((count, VEXT, rows), F32),
        jax.ShapeDtypeStruct((2 * count,), F32),
        jax.ShapeDtypeStruct(w_up.shape, BF),
        jax.ShapeDtypeStruct(w_down.shape, BF),
    ]
    return call(
        kernel,
        outs,
        (blocks, w_up, w_down),
        specs=[VM, HBM, HBM],
        out_specs=[VM, VM, VM, SMEM, VM, VM],
        scratch=[
            pltpu.VMEM((count, rows, EXT), BF),
            pltpu.VMEM((count, VEXT, rows), BF),
            pltpu.SemaphoreType.DMA((2,)),
        ],
        name="near",
        room=8,
        cost=pl.CostEstimate(flops=8 * 10**9, transcendentals=4 * 10**6, bytes_accessed=10**7),
    )


def far_stage(blocks, queries, tops, sums, low_high, segments):
    count = len(blocks)
    heads, _, rows = queries.shape

    def kernel(*refs):
        blk = refs[:count]
        query_ref, top_ref, sum_ref, bound_ref = refs[count : count + 4]
        out, keys, values, top, total, ready, sem = refs[count + 4 :]
        leave = [pltpu.make_async_copy(ready.at[j], out.at[j], sem.at[j]) for j in range(heads)]
        bounds = [load_keys(blk[b], keys.at[b], values.at[b], segments) for b in range(count)]
        for j in range(heads):
            top[...] = top_ref[j]
            total[...] = sum_ref[j]
            for b in range(count):

                @pl.when((bounds[b][0] <= bound_ref[2 * j + 1]) & (bounds[b][1] >= bound_ref[2 * j]))
                def _():
                    absorb(keys.at[b], values.at[b], query_ref.at[j], top, total)

            whole = total[...]
            ready[j] = (whole[0:HEAD_DIM] / whole[HEAD_DIM : HEAD_DIM + 1]).astype(BF)
            leave[j].start()
        for j in range(heads):
            leave[j].wait()

    return call(
        kernel,
        [jax.ShapeDtypeStruct((heads, HEAD_DIM, rows), BF)],
        (*blocks, queries, tops, sums, low_high),
        specs=[VM] * (count + 3) + [SMEM],
        out_specs=[HBM],
        scratch=[
            pltpu.VMEM((count, rows, EXT), BF),
            pltpu.VMEM((count, VEXT, rows), BF),
            pltpu.VMEM((1, rows), F32),
            pltpu.VMEM((VEXT, rows), F32),
            pltpu.VMEM((heads, HEAD_DIM, rows), BF),
            pltpu.SemaphoreType.DMA((heads,)),
        ],
        name="far",
        room=6 + count // 2 + count // 4,
        cost=pl.CostEstimate(flops=6 * 10**9, transcendentals=4 * 10**6, bytes_accessed=10**7),
    )[0]


def cut_stage(whole, pieces):
    rows, width = whole.shape
    part = width // pieces

    def kernel(whole_ref, *out):
        for i in range(pieces):
            out[i][...] = whole_ref[:, i * part : (i + 1) * part]

    outs = [jax.ShapeDtypeStruct((rows, part), BF)] * pieces
    return call(kernel, outs, (whole,), name="cut", room=4)


def mlp_stage(first, tokens, attended, w_outs, gain, w_up, w_down):
    width = tokens.shape[1]
    part, rows = attended[0].shape
    pieces = len(attended)
    hidden = w_up.shape[1]
    half = rows // 2

    def kernel(tok_ref, *refs):
        att = refs[:pieces]
        wout = refs[pieces : 2 * pieces]
        gain_ref, up, down, keep, own = refs[2 * pieces : 2 * pieces + 5]
        sends = refs[2 * pieces + 5 : 2 * pieces + 5 + SPLIT]
        stream, second, act = refs[2 * pieces + 5 + SPLIT :]
        core = lax.axis_index("head") & 1
        keep_at = pl.multiple_of(core * half, half)
        total = tok_ref[first : first + rows].astype(F32)
        for e in range(pieces):
            total += jnp.dot(
                att[e][...].astype(F32).T.astype(BF), wout[e][...], preferred_element_type=F32
            )
        stream[...] = total
        own[...] = stream[pl.ds(keep_at, half)]
        second[...] = (center_scale(stream[...]) * wide(gain_ref)).astype(BF)
        pre = jnp.dot(second[...], up[...], preferred_element_type=F32)
        act[...] = (0.5 * pre * (1.0 + lax.erf(pre * math.sqrt(0.5)))).astype(BF)
        stream[...] = jnp.dot(act[...], down[...], preferred_element_type=F32)
        keep[...] = stream[pl.ds(keep_at, half)].astype(BF)
        for i in range(SPLIT):
            at = pl.multiple_of((1 - core) * half + i * (half // SPLIT), half // SPLIT)
            sends[i][...] = stream[pl.ds(at, half // SPLIT)].astype(BF)

    outs = [
        jax.ShapeDtypeStruct((half, width), BF),
        jax.ShapeDtypeStruct((half, width), F32),
    ]
    outs += [jax.ShapeDtypeStruct((half // SPLIT, width), BF)] * SPLIT
    return call(
        kernel,
        outs,
        (tokens, *attended, *w_outs, gain, w_up, w_down),
        scratch=[
            pltpu.VMEM((rows, width), F32),
            pltpu.VMEM((rows, width), BF),
            pltpu.VMEM((rows, hidden), BF),
        ],
        name="mlp",
        room=14,
        cost=pl.CostEstimate(
            flops=2 * rows * (width * width + 2 * width * hidden),
            transcendentals=rows * hidden,
            bytes_accessed=10**7,
        ),
    )


def fold_stage(keep, own, arrived):
    half, width = keep.shape
    piece = half // SPLIT

    def kernel(keep_ref, own_ref, *refs):
        send, mine = refs[SPLIT:]
        for i in range(SPLIT):
            at = slice(i * piece, (i + 1) * piece)
            both = keep_ref[at].astype(F32) + refs[i][...].astype(F32)
            send[at] = both.astype(BF)
            mine[at] = own_ref[at] + both

    outs = [
        jax.ShapeDtypeStruct((half, width), BF),
        jax.ShapeDtypeStruct((half, width), F32),
    ]
    return call(kernel, outs, (keep, own, *arrived), name="fold", room=8)


def norm_stage(mine, arrived, gain, parts):
    half, width = mine.shape
    groups = half // 4
    each = 4 // parts

    def kernel(mine_ref, arrived_ref, gain_ref, *refs):
        out, unit = refs[:parts], refs[parts]
        total = mine_ref[...] + arrived_ref[...].astype(F32)
        normed = center_scale(total) * wide(gain_ref)
        for c in range(width // 128):
            unit[c] = normed[:, c * 128 : (c + 1) * 128]
        for u in range(4):
            for c in range(width // 128):
                at = u % each * groups
                out[u // each][at : at + groups, c * 128 : (c + 1) * 128] = unit[
                    c, pl.ds(u, groups, stride=4)
                ].astype(BF)

    return call(
        kernel,
        [jax.ShapeDtypeStruct((half // parts, width), BF)] * parts,
        (mine, arrived, gain),
        scratch=[pltpu.VMEM((width // 128, half, 128), F32)],
        name="norm",
        room=8,
    )


def project(blk, weight, rows):
    width = blk[0].shape[1]
    part = rows.shape[1] // 2
    each = blk[0].shape[0] // part
    core = lax.axis_index("head") & 1
    for i, piece in enumerate(blk):
        e, first = divmod(i * each, 4)
        at = pl.multiple_of((core ^ e) * part, part)
        for u in range(each):
            rows[first + u, pl.ds(at, part)] = piece[u * part : (u + 1) * part]
    total = jnp.zeros((rows.shape[1], weight.shape[0]), F32)
    for u in range(4):
        total += lax.dot_general(
            rows[u],
            weight[:, u * width : (u + 1) * width],
            (((1,), (1,)), ((), ())),
            preferred_element_type=F32,
        )
    return total.astype(BF)


def merge_stage(pieces, w_merge, owners, owner_total, capacity):
    part, width = pieces[0].shape
    count = len(pieces)
    groups = count * part // 4
    everyone = owners.shape[1]
    slots = owner_total * capacity

    def kernel(*refs):
        weight, owner_ref, out, dispatch, rows = refs[count:]
        owner = owner_ref[...]
        picks = owner == lax.broadcasted_iota(jnp.int32, (128, everyone), 0)
        above = lax.broadcasted_iota(jnp.int32, (everyone, everyone), 0) < lax.broadcasted_iota(
            jnp.int32, (everyone, everyone), 1
        )
        before = jnp.dot(picks.astype(BF), above.astype(BF), preferred_element_type=F32)
        rank = jnp.sum(jnp.where(picks, before, 0.0), axis=0, keepdims=True)
        slot = owner * capacity + rank.astype(jnp.int32)
        dispatch[...] = (
            slot == lax.broadcasted_iota(jnp.int32, (slots, everyone), 0)
        ).astype(BF)
        out[...] = project(refs[:count], weight, rows)

    return call(
        kernel,
        [
            jax.ShapeDtypeStruct((groups, w_merge.shape[0]), BF),
            jax.ShapeDtypeStruct((slots, everyone), BF),
        ],
        (*pieces, w_merge, owners),
        scratch=[pltpu.VMEM((4, groups, width), BF)],
        name="merge",
        room=6,
    )


def deliver_stage(earlier, dispatch, pieces, w_merge):
    part, width = pieces[0].shape
    count = len(pieces)
    groups = count * part // 4

    def kernel(done, dispatch_ref, *refs):
        weight, out, rows = refs[count:]
        last = project(refs[:count], weight, rows)
        whole = jnp.concatenate([done[...], last], axis=0)
        out[...] = jnp.dot(dispatch_ref[...], whole, preferred_element_type=F32).astype(BF)

    return call(
        kernel,
        [jax.ShapeDtypeStruct((dispatch.shape[0], w_merge.shape[0]), BF)],
        (earlier, dispatch, *pieces, w_merge),
        scratch=[pltpu.VMEM((4, groups, width), BF)],
        name="deliver",
        room=6,
    )[0]


def per_device(
    tokens,
    segment_ids,
    valid,
    owners,
    ln1_gain,
    w_qkv,
    w_out,
    ln2_gain,
    w_up,
    w_down,
    ln3_gain,
    w_merge,
):
    rows, width = tokens.shape
    heads = w_qkv.shape[2] // HEAD_DIM
    tok_total = lax.axis_size("tok")
    head_total = lax.axis_size("head")
    over_tok = lambda value, mask: lax.ppermute(value, "tok", swap_pairs(tok_total, mask))
    over_head = lambda value, mask: lax.ppermute(value, "head", swap_pairs(head_total, mask))
    teams = [list(range(g, g + heads)) for g in range(0, tok_total, heads)]
    in_team = lambda value: lax.all_to_all(
        value, "tok", 0, 0, tiled=True, axis_index_groups=teams
    )

    def all_heads(value):
        side = over_head(value, 2)
        return [value, over_head(value, 1), side, over_head(side, 1)]

    near, far = qkv_stage(
        tokens,
        ln1_gain,
        jnp.swapaxes(w_qkv, 1, 2),
        segment_ids.reshape(1, -1),
        valid.reshape(1, -1),
        heads,
    )
    far_in = []
    for k in range(heads, tok_total):
        leaving = far[k & (heads - 1)]
        if len(far_in) >= FLYING:
            leaving, far_in[-FLYING] = lax.optimization_barrier((leaving, far_in[-FLYING]))
        far_in.append(over_tok(leaving, k))
    w_outs = all_heads(w_out)
    queries, tops, sums, low_high, up, down = near_stage(
        in_team(near), tok_total, w_up, w_down
    )
    mixed = far_stage(far_in, queries, tops, sums, low_high, tok_total)
    att = in_team(mixed).reshape(heads * HEAD_DIM, rows)

    chunk = rows // CHUNKS
    gain2, gain3 = ln2_gain, ln3_gain
    weights = (w_outs, gain2, up, down)
    first, later = cut_stage(att, CHUNKS)
    attended = all_heads(first)
    side = over_head(later, 2)
    keep, own, *sends = mlp_stage(0, tokens, attended, *weights)
    send, mine0 = fold_stage(keep, own, [over_head(p, 1) for p in sends])
    later, send = lax.optimization_barrier((later, send))
    attended = [later, over_head(later, 1), side, over_head(side, 1)]
    arrived0 = over_head(send, 2)
    keep, own, *sends = mlp_stage(chunk, tokens, attended, *weights)
    send, mine1 = fold_stage(keep, own, [over_head(p, 1) for p in sends])
    mine0, _ = lax.optimization_barrier((mine0, send))
    arrived1 = over_head(send, 2)
    turned = w_merge.T
    both_cores = lambda values: values + [over_head(v, 1) for v in values]
    groups = rows // 4
    capacity = max(2, 2 * groups // tok_total)
    earlier, dispatch = merge_stage(
        both_cores(list(norm_stage(mine0, arrived0, gain3, 2))),
        turned,
        owners.reshape(1, -1),
        tok_total,
        capacity,
    )
    arrived1, earlier = lax.optimization_barrier((arrived1, earlier))
    last = both_cores(list(norm_stage(mine1, arrived1, gain3, 1)))
    outgoing = deliver_stage(earlier, dispatch, last, turned)
    outgoing = outgoing.reshape(tok_total, capacity, outgoing.shape[1])
    received = lax.all_to_all(outgoing, "tok", split_axis=0, concat_axis=0, tiled=True)
    return received.reshape(tok_total * capacity, outgoing.shape[2])


def solution(mesh):
    in_specs = (
        P("tok", None),
        P("tok"),
        P("tok"),
        P("tok", None),
        P(),
        P(None, None, "head"),
        P("head", None),
        P(),
        P(None, "head"),
        P("head", None),
        P(),
        P(None, "head"),
    )
    out_specs = P("tok", "head")
    return jax.shard_map(
        per_device, mesh=mesh, in_specs=in_specs, out_specs=out_specs, check_vma=False
    )
```

```python
import math

import jax
import jax.numpy as jnp
from jax import lax
from jax.experimental import pallas as pl
from jax.experimental.pallas import tpu as pltpu
from jax.sharding import PartitionSpec as P

HEAD_DIM = 88
EXT = 128
VEXT = 96
GONE = 64.0
FAR = -1e30
BF = jnp.bfloat16
F32 = jnp.float32
CHUNKS = 2
FLYING = 4
SPLIT = 2


def swap_pairs(size, mask):
    return [(i, i ^ mask) for i in range(size)]


def center_scale(values):
    center = values - jnp.mean(values, axis=-1, keepdims=True)
    spread = jnp.mean(center * center, axis=-1, keepdims=True)
    return center * lax.rsqrt(spread + 1e-06)


SMEM = pl.BlockSpec(memory_space=pltpu.SMEM)
VM = pl.BlockSpec(memory_space=pltpu.VMEM)
HBM = pl.BlockSpec(memory_space=pltpu.HBM)


def wide(gain_ref):
    return gain_ref[...].astype(F32).reshape(1, gain_ref.shape[0])


def call(kernel, outs, args, specs=None, out_specs=None, scratch=(), name=None, room=24, cost=None):
    specs = specs if specs is not None else [VM] * len(args)
    out_specs = out_specs if out_specs is not None else [VM] * len(outs)
    spaces = {id(VM): pltpu.VMEM, id(HBM): pltpu.HBM}
    args = [
        pltpu.with_memory_space_constraint(a, spaces[id(s)]) if id(s) in spaces else a
        for a, s in zip(args, specs)
    ]
    outs = [
        spaces[id(s)](o.shape, o.dtype) if id(s) in spaces else o for o, s in zip(outs, out_specs)
    ]
    return pl.pallas_call(
        kernel,
        out_shape=outs,
        in_specs=specs,
        out_specs=out_specs,
        scratch_shapes=scratch,
        compiler_params=pltpu.CompilerParams(vmem_limit_bytes=room * 1024 * 1024),
        cost_estimate=cost,
        name=name,
    )(*args)


def qkv_stage(tokens, gain, w_qkv, seg, valid, heads):
    rows, width = tokens.shape
    local = w_qkv.shape[1]
    scale = math.log2(math.e) / math.sqrt(HEAD_DIM)
    far_rows = VEXT + HEAD_DIM
    near_rows = far_rows + HEAD_DIM
    strip = math.gcd(rows, 128)

    def kernel(tok_hbm, gain_hbm, w_hbm, seg_hbm, valid_hbm, *rest):
        near_hbm = rest[0]
        far_hbm = rest[1 : 1 + heads]
        near, tok, weight, normed, seg_ref, valid_ref, gain_ref, sem, leave = rest[1 + heads :]
        turn = lax.axis_index("tok") & (heads - 1)
        sends = [
            pltpu.make_async_copy(near.at[turn ^ j, pl.ds(0, far_rows)], far_hbm[j], leave.at[j])
            for j in range(heads)
        ]
        sends += [
            pltpu.make_async_copy(
                near.at[h, pl.ds(at, size)], near_hbm.at[h, pl.ds(at, size)], leave.at[to + h]
            )
            for to, at, size in ((heads, 0, far_rows), (2 * heads, far_rows, HEAD_DIM))
            for h in range(heads)
        ]
        strips = [slice(i * strip, (i + 1) * strip) for i in range(rows // strip)]
        tok_copies = [
            pltpu.make_async_copy(tok_hbm.at[at], tok.at[at], sem.at[7 + i])
            for i, at in enumerate(strips)
        ]
        for c in tok_copies:
            c.start()
        seg_copy = pltpu.make_async_copy(seg_hbm, seg_ref, sem.at[4])
        seg_copy.start()
        valid_copy = pltpu.make_async_copy(valid_hbm, valid_ref, sem.at[5])
        valid_copy.start()
        gain_copy = pltpu.make_async_copy(gain_hbm, gain_ref, sem.at[6])
        gain_copy.start()
        copies = [pltpu.make_async_copy(w_hbm.at[i], weight.at[i], sem.at[i]) for i in range(3)]
        for i in (1, 2, 0):
            copies[i].start()
        spread_to = lax.broadcasted_iota(jnp.int32, (rows // 4, rows), 1) // 4
        spread_from = lax.broadcasted_iota(jnp.int32, (rows // 4, rows), 0)
        spread = (spread_to == spread_from).astype(BF)
        seg_copy.wait()
        valid_copy.wait()
        seg8 = jnp.broadcast_to(seg_ref[...].astype(F32), (8, rows // 4)).astype(BF)
        tags = jnp.dot(seg8, spread, preferred_element_type=F32)
        gone = jnp.where(valid_ref[...] == 1, 0.0, GONE)
        tags = (tags + jnp.broadcast_to(gone, (8, rows))).astype(BF)
        for h in range(heads):
            near[h, HEAD_DIM:VEXT] = tags
        gain_copy.wait()
        gains = wide(gain_ref)
        for c, at in zip(tok_copies, strips):
            c.wait()
            normed[at] = (center_scale(tok[at].astype(F32)) * gains).astype(BF)

        for i, place in ((1, 0), (2, VEXT), (0, far_rows)):
            copies[i].wait()
            turned = lax.dot_general(
                weight[i], normed[...], (((1,), (1,)), ((), ())), preferred_element_type=F32
            )
            if i == 0:
                turned = turned * scale
            for h in range(heads):
                near[h, place : place + HEAD_DIM] = turned[
                    h * HEAD_DIM : (h + 1) * HEAD_DIM
                ].astype(BF)
            if i == 2:
                for c in sends[: 2 * heads]:
                    c.start()
            if i == 0:
                for c in sends[2 * heads :]:
                    c.start()
        for c in sends:
            c.wait()

    outs = [jax.ShapeDtypeStruct((heads, near_rows, rows), BF)]
    outs += [jax.ShapeDtypeStruct((far_rows, rows), BF)] * heads
    result = call(
        kernel,
        outs,
        (tokens, gain, w_qkv, seg, valid),
        specs=[HBM] * 5,
        out_specs=[HBM] * (1 + heads),
        scratch=[
            pltpu.VMEM((heads, near_rows, rows), BF),
            pltpu.VMEM((rows, width), BF),
            pltpu.VMEM((3, local, width), BF),
            pltpu.VMEM((rows, width), BF),
            pltpu.VMEM((1, rows // 4), jnp.int32),
            pltpu.VMEM((1, rows), jnp.int32),
            pltpu.VMEM((width,), BF),
            pltpu.SemaphoreType.DMA((7 + rows // strip,)),
            pltpu.SemaphoreType.DMA((3 * heads,)),
        ],
        name="qkv",
        room=16,
        cost=pl.CostEstimate(flops=4 * 10**9, transcendentals=0, bytes_accessed=10**7),
    )
    return result[0], result[1:]


def load_keys(block_ref, keys, values, segments):
    rows = block_ref.shape[1]
    tags = block_ref[0:VEXT].astype(F32)[HEAD_DIM : HEAD_DIM + 1]
    seg = jnp.where(tags >= GONE, tags - GONE, tags)
    turned = block_ref[0:EXT].astype(F32).T
    mark = turned[:, HEAD_DIM : HEAD_DIM + 1]
    mark = jnp.where(mark >= GONE, float(segments), mark)
    line = lax.broadcasted_iota(jnp.int32, (rows, EXT), 1) - HEAD_DIM
    hot = jnp.where(line.astype(F32) == mark, 1.0, 0.0)
    keys[...] = jnp.where(line >= 0, hot, turned).astype(BF)
    vals = block_ref[VEXT : VEXT + HEAD_DIM].astype(F32)
    ones = jnp.ones((VEXT - HEAD_DIM, rows), F32)
    values[...] = jnp.concatenate([vals, ones], axis=0).astype(BF)
    return jnp.min(seg), jnp.max(seg)


def absorb(keys, values, query, top, sums):
    scores = jnp.dot(keys[...], query[...], preferred_element_type=F32)
    newest = jnp.maximum(top[...], jnp.max(scores, axis=0, keepdims=True))
    weights = jnp.exp2(scores - newest).astype(BF)
    factor = jnp.exp2(top[...] - newest)
    sums[...] = sums[...] * factor + jnp.dot(values[...], weights, preferred_element_type=F32)
    top[...] = newest


def near_stage(blocks, segments, w_up, w_down):
    count, _, rows = blocks.shape
    query_at = VEXT + HEAD_DIM

    def kernel(
        blk, up_hbm, down_hbm, queries, tops, sums, low_high, up, down, keys, values, sem
    ):
        up_copy = pltpu.make_async_copy(up_hbm, up, sem.at[0])
        down_copy = pltpu.make_async_copy(down_hbm, down, sem.at[1])
        up_copy.start()
        down_copy.start()
        bounds = []
        for b in range(count):
            bounds.append(load_keys(blk.at[b], keys.at[b], values.at[b], segments))
            low_high[2 * b] = bounds[b][0]
            low_high[2 * b + 1] = bounds[b][1]
        for j in range(count):
            query = blk[j, query_at : query_at + HEAD_DIM].astype(F32)
            top = blk[j, 0:VEXT].astype(F32)
            tags = top[HEAD_DIM : HEAD_DIM + 1]
            gone = tags >= GONE
            seg = jnp.where(gone, tags - GONE, tags)
            line = lax.broadcasted_iota(jnp.int32, (EXT - HEAD_DIM, rows), 0).astype(F32)
            wall = jnp.where(line == seg, 0.0, FAR)
            queries[j] = jnp.concatenate([query, wall], axis=0).astype(BF)
            own = jnp.sum(query * top[0:HEAD_DIM], axis=0, keepdims=True)
            tops[j] = jnp.where(gone, own, FAR)
            sums[j] = jnp.where(gone, values[j].astype(F32), 0.0)
        for j in range(count):
            for b in range(count):

                @pl.when((bounds[b][0] <= bounds[j][1]) & (bounds[b][1] >= bounds[j][0]))
                def _():
                    absorb(keys.at[b], values.at[b], queries.at[j], tops.at[j], sums.at[j])

        up_copy.wait()
        down_copy.wait()

    outs = [
        jax.ShapeDtypeStruct((count, EXT, rows), BF),
        jax.ShapeDtypeStruct((count, 1, rows), F32),
        jax.ShapeDtypeStruct((count, VEXT, rows), F32),
        jax.ShapeDtypeStruct((2 * count,), F32),
        jax.ShapeDtypeStruct(w_up.shape, BF),
        jax.ShapeDtypeStruct(w_down.shape, BF),
    ]
    return call(
        kernel,
        outs,
        (blocks, w_up, w_down),
        specs=[VM, HBM, HBM],
        out_specs=[VM, VM, VM, SMEM, VM, VM],
        scratch=[
            pltpu.VMEM((count, rows, EXT), BF),
            pltpu.VMEM((count, VEXT, rows), BF),
            pltpu.SemaphoreType.DMA((2,)),
        ],
        name="near",
        room=8,
        cost=pl.CostEstimate(flops=8 * 10**9, transcendentals=4 * 10**6, bytes_accessed=10**7),
    )


def far_stage(blocks, queries, tops, sums, low_high, segments):
    count = len(blocks)
    heads, _, rows = queries.shape

    def kernel(*refs):
        blk = refs[:count]
        query_ref, top_ref, sum_ref, bound_ref = refs[count : count + 4]
        out, keys, values, top, total, ready, sem = refs[count + 4 :]
        leave = [pltpu.make_async_copy(ready.at[j], out.at[j], sem.at[j]) for j in range(heads)]
        bounds = [load_keys(blk[b], keys.at[b], values.at[b], segments) for b in range(count)]
        for j in range(heads):
            top[...] = top_ref[j]
            total[...] = sum_ref[j]
            for b in range(count):

                @pl.when((bounds[b][0] <= bound_ref[2 * j + 1]) & (bounds[b][1] >= bound_ref[2 * j]))
                def _():
                    absorb(keys.at[b], values.at[b], query_ref.at[j], top, total)

            whole = total[...]
            ready[j] = (whole[0:HEAD_DIM] / whole[HEAD_DIM : HEAD_DIM + 1]).astype(BF)
            leave[j].start()
        for j in range(heads):
            leave[j].wait()

    return call(
        kernel,
        [jax.ShapeDtypeStruct((heads, HEAD_DIM, rows), BF)],
        (*blocks, queries, tops, sums, low_high),
        specs=[VM] * (count + 3) + [SMEM],
        out_specs=[HBM],
        scratch=[
            pltpu.VMEM((count, rows, EXT), BF),
            pltpu.VMEM((count, VEXT, rows), BF),
            pltpu.VMEM((1, rows), F32),
            pltpu.VMEM((VEXT, rows), F32),
            pltpu.VMEM((heads, HEAD_DIM, rows), BF),
            pltpu.SemaphoreType.DMA((heads,)),
        ],
        name="far",
        room=6 + count // 2 + count // 4,
        cost=pl.CostEstimate(flops=6 * 10**9, transcendentals=4 * 10**6, bytes_accessed=10**7),
    )[0]


def cut_stage(whole, pieces):
    rows, width = whole.shape
    part = width // pieces

    def kernel(whole_ref, *out):
        for i in range(pieces):
            out[i][...] = whole_ref[:, i * part : (i + 1) * part]

    outs = [jax.ShapeDtypeStruct((rows, part), BF)] * pieces
    return call(kernel, outs, (whole,), name="cut", room=4)


def mlp_stage(first, tokens, attended, w_outs, gain, w_up, w_down):
    width = tokens.shape[1]
    part, rows = attended[0].shape
    pieces = len(attended)
    hidden = w_up.shape[1]
    half = rows // 2

    def kernel(tok_ref, *refs):
        att = refs[:pieces]
        wout = refs[pieces : 2 * pieces]
        gain_ref, up, down, keep, own = refs[2 * pieces : 2 * pieces + 5]
        sends = refs[2 * pieces + 5 : 2 * pieces + 5 + SPLIT]
        stream, second, act = refs[2 * pieces + 5 + SPLIT :]
        core = lax.axis_index("head") & 1
        keep_at = pl.multiple_of(core * half, half)
        total = tok_ref[first : first + rows].astype(F32)
        for e in range(pieces):
            total += jnp.dot(
                att[e][...].astype(F32).T.astype(BF), wout[e][...], preferred_element_type=F32
            )
        stream[...] = total
        own[...] = stream[pl.ds(keep_at, half)]
        second[...] = (center_scale(stream[...]) * wide(gain_ref)).astype(BF)
        pre = jnp.dot(second[...], up[...], preferred_element_type=F32)
        act[...] = (0.5 * pre * (1.0 + lax.erf(pre * math.sqrt(0.5)))).astype(BF)
        stream[...] = jnp.dot(act[...], down[...], preferred_element_type=F32)
        keep[...] = stream[pl.ds(keep_at, half)].astype(BF)
        for i in range(SPLIT):
            at = pl.multiple_of((1 - core) * half + i * (half // SPLIT), half // SPLIT)
            sends[i][...] = stream[pl.ds(at, half // SPLIT)].astype(BF)

    outs = [
        jax.ShapeDtypeStruct((half, width), BF),
        jax.ShapeDtypeStruct((half, width), F32),
    ]
    outs += [jax.ShapeDtypeStruct((half // SPLIT, width), BF)] * SPLIT
    return call(
        kernel,
        outs,
        (tokens, *attended, *w_outs, gain, w_up, w_down),
        scratch=[
            pltpu.VMEM((rows, width), F32),
            pltpu.VMEM((rows, width), BF),
            pltpu.VMEM((rows, hidden), BF),
        ],
        name="mlp",
        room=14,
        cost=pl.CostEstimate(
            flops=2 * rows * (width * width + 2 * width * hidden),
            transcendentals=rows * hidden,
            bytes_accessed=10**7,
        ),
    )


def fold_stage(keep, own, arrived):
    half, width = keep.shape
    piece = half // SPLIT

    def kernel(keep_ref, own_ref, *refs):
        send, mine = refs[SPLIT:]
        for i in range(SPLIT):
            at = slice(i * piece, (i + 1) * piece)
            both = keep_ref[at].astype(F32) + refs[i][...].astype(F32)
            send[at] = both.astype(BF)
            mine[at] = own_ref[at] + both

    outs = [
        jax.ShapeDtypeStruct((half, width), BF),
        jax.ShapeDtypeStruct((half, width), F32),
    ]
    return call(kernel, outs, (keep, own, *arrived), name="fold", room=8)


def norm_stage(mine, arrived, gain, parts):
    half, width = mine.shape
    groups = half // 4
    each = 4 // parts

    def kernel(mine_ref, arrived_ref, gain_ref, *refs):
        out, unit = refs[:parts], refs[parts]
        total = mine_ref[...] + arrived_ref[...].astype(F32)
        normed = center_scale(total) * wide(gain_ref)
        for c in range(width // 128):
            unit[c] = normed[:, c * 128 : (c + 1) * 128]
        for u in range(4):
            for c in range(width // 128):
                at = u % each * groups
                out[u // each][at : at + groups, c * 128 : (c + 1) * 128] = unit[
                    c, pl.ds(u, groups, stride=4)
                ].astype(BF)

    return call(
        kernel,
        [jax.ShapeDtypeStruct((half // parts, width), BF)] * parts,
        (mine, arrived, gain),
        scratch=[pltpu.VMEM((width // 128, half, 128), F32)],
        name="norm",
        room=8,
    )


def project(blk, weight, rows):
    width = blk[0].shape[1]
    part = rows.shape[1] // 2
    each = blk[0].shape[0] // part
    core = lax.axis_index("head") & 1
    for i, piece in enumerate(blk):
        e, first = divmod(i * each, 4)
        at = pl.multiple_of((core ^ e) * part, part)
        for u in range(each):
            rows[first + u, pl.ds(at, part)] = piece[u * part : (u + 1) * part]
    total = jnp.zeros((weight.shape[0], rows.shape[1]), F32)
    for u in range(4):
        total += lax.dot_general(
            weight[:, u * width : (u + 1) * width],
            rows[u],
            (((1,), (1,)), ((), ())),
            preferred_element_type=F32,
        )
    return total.astype(BF)


def merge_stage(pieces, w_merge, owners, owner_total, capacity):
    part, width = pieces[0].shape
    count = len(pieces)
    groups = count * part // 4
    everyone = owners.shape[1]
    slots = owner_total * capacity

    def kernel(*refs):
        weight, owner_ref, out, dispatch, rows = refs[count:]
        owner = owner_ref[...]
        picks = owner == lax.broadcasted_iota(jnp.int32, (128, everyone), 0)
        above = lax.broadcasted_iota(jnp.int32, (everyone, everyone), 0) < lax.broadcasted_iota(
            jnp.int32, (everyone, everyone), 1
        )
        before = jnp.dot(picks.astype(BF), above.astype(BF), preferred_element_type=F32)
        rank = jnp.sum(jnp.where(picks, before, 0.0), axis=0, keepdims=True)
        slot = owner * capacity + rank.astype(jnp.int32)
        dispatch[...] = (
            slot == lax.broadcasted_iota(jnp.int32, (slots, everyone), 0)
        ).astype(BF)
        out[...] = project(refs[:count], weight, rows)

    return call(
        kernel,
        [
            jax.ShapeDtypeStruct((w_merge.shape[0], groups), BF),
            jax.ShapeDtypeStruct((slots, everyone), BF),
        ],
        (*pieces, w_merge, owners),
        scratch=[pltpu.VMEM((4, groups, width), BF)],
        name="merge",
        room=6,
    )


def deliver_stage(earlier, dispatch, pieces, w_merge):
    part, width = pieces[0].shape
    count = len(pieces)
    groups = count * part // 4

    def kernel(done, dispatch_ref, *refs):
        weight, out, rows = refs[count:]
        last = project(refs[:count], weight, rows)
        whole = jnp.concatenate([done[...], last], axis=1)
        out[...] = lax.dot_general(
            dispatch_ref[...], whole, (((1,), (1,)), ((), ())), preferred_element_type=F32
        ).astype(BF)

    return call(
        kernel,
        [jax.ShapeDtypeStruct((dispatch.shape[0], w_merge.shape[0]), BF)],
        (earlier, dispatch, *pieces, w_merge),
        scratch=[pltpu.VMEM((4, groups, width), BF)],
        name="deliver",
        room=6,
    )[0]


def per_device(
    tokens,
    segment_ids,
    valid,
    owners,
    ln1_gain,
    w_qkv,
    w_out,
    ln2_gain,
    w_up,
    w_down,
    ln3_gain,
    w_merge,
):
    rows, width = tokens.shape
    heads = w_qkv.shape[2] // HEAD_DIM
    tok_total = lax.axis_size("tok")
    head_total = lax.axis_size("head")
    over_tok = lambda value, mask: lax.ppermute(value, "tok", swap_pairs(tok_total, mask))
    over_head = lambda value, mask: lax.ppermute(value, "head", swap_pairs(head_total, mask))
    teams = [list(range(g, g + heads)) for g in range(0, tok_total, heads)]
    in_team = lambda value: lax.all_to_all(
        value, "tok", 0, 0, tiled=True, axis_index_groups=teams
    )

    def all_heads(value):
        side = over_head(value, 2)
        return [value, over_head(value, 1), side, over_head(side, 1)]

    near, far = qkv_stage(
        tokens,
        ln1_gain,
        jnp.swapaxes(w_qkv, 1, 2),
        segment_ids.reshape(1, -1),
        valid.reshape(1, -1),
        heads,
    )
    far_in = []
    for k in range(heads, tok_total):
        leaving = far[k & (heads - 1)]
        if len(far_in) >= FLYING:
            leaving, far_in[-FLYING] = lax.optimization_barrier((leaving, far_in[-FLYING]))
        far_in.append(over_tok(leaving, k))
    w_outs = all_heads(w_out)
    queries, tops, sums, low_high, up, down = near_stage(
        in_team(near), tok_total, w_up, w_down
    )
    mixed = far_stage(far_in, queries, tops, sums, low_high, tok_total)
    att = in_team(mixed).reshape(heads * HEAD_DIM, rows)

    chunk = rows // CHUNKS
    gain2, gain3 = ln2_gain, ln3_gain
    weights = (w_outs, gain2, up, down)
    first, later = cut_stage(att, CHUNKS)
    attended = all_heads(first)
    side = over_head(later, 2)
    keep, own, *sends = mlp_stage(0, tokens, attended, *weights)
    send, mine0 = fold_stage(keep, own, [over_head(p, 1) for p in sends])
    later, send = lax.optimization_barrier((later, send))
    attended = [later, over_head(later, 1), side, over_head(side, 1)]
    arrived0 = over_head(send, 2)
    keep, own, *sends = mlp_stage(chunk, tokens, attended, *weights)
    send, mine1 = fold_stage(keep, own, [over_head(p, 1) for p in sends])
    mine0, _ = lax.optimization_barrier((mine0, send))
    arrived1 = over_head(send, 2)
    turned = w_merge.T
    both_cores = lambda values: values + [over_head(v, 1) for v in values]
    groups = rows // 4
    capacity = max(2, 2 * groups // tok_total)
    earlier, dispatch = merge_stage(
        both_cores(list(norm_stage(mine0, arrived0, gain3, 2))),
        turned,
        owners.reshape(1, -1),
        tok_total,
        capacity,
    )
    arrived1, earlier = lax.optimization_barrier((arrived1, earlier))
    last = both_cores(list(norm_stage(mine1, arrived1, gain3, 1)))
    outgoing = deliver_stage(earlier, dispatch, last, turned)
    outgoing = outgoing.reshape(tok_total, capacity, outgoing.shape[1])
    received = lax.all_to_all(outgoing, "tok", split_axis=0, concat_axis=0, tiled=True)
    return received.reshape(tok_total * capacity, outgoing.shape[2])


def solution(mesh):
    in_specs = (
        P("tok", None),
        P("tok"),
        P("tok"),
        P("tok", None),
        P(),
        P(None, None, "head"),
        P("head", None),
        P(),
        P(None, "head"),
        P("head", None),
        P(),
        P(None, "head"),
    )
    out_specs = P("tok", "head")
    return jax.shard_map(
        per_device, mesh=mesh, in_specs=in_specs, out_specs=out_specs, check_vma=False
    )
```
